256 devices in a mesh: sample: 2 (over z_hi), fsdp: 4 (over x), seq: 32 (over y, z_lo, core).
Axes of the slice: x: 4, y: 4, z: 8 (z_hi: 2, z_lo: 4; z = z_hi * 4 + z_lo), core: 2. Of those that a mesh axis runs over, the one named last changes fastest.
Arguments:
- token_act: bfloat16 [8, 4096, 768], P(('sample', 'fsdp'), 'seq'), may hold values from -40 to 40
- token_cond: bfloat16 [8, 4096, 768], P(('sample', 'fsdp'), 'seq'), may hold values from -40 to 40
- pair_bias: bfloat16 [16, 4096, 4096], P('fsdp', 'seq'), may hold values from -8 to 296
- token_mask: int32 [4096], P('seq'), may hold values 0 or 1
- ada_weights: bfloat16 [4, 768, 768], P(None, None, 'fsdp'), may hold values from -0.21875 to 0.21875
- attention_in: bfloat16 [4, 768, 768], P(None, None, 'fsdp'), may hold values from -0.21875 to 0.21875
- attention_out: bfloat16 [768, 768], P('fsdp'), may hold values from -0.21875 to 0.21875
- transition_in: bfloat16 [2, 768, 1536], P(None, None, 'fsdp'), may hold values from -0.21875 to 0.21875
- transition_out: bfloat16 [1536, 768], P('fsdp'), may hold values from -0.15625 to 0.15625
- token_vectors: float32 [3, 768], replicated, may hold values from -4 to 4
- atom_skip: bfloat16 [8, 32768, 128], P(('sample', 'fsdp'), 'seq'), may hold values from -40 to 40
- atom_cond: bfloat16 [32768, 128], P('seq'), may hold values from -40 to 40
- atom_bias: bfloat16 [4, 32768, 128], P(None, 'seq'), may hold values from -6 to 296
- window_bounds: int32 [1024, 2], P('seq'), may hold values from 0 to 32768, as said below
- atom_token: int32 [32768], P('seq'), may hold values from 0 to 4095, as said below
- atom_weights: bfloat16 [7, 128, 128], P(None, None, 'fsdp'), may hold values from -0.5 to 0.5
- token_to_atom: bfloat16 [768, 128], P('fsdp'), may hold values from -0.21875 to 0.21875
- atom_vectors: float32 [2, 128], replicated, may hold values from -4 to 4
- position_out: bfloat16 [3, 128], replicated, may hold values from -0.5 to 0.5
Outputs:
- token_out: bfloat16 [8, 4096, 768], P(('sample', 'fsdp'), 'seq')
- position_update: float32 [8, 3, 32768], P(('sample', 'fsdp'), None, 'seq')
The draws below stay inside these ranges and needn't reach their ends.
Inputs may be any that keep to these rules, and one draw needn't show every extreme that they name: `window_bounds`: row b belongs to the atoms 32 * b to 32 * b + 31; column 0 is at least 0 and at least 32 * b - 48, and at most 32 * b; column 1 is at least 32 * b + 32, at most 32 * b + 80 and at most 32768. `atom_token`: atoms are numbered in token order: the value never falls from one atom to the next, the first atom belongs to token 0, the last to token 4095, and every token owns 1 to 24 atoms.
All inputs are finite; a program needn't handle non-finite values. No bound on the sum of `token_mask` on one device may be relied on, other than what follows from the above.
Results may differ from the reference program's by a relative error of at most 0.014.
Values may be sent and summed in bfloat16 or wider, within the bound.
No kernel may reach another device: no remote copies, remote signals or barrier semaphores. Data moves between devices by JAX's collectives and lax.ppermute only.
A program may use at most 128 MiB of HBM per device.

```python
import math
import jax
import jax.numpy as jnp
from jax import lax

D = 768
H = 16
FF = 1536
CA = 128
HA = 4
WQ = 32
WK = 128
TOKENS = 4096
ATOMS = 32768
BLOCKS = 1024
SAMPLES = 8
HD = 48


def feature_draw(key, shape):
    base = jnp.clip(jax.random.normal(jax.random.fold_in(key, 11), shape, jnp.float32), -4.0, 4.0)
    return base.astype(jnp.bfloat16)


def draw_token_act(key, part):
    return feature_draw(jax.random.fold_in(key, 101), (SAMPLES, TOKENS, D))


def draw_token_cond(key, part):
    return feature_draw(jax.random.fold_in(key, 102), (SAMPLES, TOKENS, D))


def draw_atom_skip(key, part):
    return feature_draw(jax.random.fold_in(key, 103), (SAMPLES, ATOMS, CA))


def draw_atom_cond(key, part):
    return feature_draw(jax.random.fold_in(key, 104), (ATOMS, CA))


def draw_pair_bias(key, part):
    key = jax.random.fold_in(key, 301)
    values = jnp.clip(2.0 * jax.random.normal(jax.random.fold_in(key, 1), (H, TOKENS, TOKENS), jnp.float32), -8.0, 8.0)
    return values.astype(jnp.bfloat16)


def draw_atom_bias(key, part):
    key = jax.random.fold_in(key, 401)
    values = jnp.clip(1.5 * jax.random.normal(jax.random.fold_in(key, 1), (HA, ATOMS, WK), jnp.float32), -6.0, 6.0)
    return values.astype(jnp.bfloat16)


def draw_window_bounds(key, part):
    key = jax.random.fold_in(key, 501)
    rim_width = (WK - WQ) // 2
    block_start = WQ * jnp.arange(BLOCKS, dtype=jnp.int32)
    lower_end = jnp.maximum(block_start - jax.random.randint(jax.random.fold_in(key, 1), (BLOCKS,), 0, rim_width + 1), 0)
    upper_end = jnp.minimum(block_start + WQ + jax.random.randint(jax.random.fold_in(key, 2), (BLOCKS,), 0, rim_width + 1), ATOMS)
    return jnp.stack([lower_end, upper_end], axis=1).astype(jnp.int32)


def paired_runs(key, pair_count, pair_total):
    first = jax.random.randint(key, (pair_count,), 1, pair_total)
    return jnp.stack([first, pair_total - first], axis=1).reshape(-1).astype(jnp.int32)


def draw_atom_token(key, part):
    key = jax.random.fold_in(key, 601)
    quarter = TOKENS // 4
    group_size = TOKENS // 16
    long_runs = jnp.full((quarter,), 24, jnp.int32)
    middle_runs = paired_runs(jax.random.fold_in(key, 1), quarter // 2, 8)
    short_runs = paired_runs(jax.random.fold_in(key, 2), quarter, 4)
    lengths = jnp.concatenate([long_runs, middle_runs, short_runs]).astype(jnp.int32)
    rest_order = jax.random.permutation(jax.random.fold_in(key, 3), 12).astype(jnp.int32) + 4
    order = jnp.concatenate([jnp.arange(4, dtype=jnp.int32), rest_order]).astype(jnp.int32)
    lengths = jnp.take(lengths.reshape(16, group_size), order, axis=0).reshape(-1).astype(jnp.int32)
    run_ends = jnp.cumsum(lengths)
    marks = jnp.zeros((ATOMS,), jnp.int32).at[run_ends[:-1]].add(1)
    return jnp.cumsum(marks).astype(jnp.int32)


def place_ends(drawn, key, smallest, largest):
    longest = drawn.shape.index(max(drawn.shape))
    spots = []
    for shift in (0, 1):
        where = [jax.random.randint(jax.random.fold_in(key, axis), (), 0, length) for axis, length in enumerate(drawn.shape)]
        where[longest] = (where[longest] + shift) % drawn.shape[longest]
        spots.append(tuple(where))
    return drawn.at[spots[0]].set(smallest).at[spots[1]].set(largest)


def steps_of(key, dims, split, low, largest):
    def one(dim, shards_of):
        steps = jax.random.uniform(jax.random.fold_in(jax.random.fold_in(key, 6), dim), (shards_of,), jnp.float32, low / len(split), largest / len(split))
        return jnp.repeat(jnp.exp(steps), dims[dim] // shards_of).reshape((-1,) + (1,) * (len(dims) - dim - 1))

    loudness = one(*split[0])
    for cut in split[1:]:
        loudness = loudness * one(*cut)
    return loudness


def bell_draw(stream_key, shape, scale, limit, shards=(), kind=jnp.bfloat16):
    values = jax.random.normal(stream_key, shape, jnp.float32) * scale
    if len(shards) > 0:
        values = steps_of(stream_key, shape, shards, -0.22, 0.18) * values
    return jnp.clip(values, min=-limit, max=limit).astype(kind)


def setup_inputs(seed: int = 0) -> dict:
    arg_keys = jax.random.split(jax.random.key(seed), 20)
    token_act = draw_token_act(jax.random.fold_in(arg_keys[19], 71), 0)
    token_cond = draw_token_cond(jax.random.fold_in(arg_keys[19], 71), 0)
    pair_bias = draw_pair_bias(jax.random.fold_in(arg_keys[19], 71), 0)
    token_mask = place_ends((jax.random.randint(arg_keys[3], (TOKENS,), 0, 8) < 7).astype(jnp.int32), jax.random.fold_in(arg_keys[3], 1), 0, 1)
    ada_weights = bell_draw(arg_keys[4], (4, D, D), D ** -0.5, 0.21875, ((2, 4),))
    attention_in = bell_draw(arg_keys[5], (4, D, D), D ** -0.5, 0.21875, ((2, 4),))
    attention_out = bell_draw(arg_keys[6], (D, D), D ** -0.5, 0.21875, ((0, 4),))
    transition_in = bell_draw(arg_keys[7], (2, D, FF), D ** -0.5, 0.21875, ((2, 4),))
    transition_out = bell_draw(arg_keys[8], (FF, D), FF ** -0.5, 0.15625, ((0, 4),))
    token_vectors = bell_draw(arg_keys[9], (3, D), 1.0, 4.0, (), jnp.float32)
    atom_skip = draw_atom_skip(jax.random.fold_in(arg_keys[19], 71), 0)
    atom_cond = draw_atom_cond(jax.random.fold_in(arg_keys[19], 71), 0)
    atom_bias = draw_atom_bias(jax.random.fold_in(arg_keys[19], 71), 0)
    window_bounds = draw_window_bounds(jax.random.fold_in(arg_keys[19], 71), 0)
    atom_token = draw_atom_token(jax.random.fold_in(arg_keys[19], 71), 0)
    atom_weights = bell_draw(arg_keys[15], (7, CA, CA), CA ** -0.5, 0.5, ((2, 4),))
    token_to_atom = bell_draw(arg_keys[16], (D, CA), D ** -0.5, 0.21875, ((0, 4),))
    atom_vectors = bell_draw(arg_keys[17], (2, CA), 1.0, 4.0, (), jnp.float32)
    position_out = bell_draw(arg_keys[18], (3, CA), CA ** -0.5, 0.5)
    return {"token_act": token_act, "token_cond": token_cond, "pair_bias": pair_bias, "token_mask": token_mask, "ada_weights": ada_weights, "attention_in": attention_in, "attention_out": attention_out, "transition_in": transition_in, "transition_out": transition_out, "token_vectors": token_vectors, "atom_skip": atom_skip, "atom_cond": atom_cond, "atom_bias": atom_bias, "window_bounds": window_bounds, "atom_token": atom_token, "atom_weights": atom_weights, "token_to_atom": token_to_atom, "atom_vectors": atom_vectors, "position_out": position_out}


EPS = 1e-05
FAR = -1e+30

def layer_norm(values):
    values = values.astype(jnp.float32)
    center = values - lax.optimization_barrier(jnp.mean(values, axis=-1, keepdims=True))
    spread = lax.optimization_barrier(jnp.mean(center * center, axis=-1, keepdims=True))
    return center * lax.rsqrt(spread + EPS)

def matmul(left_side, right_side):
    return jnp.dot(left_side, right_side, preferred_element_type=jnp.float32)

def adaptive(values, normed_cond, scale_weight, shift_weight, offset):
    return jax.nn.sigmoid(matmul(normed_cond, scale_weight) + offset) * layer_norm(values) + matmul(normed_cond, shift_weight)

def window_attention(queries, pairs, bias_rows, bounds):
    atom_count, feature_count = queries.shape
    block_count = atom_count // WQ
    step_count = WK // WQ
    rim_width = (WK - WQ) // 2
    head_width = feature_count // HA
    padded = jnp.pad(pairs, ((rim_width, rim_width), (0, 0)))
    tile_rows = padded.reshape(block_count + step_count - 1, WQ, 2 * feature_count)
    windows = jnp.concatenate([tile_rows[position:position + block_count] for position in range(step_count)], axis=1)
    key_rows = windows[:, :, :feature_count].reshape(block_count, WK, HA, head_width)
    value_rows = windows[:, :, feature_count:].reshape(block_count, WK, HA, head_width)
    query_rows = queries.reshape(block_count, WQ, HA, head_width)
    scores = jnp.einsum('bqhd,bkhd->hbqk', query_rows.astype(jnp.float32), key_rows.astype(jnp.float32)) * (1.0 / math.sqrt(head_width))
    scores = scores + bias_rows.reshape(HA, block_count, WQ, WK).astype(jnp.float32)
    slot_atoms = WQ * jnp.arange(block_count, dtype=jnp.int32)[:, None] - rim_width + jnp.arange(WK, dtype=jnp.int32)[None, :]
    in_window = (slot_atoms >= bounds[:, 0:1]) & (slot_atoms < bounds[:, 1:2])
    scores = jnp.where(in_window[None, :, None, :], scores, FAR)
    maxima = lax.optimization_barrier(jnp.max(scores, axis=-1, keepdims=True))
    weights = jnp.exp(scores - maxima)
    totals = lax.optimization_barrier(jnp.sum(weights, axis=-1))
    attended = jnp.einsum('hbqk,bkhd->bqhd', weights.astype(jnp.bfloat16).astype(jnp.float32), value_rows.astype(jnp.float32))
    attended = attended / jnp.transpose(totals, (1, 2, 0))[..., None]
    return attended.reshape(atom_count, feature_count)

def reference(token_act, token_cond, pair_bias, token_mask, ada_weights, attention_in, attention_out, transition_in, transition_out, token_vectors, atom_skip, atom_cond, atom_bias, window_bounds, atom_token, atom_weights, token_to_atom, atom_vectors, position_out):
    cond_normed = layer_norm(token_cond).astype(jnp.bfloat16)
    attend_x = adaptive(token_act, cond_normed, ada_weights[0], ada_weights[1], token_vectors[0]).astype(jnp.bfloat16)
    transit_x = adaptive(token_act, cond_normed, ada_weights[2], ada_weights[3], token_vectors[1]).astype(jnp.bfloat16)
    query_rows = (matmul(attend_x, attention_in[0]) + token_vectors[2]).astype(jnp.bfloat16)
    key_rows = matmul(attend_x, attention_in[1]).astype(jnp.bfloat16)
    value_rows = matmul(attend_x, attention_in[2]).astype(jnp.bfloat16)
    gate_rows = matmul(attend_x, attention_in[3]).astype(jnp.bfloat16)
    query_heads = query_rows.reshape(SAMPLES, TOKENS, H, HD)
    key_heads = key_rows.reshape(SAMPLES, TOKENS, H, HD)
    value_heads = value_rows.reshape(SAMPLES, TOKENS, H, HD)
    live_keys = token_mask > 0
    score_scale = 1.0 / math.sqrt(HD)

    def one_head(combined):
        sample = (combined // H).astype(jnp.int32)
        head_id = (combined % H).astype(jnp.int32)
        query_one = lax.dynamic_index_in_dim(lax.dynamic_index_in_dim(query_heads, sample, 0, False), head_id, 1, False)
        key_one = lax.dynamic_index_in_dim(lax.dynamic_index_in_dim(key_heads, sample, 0, False), head_id, 1, False)
        value_one = lax.dynamic_index_in_dim(lax.dynamic_index_in_dim(value_heads, sample, 0, False), head_id, 1, False)
        bias_one = lax.dynamic_index_in_dim(pair_bias, head_id, 0, False).astype(jnp.float32)
        scores = jnp.dot(query_one, key_one.T, preferred_element_type=jnp.float32) * score_scale + bias_one
        scores = jnp.where(live_keys[None, :], scores, FAR)
        maxima = lax.optimization_barrier(jnp.max(scores, axis=-1, keepdims=True))
        weights = jnp.exp(scores - maxima)
        totals = lax.optimization_barrier(jnp.sum(weights, axis=-1, keepdims=True))
        return matmul(weights.astype(jnp.bfloat16), value_one) / totals
    head_outputs = lax.map(one_head, jnp.arange(SAMPLES * H, dtype=jnp.int32))
    attended = head_outputs.reshape(SAMPLES, H, TOKENS, HD).transpose(0, 2, 1, 3).reshape(SAMPLES, TOKENS, D)
    gated = (attended * jax.nn.sigmoid(gate_rows.astype(jnp.float32))).astype(jnp.bfloat16)
    hidden = (jax.nn.silu(matmul(transit_x, transition_in[0])) * matmul(transit_x, transition_in[1])).astype(jnp.bfloat16)
    token_out = (token_act.astype(jnp.float32) + matmul(gated, attention_out) + matmul(hidden, transition_out)).astype(jnp.bfloat16)
    token_rows = matmul(token_out, token_to_atom).astype(jnp.bfloat16)
    atom_state = atom_skip.astype(jnp.float32) + jnp.take(token_rows, atom_token, axis=1).astype(jnp.float32)
    atom_normed = layer_norm(atom_cond).astype(jnp.bfloat16)
    atom_x = adaptive(atom_state, atom_normed, atom_weights[0], atom_weights[1], atom_vectors[0]).astype(jnp.bfloat16)
    atom_query = (matmul(atom_x, atom_weights[2]) + atom_vectors[1]).astype(jnp.bfloat16)
    atom_key = matmul(atom_x, atom_weights[3]).astype(jnp.bfloat16)
    atom_value = matmul(atom_x, atom_weights[4]).astype(jnp.bfloat16)
    atom_gate = matmul(atom_x, atom_weights[5]).astype(jnp.bfloat16)
    pairs = jnp.concatenate([atom_key, atom_value], axis=-1)

    def one_sample(operands):
        return window_attention(operands[0], operands[1], atom_bias, window_bounds)
    atom_attended = lax.map(one_sample, (atom_query, pairs))
    atom_gated = (atom_attended * jax.nn.sigmoid(atom_gate.astype(jnp.float32))).astype(jnp.bfloat16)
    atom_new = atom_state + matmul(atom_gated, atom_weights[6])
    final_normed = layer_norm(atom_new).astype(jnp.bfloat16)
    position_update = jnp.einsum('ck,sak->sca', position_out.astype(jnp.float32), final_normed.astype(jnp.float32))
    return (token_out, position_update)
```

```python
import functools
import math

import jax
import jax.numpy as jnp
from jax import lax
from jax.experimental import pallas as pl
from jax.experimental.pallas import tpu as pltpu
from jax.sharding import PartitionSpec as P

EPS = 1e-05
FAR = -1e30
SENT = 1e30
LOG2E = 1.4426950408889634
HD = 48
HA = 4
WQ = 32
WK = 128
RIM = 48
NX = 4
NY = 4
NZ = 4
NC = 2
ROWS = 128
DIM = 768
COLS = 192
HEADS = 4
ATOMS = 1024
EXT = ATOMS + 2 * RIM
CHUNK = 112
CHUNKS = EXT // CHUNK
CA = 128
F32 = jnp.float32
BF16 = jnp.bfloat16


def x_shift(a, k):
    return lax.ppermute(a, "fsdp", [(i, (i + k) % NX) for i in range(NX)])


def y_shift(a, k):
    group = NZ * NC
    pairs = [(t, ((t // group + k) % NY) * group + t % group) for t in range(NY * group)]
    return lax.ppermute(a, "seq", pairs)


def z_shift(a, k):
    group = NZ * NC
    pairs = [
        (t, (t // group) * group + ((t // NC + k) % NZ) * NC + t % NC) for t in range(NY * group)
    ]
    return lax.ppermute(a, "seq", pairs)


def y_exchange(a):
    group = NZ * NC
    groups = [[y * group + n for y in range(NY)] for n in range(group)]
    return lax.all_to_all(
        a, "seq", split_axis=0, concat_axis=0, axis_index_groups=groups, tiled=True
    )


def c_shift(a):
    return lax.ppermute(a, "seq", [(t, t ^ 1) for t in range(NY * NZ * NC)])


def norm(values):
    center = values - jnp.mean(values, axis=-1, keepdims=True)
    spread = jnp.mean(center * center, axis=-1, keepdims=True)
    return center * lax.rsqrt(spread + EPS)


def sigmoid(v):
    return 1.0 / (1.0 + jnp.exp(-v))


def dot(a, b):
    return jnp.dot(a, b, preferred_element_type=F32)


def dot_nt(a, b):
    return lax.dot_general(a, b, (((1,), (1,)), ((), ())), preferred_element_type=F32)


def kernel_call(body, name, out_shape, args, scalars=(), scratch=(), flops=0, size=0, limit=40):
    vmem = pl.BlockSpec(memory_space=pltpu.VMEM)
    smem = pl.BlockSpec(memory_space=pltpu.SMEM)
    ins = [vmem] * len(args)
    args = (*scalars, *args)
    ins = [smem] * len(scalars) + ins
    return pl.pallas_call(
        body,
        out_shape=out_shape,
        in_specs=ins,
        out_specs=jax.tree.map(lambda _: vmem, out_shape),
        scratch_shapes=list(scratch),
        compiler_params=pltpu.CompilerParams(vmem_limit_bytes=limit << 20),
        cost_estimate=pl.CostEstimate(flops=flops, bytes_accessed=size, transcendentals=0),
        name=name,
    )(*args)


def shape(dims, kind=BF16):
    return jax.ShapeDtypeStruct(dims, kind)


def prepare_body(pos, act, cond, *outs):
    f = pos[0]
    normed = norm(cond[...].astype(F32)).astype(BF16)
    hat = norm(act[...].astype(F32))
    for k in range(NX):
        dest = lax.rem(f + k, NX)
        part = hat[:, 0:COLS]
        for j in range(1, NX):
            part = jnp.where(dest == j, hat[:, j * COLS : (j + 1) * COLS], part)
        outs[k][:, 0:DIM] = normed
        outs[k][:, DIM : DIM + COLS] = part.astype(BF16)


def adaptive_body(m0, m1, m2, m3, ada, offset, maps, attend, message):
    parts = (m0, m1, m2, m3)
    normed = jnp.concatenate([m[:, 0:DIM] for m in parts], axis=0)
    hat = jnp.concatenate([m[:, DIM : DIM + COLS] for m in parts], axis=0).astype(F32)
    message[DIM:, :] = maps[...]
    for n in range(2):
        scale = sigmoid(dot(normed, ada[2 * n]) + offset[n : n + 1, :])
        result = (scale * hat + dot(normed, ada[2 * n + 1])).astype(BF16)
        wide = jnp.concatenate([result[k * ROWS : (k + 1) * ROWS] for k in range(NX)], axis=1)
        if n == 0:
            attend[...] = wide
        else:
            for i in range(DIM // 128):
                message[i * ROWS : (i + 1) * ROWS, :] = wide[:, i * 128 : (i + 1) * 128]


def gathered_rows(part, j):
    return jnp.concatenate(
        [part[:, ((r - j) % NX) * COLS : ((r - j) % NX + 1) * COLS] for r in range(NX)],
        axis=0,
    )


def project_body(pos, a0, a1, a2, a3, weights, offset, mask, q, kv, g):
    f = pos[0]
    parts = (a0, a1, a2, a3)
    sums = [None] * 4
    for j in range(NX):
        rows = gathered_rows(parts[j][...], j)
        at = pl.multiple_of(lax.rem(f + NX - j, NX) * COLS, COLS)
        for n in range(4):
            term = dot(rows, weights[n, pl.ds(at, COLS), :])
            sums[n] = term if j == 0 else sums[n] + term
    live = mask[...] > 0
    for r in range(NX):
        own = slice(r * ROWS, (r + 1) * ROWS)
        to = slice(r * COLS, (r + 1) * COLS)
        q[:, to] = ((sums[0][own] + offset[0:1, :]) * (LOG2E / math.sqrt(HD))).astype(BF16)
        kv[0:ROWS, to] = jnp.where(live, sums[1][own], SENT).astype(BF16)
        kv[ROWS:, to] = sums[2][own].astype(BF16)
        g[:, to] = sums[3][own].astype(BF16)


def hidden_body(pos, t0, t1, t2, t3, w_in, w_out, out):
    f = pos[0]
    parts = (t0, t1, t2, t3)
    gate, up = None, None
    for j in range(NX):
        wide = jnp.concatenate(
            [parts[j][i * ROWS : (i + 1) * ROWS, :] for i in range(DIM // 128)], axis=1
        )
        rows = gathered_rows(wide, j)
        at = pl.multiple_of(lax.rem(f + NX - j, NX) * COLS, COLS)
        gate_term = dot(rows, w_in[0, pl.ds(at, COLS), :])
        up_term = dot(rows, w_in[1, pl.ds(at, COLS), :])
        gate = gate_term if j == 0 else gate + gate_term
        up = up_term if j == 0 else up + up_term
    hidden = (gate / (1.0 + jnp.exp(-gate)) * up).astype(BF16)
    out[...] = dot(hidden, w_out[...])


KEYS = NZ * NC * ROWS


def attention_body(pos, *refs):
    q = refs[0:4]
    pairs = refs[4:12]
    bias = refs[12]
    out = refs[13:17]
    q_all, key_all, value_all, far_row, bias_all, stats = refs[17:23]
    h = pl.program_id(0)

    @pl.when(h == 0)
    def _():
        unit = (lax.broadcasted_iota(jnp.int32, (8, 128), 1) == 0).astype(F32).astype(BF16)
        for side in range(2):
            core = pos[2] if side == 0 else 1 - pos[2]
            for n in range(NZ):
                block = pairs[side * NZ + n][0:ROWS, :]
                place = lax.rem(pos[1] + NZ - n, NZ) * NC + core
                at = pl.multiple_of(place * ROWS, ROWS)
                first = dot_nt(unit, block[:, 0:128])
                far_row[:, pl.ds(at, ROWS)] = jnp.where(first > 1e20, FAR, 0.0)
                wide = block.astype(F32)
                key_all[pl.ds(at, ROWS), :] = jnp.where(wide[:, 0:1] > 1e20, 0.0, wide).astype(BF16)
                value_all[pl.ds(at, ROWS), :] = pairs[side * NZ + n][ROWS:, :]
        for n in range(NY):
            q_all[n * ROWS : (n + 1) * ROWS, :] = q[n][...]
        stats[...] = jnp.zeros_like(stats)

    for n in range(NY):
        part = bias[lax.rem(pos[0] + NY - n, NY), 0]
        bias_all[n] = part.astype(F32) * LOG2E + far_row[0:1, :]

    lane = lax.broadcasted_iota(jnp.int32, (NY * ROWS, 256), 1)
    slot = lax.broadcasted_iota(jnp.int32, (ROWS, 128), 1)
    for s in range(NX):
        lane0 = COLS * s + HD * h
        start = jnp.minimum(lane0 // 128, (DIM - 256) // 128)
        off = lane0 - start * 128
        window = pl.ds(pl.multiple_of(start * 128, 128), 256)
        mine = (lane >= off) & (lane < off + HD)
        index = s * HEADS + h
        of_max = (lax.rem(slot, 16) == index) & (slot < 48)
        of_total = (lax.rem(slot, 16) == index) & (slot >= 48) & (slot < 96)
        rows = jnp.where(mine, q_all[:, window].astype(F32), 0.0).astype(BF16)
        scores = dot_nt(rows, key_all[:, window])
        probs, totals = [], []
        for n in range(NY):
            part = scores[n * ROWS : (n + 1) * ROWS] + bias_all[n]
            top = jnp.max(part, axis=1, keepdims=True)
            part = jnp.exp2(part - top)
            total = jnp.sum(part, axis=1, keepdims=True)
            probs.append(part.astype(BF16))
            totals.append(total)
            stats[n] = jnp.where(of_max, top, jnp.where(of_total, total, stats[n]))
        summed = dot(jnp.concatenate(probs, axis=0), value_all[:, window])
        for n in range(NY):
            own = slice(n * ROWS, (n + 1) * ROWS)
            scaled = summed[own] * (1.0 / totals[n])
            before = out[n][:, window].astype(F32)
            out[n][:, window] = jnp.where(mine[own], scaled, before).astype(BF16)

    @pl.when(h == HEADS - 1)
    def _():
        third = lax.rem(slot // 16, 3)
        for n in range(NY):
            whole = stats[n]
            high = whole.astype(BF16).astype(F32)
            rest = whole - high
            middle = rest.astype(BF16).astype(F32)
            low = rest - middle
            sent = jnp.where(third == 0, high, jnp.where(third == 1, middle, low))
            out[n][:, DIM : DIM + 128] = sent.astype(BF16)


def attention(pos, q, pairs, bias):
    in_specs = [pl.BlockSpec(memory_space=pltpu.SMEM)]
    in_specs += [pl.BlockSpec((ROWS, DIM), lambda h: (0, 0))] * 4
    in_specs += [pl.BlockSpec((2 * ROWS, DIM), lambda h: (0, 0))] * 8
    in_specs += [pl.BlockSpec((NY, 1, ROWS, KEYS), lambda h: (0, h, 0, 0))]
    return pl.pallas_call(
        attention_body,
        grid=(HEADS,),
        out_shape=[shape((ROWS, DIM + 128))] * 4,
        in_specs=in_specs,
        out_specs=[pl.BlockSpec((ROWS, DIM + 128), lambda h: (0, 0))] * 4,
        scratch_shapes=[
            pltpu.VMEM((NY * ROWS, DIM), BF16),
            pltpu.VMEM((KEYS, DIM), BF16),
            pltpu.VMEM((KEYS, DIM), BF16),
            pltpu.VMEM((8, KEYS), F32),
            pltpu.VMEM((NY, ROWS, KEYS), F32),
            pltpu.VMEM((NY, ROWS, 128), F32),
        ],
        compiler_params=pltpu.CompilerParams(
            dimension_semantics=("arbitrary",), vmem_limit_bytes=48 << 20
        ),
        cost_estimate=pl.CostEstimate(
            flops=16 * 512 * 1024 * 512 * 2, bytes_accessed=12 << 20, transcendentals=8 << 20
        ),
        name="attention",
    )(pos, *q, *pairs, bias)


def combine_body(o0, o1, o2, o3, gate, ffn, w_out, w_atom, act, *outs):
    parts = (o0, o1, o2, o3)
    tops, totals = [], []
    for o in parts:
        sent = o[:, DIM : DIM + 128].astype(F32)
        whole = sent + pltpu.roll(sent, 128 - 16, 1) + pltpu.roll(sent, 128 - 32, 1)
        tops.append(whole)
        totals.append(pltpu.roll(whole, 128 - 48, 1))
    used = lax.broadcasted_iota(jnp.int32, (ROWS, 128), 1) < 16
    tops = [jnp.where(used, t, 0.0) for t in tops]
    totals = [jnp.where(used, t, 1.0) for t in totals]
    top = jnp.maximum(jnp.maximum(tops[0], tops[1]), jnp.maximum(tops[2], tops[3]))
    shares = [n * jnp.exp2(t - top) for t, n in zip(tops, totals)]
    inverse = 1.0 / (shares[0] + shares[1] + shares[2] + shares[3])
    head = lax.broadcasted_iota(jnp.int32, (128, DIM), 0) * HD
    lane = lax.broadcasted_iota(jnp.int32, (128, DIM), 1)
    spread = ((lane >= head) & (lane < head + HD)).astype(F32).astype(BF16)
    attended = None
    for o, share in zip(parts, shares):
        share = share * inverse
        high = share.astype(BF16)
        low = (share - high.astype(F32)).astype(BF16)
        term = (dot(high, spread) + dot(low, spread)) * o[:, 0:DIM].astype(F32)
        attended = term if attended is None else attended + term
    gated = (attended * sigmoid(gate[...].astype(F32))).astype(BF16)
    for r in range(NX):
        part = dot(gated[:, r * COLS : (r + 1) * COLS], w_out[...]) + ffn[r * ROWS : (r + 1) * ROWS]
        small = part.astype(BF16)
        rows = dot(small, w_atom[...])
        if r == 0:
            outs[0][...] = part + act[...].astype(F32)
            outs[4][...] = rows + dot(act[...], w_atom[...])
        else:
            outs[r][...] = small
            outs[4 + r][...] = rows.astype(BF16)


def atom_first_body(pos, starts, w0, w1, w2, w3, cond, tokens, offset, *outs):
    weights, project, scale, shift, select = outs
    for k, w in enumerate((w0, w1, w2, w3)):
        src = lax.rem(pos[0] + NX - k, NX)
        project[pl.ds(pl.multiple_of(src * COLS, COLS), COLS), :] = w[DIM : DIM + COLS, :]
        at = pl.multiple_of(src * 32, 32)
        for i in range(7):
            line = DIM + COLS + i * 32
            weights[i, pl.ds(at, 32), :] = w[line : line + 32, :]
    normed = norm(cond[...].astype(F32)).astype(BF16)
    scale[...] = sigmoid(dot_nt(normed, weights[0]) + offset[0:1, :])
    shift[...] = dot_nt(normed, weights[1])
    row = lax.broadcasted_iota(jnp.int32, (128, CHUNK), 0)
    for i in range(CHUNKS):
        hit = ((row + starts[i]) == tokens[i : i + 1, :]).astype(F32)
        select[i * CHUNK : (i + 1) * CHUNK, :] = hit.T.astype(BF16)


def atom_body(pos, starts, bounds, near, far, before, own_skip, after, *refs):
    scale, shift, select, weights, offset, bias, spots, out = refs[0:8]
    table, skip, state, xs, qs, ks, vs, gs, at_all = refs[8:]
    skip[0:RIM, :] = before[0:RIM, :]
    skip[RIM : RIM + ATOMS, :] = own_skip[...]
    skip[RIM + ATOMS :, :] = after[0:RIM, :]
    y, z, c = pos[0], pos[1], pos[2]
    for ky in range(NY):
        for kz in range(NZ):
            place = lax.rem(y + NY - ky, NY) * (NZ * NC) + lax.rem(z + NZ - kz, NZ) * NC
            n = (kz * NY + ky) * ROWS
            own = pl.multiple_of((place + c) * ROWS, ROWS)
            other = pl.multiple_of((place + 1 - c) * ROWS, ROWS)
            table[pl.ds(own, ROWS), :] = near[n : n + ROWS, :]
            table[pl.ds(other, ROWS), :] = far[n : n + ROWS, :]
    for i in range(CHUNKS):
        rows = slice(i * CHUNK, (i + 1) * CHUNK)
        taken = table[pl.ds(pl.multiple_of(starts[i], 16), 128), :]
        now = skip[rows, :].astype(F32) + dot(select[rows, :], taken)
        state[rows, :] = now
        xs[rows, :] = (scale[rows, :] * norm(now) + shift[rows, :]).astype(BF16)
    x = xs[...]
    own = slice(RIM, RIM + ATOMS)
    mine = xs[own, :]
    qs[...] = (
        (dot_nt(mine, weights[2]) + offset[1:2, :]) * (LOG2E / math.sqrt(CA // HA))
    ).astype(BF16)
    ks[...] = dot_nt(x, weights[3]).astype(BF16)
    vs[...] = dot_nt(x, weights[4]).astype(BF16)
    gs[...] = sigmoid(dot_nt(mine, weights[5]).astype(BF16).astype(F32))
    width = CA // HA
    head_of_row = lax.broadcasted_iota(jnp.int32, (HA * WQ, CA), 0) // WQ
    head_of_lane = lax.broadcasted_iota(jnp.int32, (HA * WQ, CA), 1) // width
    same = head_of_row == head_of_lane
    lane_head = lax.broadcasted_iota(jnp.int32, (WQ, CA), 1) // width
    key_slot = lax.broadcasted_iota(jnp.int32, (HA * WQ, WK), 1)
    for b in range(ATOMS // WQ):
        rows = slice(b * WQ, (b + 1) * WQ)
        one = qs[rows, :].astype(F32)
        four = jnp.where(same, jnp.concatenate([one] * HA, axis=0), 0.0).astype(BF16)
        span = slice(b * WQ, b * WQ + WK)
        extra = jnp.concatenate([bias[i, rows, :] for i in range(HA)], axis=0).astype(F32)
        scores = dot_nt(four, ks[span, :]) + extra * LOG2E
        base = pos[3] + b * WQ - RIM
        low = bounds[0, b] - base
        high = bounds[1, b] - base
        scores = jnp.where((key_slot >= low) & (key_slot < high), scores, FAR)
        probs = jnp.exp2(scores - jnp.max(scores, axis=1, keepdims=True))
        total = jnp.sum(probs, axis=1, keepdims=True)
        summed = dot(probs.astype(BF16), vs[span, :]) / total
        picked = summed[0:WQ]
        for i in range(1, HA):
            picked = jnp.where(lane_head == i, summed[i * WQ : (i + 1) * WQ], picked)
        at_all[rows, :] = picked
    gated = (at_all[...] * gs[...]).astype(BF16)
    new = state[own, :] + dot_nt(gated, weights[6])
    final = norm(new).astype(BF16)
    out[...] = dot_nt(spots[...], final)


def per_device(
    token_act,
    token_cond,
    pair_bias,
    token_mask,
    ada_weights,
    attention_in,
    attention_out,
    transition_in,
    transition_out,
    token_vectors,
    atom_skip,
    atom_cond,
    atom_bias,
    window_bounds,
    atom_token,
    atom_weights,
    token_to_atom,
    atom_vectors,
    position_out,
):
    f = lax.axis_index("fsdp").astype(jnp.int32)
    t = lax.axis_index("seq").astype(jnp.int32)
    y, z, c = t // (NZ * NC), (t // NC) % NZ, t % NC
    f_pos = f.reshape(1)
    act = token_act[0]

    sent = kernel_call(
        prepare_body,
        "prepare",
        [shape((ROWS, DIM + COLS))] * 4,
        (act, token_cond[0]),
        (f_pos,),
        size=2 << 20,
    )
    normed = [sent[0]] + [x_shift(sent[k], k) for k in (1, 2, 3)]

    span = pair_bias.shape[2] // NY
    cut = jnp.stack([pair_bias[:, :, i * span : (i + 1) * span] for i in range(NY)])
    bias = y_exchange(cut)

    turned = jnp.swapaxes(atom_weights, 1, 2).reshape(7 * 32, CA)
    own_maps = jnp.concatenate([token_to_atom, turned], axis=0)
    skip = atom_skip[0]
    coded = jnp.stack([atom_token // 64, atom_token % 64]).astype(BF16)

    def edge(lo, hi):
        codes = jnp.pad(coded[:, lo:hi], ((0, 14), (0, CA - RIM)))
        return jnp.concatenate([skip[lo:hi], atom_cond[lo:hi], codes], axis=0)

    size = lax.axis_size("seq")
    up = [(i, i + 1) for i in range(size - 1)]
    before = lax.ppermute(edge(ATOMS - RIM, ATOMS), "seq", up)
    after = lax.ppermute(edge(0, RIM), "seq", [(j, i) for i, j in up])

    def decoded(side):
        pair = side[2 * RIM : 2 * RIM + 2, 0:RIM].astype(jnp.int32)
        return pair[0] * 64 + pair[1]

    cond_ext = jnp.concatenate([before[RIM : 2 * RIM], atom_cond, after[RIM : 2 * RIM]], axis=0)
    token_ext = jnp.concatenate([decoded(before), atom_token, decoded(after)])
    by_chunk = token_ext.reshape(CHUNKS, CHUNK)
    token_count = size * ROWS
    starts = jnp.minimum((by_chunk[:, 0] // 16) * 16, token_count - 128)

    offsets = lax.dynamic_slice_in_dim(token_vectors, f * COLS, COLS, 1)
    attend, message = kernel_call(
        adaptive_body,
        "adaptive",
        [shape((ROWS, DIM)), shape((DIM + COLS + 7 * 32, CA))],
        (*normed, ada_weights, offsets[0:2], own_maps),
        flops=4 * 2 * 512 * 768 * 192,
        size=3 << 20,
    )
    attend_all = [attend] + [x_shift(attend, k) for k in (1, 2, 3)]
    q, kv_own, gate = kernel_call(
        project_body,
        "project",
        [shape((ROWS, DIM)), shape((2 * ROWS, DIM)), shape((ROWS, DIM))],
        (*attend_all, attention_in, offsets[2:3], token_mask.reshape(ROWS, 1)),
        (f_pos,),
        flops=4 * 2 * 512 * 768 * 192,
        size=4 << 20,
    )
    q_all = [q] + [y_shift(q, k) for k in (1, 2, 3)]
    near = [kv_own] + [z_shift(kv_own, k) for k in (1, 2, 3)]
    pairs = near + [c_shift(a) for a in near]

    messages = [message] + [x_shift(message, k) for k in (1, 2, 3)]
    ffn = kernel_call(
        hidden_body,
        "hidden",
        shape((NX * ROWS, DIM), F32),
        (*messages, transition_in, transition_out),
        (f_pos,),
        flops=3 * 2 * 512 * 768 * 384,
        size=6 << 20,
    )
    atom_maps, project_full, scale, shift, select = kernel_call(
        atom_first_body,
        "atom_first",
        [
            shape((7, CA, CA)),
            shape((DIM, CA)),
            shape((EXT, CA), F32),
            shape((EXT, CA), F32),
            shape((EXT, 128)),
        ],
        (*messages, cond_ext, by_chunk, atom_vectors),
        (f_pos, starts),
        flops=4 * EXT * CA * CA,
        size=3 << 20,
    )

    out = attention(jnp.stack([y, z, c]), q_all, pairs, bias)
    parts = [out[0]] + [y_shift(out[k], NY - k) for k in (1, 2, 3)]
    sums = kernel_call(
        combine_body,
        "combine",
        [shape((ROWS, DIM), F32)]
        + [shape((ROWS, DIM))] * 3
        + [shape((ROWS, CA), F32)]
        + [shape((ROWS, CA))] * 3,
        (*parts, gate, ffn, attention_out, project_full, act),
        flops=4 * 2 * 128 * 768 * (192 + 128) + 8 * 2 * 128 * 128 * 768,
        size=5 << 20,
    )
    arrived = [x_shift(sums[4 + k], NX - k) for k in (1, 2, 3)]
    rows = (
        sums[4] + arrived[0].astype(F32) + arrived[1].astype(F32) + arrived[2].astype(F32)
    ).astype(BF16)

    by_y = jnp.concatenate([rows] + [y_shift(rows, k) for k in (1, 2, 3)], axis=0)
    by_z = jnp.concatenate([by_y] + [z_shift(by_y, k) for k in (1, 2, 3)], axis=0)
    by_c = c_shift(by_z)
    by_c, *partial = lax.optimization_barrier((by_c, *sums[1:4]))
    main = [x_shift(partial[k - 1], NX - k) for k in (1, 2, 3)]

    scalars = (jnp.stack([y, z, c, t * ATOMS]), starts, window_bounds.T)
    update = kernel_call(
        atom_body,
        "atoms",
        shape((3, ATOMS), F32),
        (
            by_z,
            by_c,
            before,
            skip,
            after,
            scale,
            shift,
            select,
            atom_maps,
            atom_vectors,
            atom_bias,
            position_out,
        ),
        scalars,
        scratch=[
            pltpu.VMEM((token_count, CA), BF16),
            pltpu.VMEM((EXT, CA), BF16),
            pltpu.VMEM((EXT, CA), F32),
            pltpu.VMEM((EXT, CA), BF16),
            pltpu.VMEM((ATOMS, CA), BF16),
            pltpu.VMEM((EXT, CA), BF16),
            pltpu.VMEM((EXT, CA), BF16),
            pltpu.VMEM((ATOMS, CA), F32),
            pltpu.VMEM((ATOMS, CA), F32),
        ],
        flops=2 * 1120 * 128 * 128 * 10,
        size=6 << 20,
    )
    update, *main = lax.optimization_barrier((update, *main))
    token_result = (
        sums[0] + main[0].astype(F32) + main[1].astype(F32) + main[2].astype(F32)
    ).astype(BF16)
    return (token_result[None], update[None])


def solution(mesh):
    in_specs = (
        P(("sample", "fsdp"), "seq", None),
        P(("sample", "fsdp"), "seq", None),
        P("fsdp", "seq", None),
        P("seq"),
        P(None, None, "fsdp"),
        P(None, None, "fsdp"),
        P("fsdp", None),
        P(None, None, "fsdp"),
        P("fsdp", None),
        P(),
        P(("sample", "fsdp"), "seq", None),
        P("seq", None),
        P(None, "seq", None),
        P("seq", None),
        P("seq"),
        P(None, None, "fsdp"),
        P("fsdp", None),
        P(),
        P(),
    )
    out_specs = (P(("sample", "fsdp"), "seq", None), P(("sample", "fsdp"), None, "seq"))
    return jax.shard_map(
        per_device, mesh=mesh, in_specs=in_specs, out_specs=out_specs, check_vma=False
    )
```

```python
import math

import jax
import jax.numpy as jnp
from jax import lax
from jax.experimental import pallas as pl
from jax.experimental.pallas import tpu as pltpu
from jax.sharding import PartitionSpec as P

EPS = 1e-05
FAR = -1e30
SENT = 1e30
LOG2E = 1.4426950408889634
HD = 48
HA = 4
WQ = 32
WK = 128
RIM = 48
NX = 4
NY = 4
NZ = 4
NC = 2
ROWS = 128
DIM = 768
COLS = 192
SLOTS = 4
HALF = SLOTS * COLS
HEADS = 4
ATOMS = 1024
EXT = ATOMS + 2 * RIM
CHUNK = 112
CHUNKS = EXT // CHUNK
CA = 128
F32 = jnp.float32
BF16 = jnp.bfloat16


def x_shift(a, k):
    return lax.ppermute(a, "fsdp", [(i, (i + k) % NX) for i in range(NX)])


def y_shift(a, k):
    group = NZ * NC
    pairs = [(t, ((t // group + k) % NY) * group + t % group) for t in range(NY * group)]
    return lax.ppermute(a, "seq", pairs)


def z_shift(a, k):
    group = NZ * NC
    pairs = [
        (t, (t // group) * group + ((t // NC + k) % NZ) * NC + t % NC) for t in range(NY * group)
    ]
    return lax.ppermute(a, "seq", pairs)


def y_exchange(a):
    group = NZ * NC
    groups = [[y * group + n for y in range(NY)] for n in range(group)]
    return lax.all_to_all(
        a, "seq", split_axis=0, concat_axis=0, axis_index_groups=groups, tiled=True
    )


def y_collect(a):
    group = NZ * NC
    groups = [[y * group + n for y in range(NY)] for n in range(group)]
    return lax.all_gather(a, "seq", axis=0, axis_index_groups=groups)


def c_shift(a):
    return lax.ppermute(a, "seq", [(t, t ^ 1) for t in range(NY * NZ * NC)])


def norm(values):
    center = values - jnp.mean(values, axis=-1, keepdims=True)
    spread = jnp.mean(center * center, axis=-1, keepdims=True)
    return center * lax.rsqrt(spread + EPS)


def sigmoid(v):
    return 1.0 / (1.0 + jnp.exp(-v))


def dot(a, b):
    return jnp.dot(a, b, preferred_element_type=F32)


def dot_nt(a, b):
    return lax.dot_general(a, b, (((1,), (1,)), ((), ())), preferred_element_type=F32)


def kernel_call(body, name, out_shape, args, scalars=(), scratch=(), flops=0, size=0, free=0):
    def whole(a):
        return pl.BlockSpec(
            a.shape, lambda i, n=len(a.shape): (0,) * n, pipeline_mode=pl.Buffered(1)
        )

    args = [
        a if i < free else pltpu.with_memory_space_constraint(a, pltpu.HBM)
        for i, a in enumerate(args)
    ]
    return pl.pallas_call(
        body,
        grid=(1,),
        out_shape=out_shape,
        in_specs=[pl.BlockSpec(memory_space=pltpu.SMEM)] * len(scalars) + [whole(a) for a in args],
        out_specs=jax.tree.map(whole, out_shape),
        scratch_shapes=list(scratch),
        compiler_params=pltpu.CompilerParams(
            dimension_semantics=("arbitrary",), vmem_limit_bytes=24 << 20
        ),
        cost_estimate=pl.CostEstimate(flops=flops, bytes_accessed=size, transcendentals=0),
        name=name,
    )(*scalars, *args)


def shape(dims, kind=BF16):
    return pltpu.HBM(dims, kind)


def sent_shape(dims, kind=BF16):
    return jax.ShapeDtypeStruct(dims, kind)


def prepare_body(pos, act, cond, *outs):
    f = pos[0]
    normed = norm(cond[...].astype(F32)).astype(BF16)
    hat = norm(act[...].astype(F32))
    for k in range(NX):
        dest = lax.rem(f + k, NX)
        part = hat[:, 0:COLS]
        for j in range(1, NX):
            part = jnp.where(dest == j, hat[:, j * COLS : (j + 1) * COLS], part)
        outs[k][:, 0:DIM] = normed
        outs[k][:, DIM : DIM + COLS] = part.astype(BF16)


def adaptive_body(m0, m1, m2, m3, ada, offset, maps, attend, message):
    parts = (m0, m1, m2, m3)
    normed = jnp.concatenate([m[:, 0:DIM] for m in parts], axis=0)
    hat = jnp.concatenate([m[:, DIM : DIM + COLS] for m in parts], axis=0).astype(F32)
    message[DIM:, :] = maps[...]
    for n in range(2):
        scale = sigmoid(dot(normed, ada[2 * n]) + offset[n : n + 1, :])
        result = (scale * hat + dot(normed, ada[2 * n + 1])).astype(BF16)
        wide = jnp.concatenate([result[k * ROWS : (k + 1) * ROWS] for k in range(NX)], axis=1)
        if n == 0:
            attend[...] = wide
        else:
            for i in range(DIM // 128):
                message[i * ROWS : (i + 1) * ROWS, :] = wide[:, i * 128 : (i + 1) * 128]


def gathered_rows(part, j):
    return jnp.concatenate(
        [part[:, ((r - j) % NX) * COLS : ((r - j) % NX + 1) * COLS] for r in range(NX)],
        axis=0,
    )


def project_body(pos, a0, a1, a2, a3, weights, offset, mask, q, kv, g):
    f = pos[0]
    parts = (a0, a1, a2, a3)
    sums = [None] * 4
    for j in range(NX):
        rows = gathered_rows(parts[j][...], j)
        at = pl.multiple_of(lax.rem(f + NX - j, NX) * COLS, COLS)
        for n in range(4):
            term = dot(rows, weights[n, pl.ds(at, COLS), :])
            sums[n] = term if j == 0 else sums[n] + term
    live = mask[...] > 0
    for r in range(NX):
        own = slice(r * ROWS, (r + 1) * ROWS)
        to = slice(r * COLS, (r + 1) * COLS)
        q[:, to] = ((sums[0][own] + offset[0:1, :]) * (LOG2E / math.sqrt(HD))).astype(BF16)
        kv[0:ROWS, to] = jnp.where(live, sums[1][own], SENT).astype(BF16)
        kv[ROWS:, to] = sums[2][own].astype(BF16)
        g[:, to] = sums[3][own].astype(BF16)


def hidden_body(pos, parts, w_in, w_out, out):
    f = pos[0]
    gate, up = None, None
    for j in range(NX):
        src = lax.rem(f + NX - j, NX)
        wide = jnp.concatenate(
            [parts[src, i * ROWS : (i + 1) * ROWS, :] for i in range(DIM // 128)], axis=1
        )
        rows = gathered_rows(wide, j)
        at = pl.multiple_of(src * COLS, COLS)
        gate_term = dot(rows, w_in[0, pl.ds(at, COLS), :])
        up_term = dot(rows, w_in[1, pl.ds(at, COLS), :])
        gate = gate_term if j == 0 else gate + gate_term
        up = up_term if j == 0 else up + up_term
    hidden = (gate / (1.0 + jnp.exp(-gate)) * up).astype(BF16)
    out[...] = dot(hidden, w_out[...])


KEYS = NZ * NC * ROWS


def attention_body(pos, *refs):
    q = refs[0]
    pairs = refs[1:9]
    bias = refs[9]
    out = refs[10:14]
    q_all, key_all, value_all, far_row, bias_all, stats, probs = refs[14:21]
    scores = refs[21:23]
    h = pl.program_id(0)

    @pl.when(h == 0)
    def _():
        unit = (lax.broadcasted_iota(jnp.int32, (8, 128), 1) == 0).astype(F32).astype(BF16)
        for side in range(2):
            core = pos[2] if side == 0 else 1 - pos[2]
            for n in range(NZ):
                block = pairs[side * NZ + n][0:ROWS, :]
                place = lax.rem(pos[1] + NZ - n, NZ) * NC + core
                at = pl.multiple_of(place * ROWS, ROWS)
                first = dot_nt(unit, block[:, 0:128])
                far_row[:, pl.ds(at, ROWS)] = jnp.where(first > 1e20, FAR, 0.0)
                wide = block.astype(F32)
                key_all[pl.ds(at, ROWS), :] = jnp.where(wide[:, 0:1] > 1e20, 0.0, wide).astype(BF16)
                value_all[pl.ds(at, ROWS), :] = pairs[side * NZ + n][ROWS:, :]
        for n in range(NY):
            q_all[n * ROWS : (n + 1) * ROWS, :] = q[lax.rem(pos[0] + NY - n, NY)]
        stats[...] = jnp.zeros_like(stats)

    for n in range(NY):
        part = bias[lax.rem(pos[0] + NY - n, NY), 0]
        bias_all[n] = part.astype(F32) * LOG2E + far_row[0:1, :]

    lane = lax.broadcasted_iota(jnp.int32, (NY * ROWS, 256), 1)
    slot = lax.broadcasted_iota(jnp.int32, (ROWS, 128), 1)
    windows, mines, rows = [], [], []
    for s in range(SLOTS):
        lane0 = COLS * s + HD * h
        start = jnp.minimum(lane0 // 128, (HALF - 256) // 128)
        off = lane0 - start * 128
        window = pl.ds(pl.multiple_of(start * 128, 128), 256)
        mine = (lane >= off) & (lane < off + HD)
        windows.append(window)
        mines.append(mine)
        rows.append(jnp.where(mine, q_all[:, window].astype(F32), 0.0).astype(BF16))

    tile = KEYS // NY

    def score(s, j):
        keys = slice(j * tile, (j + 1) * tile)
        scores[s % 2][:, keys] = dot_nt(rows[s], key_all[keys, windows[s]])

    for j in range(NY):
        score(0, j)
    for s in range(SLOTS):
        index = s * HEADS + h
        of_max = (lax.rem(slot, 16) == index) & (slot < 48)
        of_total = (lax.rem(slot, 16) == index) & (slot >= 48) & (slot < 96)
        totals = []
        for n in range(NY):
            if s + 1 < SLOTS:
                score(s + 1, n)
            own = slice(n * ROWS, (n + 1) * ROWS)
            part = scores[s % 2][own, :] + bias_all[n]
            top = jnp.max(part, axis=1, keepdims=True)
            part = jnp.exp2(part - top)
            total = jnp.sum(part, axis=1, keepdims=True)
            probs[own, :] = part.astype(BF16)
            totals.append(total)
            stats[n] = jnp.where(of_max, top, jnp.where(of_total, total, stats[n]))
        summed = dot(probs[...], value_all[:, windows[s]])
        for n in range(NY):
            own = slice(n * ROWS, (n + 1) * ROWS)
            scaled = summed[own] * (1.0 / totals[n])
            before = out[n][:, windows[s]].astype(F32)
            out[n][:, windows[s]] = jnp.where(mines[s][own], scaled, before).astype(BF16)

    @pl.when(h == HEADS - 1)
    def _():
        third = lax.rem(slot // 16, 3)
        for n in range(NY):
            whole = stats[n]
            high = whole.astype(BF16).astype(F32)
            rest = whole - high
            middle = rest.astype(BF16).astype(F32)
            low = rest - middle
            sent = jnp.where(third == 0, high, jnp.where(third == 1, middle, low))
            out[n][:, HALF : HALF + 128] = sent.astype(BF16)


def attention(pos, q, pairs, bias):
    once = pl.Buffered(1)
    in_specs = [pl.BlockSpec(memory_space=pltpu.SMEM)]
    in_specs += [pl.BlockSpec((NY, ROWS, DIM), lambda h: (0, 0, 0), pipeline_mode=once)]
    in_specs += [pl.BlockSpec((2 * ROWS, HALF), lambda h: (0, 0), pipeline_mode=once)] * 8
    in_specs += [pl.BlockSpec((NY, 1, ROWS, KEYS), lambda h: (0, h, 0, 0))]
    return pl.pallas_call(
        attention_body,
        grid=(HEADS,),
        out_shape=[shape((ROWS, HALF + 128))] * 4,
        in_specs=in_specs,
        out_specs=[pl.BlockSpec((ROWS, HALF + 128), lambda h: (0, 0))] * 4,
        scratch_shapes=[
            pltpu.VMEM((NY * ROWS, HALF), BF16),
            pltpu.VMEM((KEYS, HALF), BF16),
            pltpu.VMEM((KEYS, HALF), BF16),
            pltpu.VMEM((8, KEYS), F32),
            pltpu.VMEM((NY, ROWS, KEYS), F32),
            pltpu.VMEM((NY, ROWS, 128), F32),
            pltpu.VMEM((NY * ROWS, KEYS), BF16),
            pltpu.VMEM((NY * ROWS, KEYS), F32),
            pltpu.VMEM((NY * ROWS, KEYS), F32),
        ],
        compiler_params=pltpu.CompilerParams(
            dimension_semantics=("arbitrary",), vmem_limit_bytes=36 << 20
        ),
        cost_estimate=pl.CostEstimate(
            flops=SLOTS * 4 * 512 * 1024 * 512 * 2,
            bytes_accessed=6 << 20,
            transcendentals=4 << 20,
        ),
        name="attention",
    )(pos, *(pltpu.with_memory_space_constraint(a, pltpu.HBM) for a in (q, *pairs, bias)))


def combined(parts):
    tops, totals = [], []
    for o in parts:
        sent = o[:, HALF : HALF + 128].astype(F32)
        whole = sent + pltpu.roll(sent, 128 - 16, 1) + pltpu.roll(sent, 128 - 32, 1)
        tops.append(whole)
        totals.append(pltpu.roll(whole, 128 - 48, 1))
    used = lax.broadcasted_iota(jnp.int32, (ROWS, 128), 1) < SLOTS * HEADS
    tops = [jnp.where(used, t, 0.0) for t in tops]
    totals = [jnp.where(used, t, 1.0) for t in totals]
    top = jnp.maximum(jnp.maximum(tops[0], tops[1]), jnp.maximum(tops[2], tops[3]))
    shares = [n * jnp.exp2(t - top) for t, n in zip(tops, totals)]
    inverse = 1.0 / (shares[0] + shares[1] + shares[2] + shares[3])
    head = lax.broadcasted_iota(jnp.int32, (128, HALF), 0) * HD
    lane = lax.broadcasted_iota(jnp.int32, (128, HALF), 1)
    spread = ((lane >= head) & (lane < head + HD)).astype(F32).astype(BF16)
    attended = None
    for o, share in zip(parts, shares):
        share = share * inverse
        high = share.astype(BF16)
        low = (share - high.astype(F32)).astype(BF16)
        term = (dot(high, spread) + dot(low, spread)) * o[:, 0:HALF].astype(F32)
        attended = term if attended is None else attended + term
    return attended


def combine_body(*refs):
    gate, ffn, w_out, w_atom, act = refs[4:9]
    outs = refs[9:]
    attended = combined(refs[0:4])
    gated = (attended * sigmoid(gate[...].astype(F32))).astype(BF16)
    for r in range(NX):
        part = dot(gated[:, r * COLS : (r + 1) * COLS], w_out[...]) + ffn[r * ROWS : (r + 1) * ROWS]
        small = part.astype(BF16)
        rows = dot(small, w_atom[...])
        if r == 0:
            outs[0][...] = part + act[...].astype(F32)
            outs[4][...] = rows + dot(act[...], w_atom[...])
        else:
            outs[r][...] = small
            outs[4 + r][...] = rows.astype(BF16)


def atom_first_body(starts, maps, cond, tokens, offset, *outs):
    weights, project, scale, shift, select = outs
    for src in range(NX):
        project[src * COLS : (src + 1) * COLS, :] = maps[src, DIM : DIM + COLS, :]
        for i in range(7):
            line = DIM + COLS + i * 32
            weights[i, src * 32 : (src + 1) * 32, :] = maps[src, line : line + 32, :]
    normed = norm(cond[...].astype(F32)).astype(BF16)
    scale[...] = sigmoid(dot_nt(normed, weights[0]) + offset[0:1, :])
    shift[...] = dot_nt(normed, weights[1])
    row = lax.broadcasted_iota(jnp.int32, (128, CHUNK), 0)
    for i in range(CHUNKS):
        hit = ((row + starts[i]) == tokens[i : i + 1, :]).astype(F32)
        select[i * CHUNK : (i + 1) * CHUNK, :] = hit.T.astype(BF16)


def atom_body(pos, starts, bounds, near, far, before, own_skip, after, *refs):
    scale, shift, select, weights, offset, bias, spots, out = refs[0:8]
    table, skip, state, xs, qs, ks, vs, gs, at_all = refs[8:]
    skip[0:RIM, :] = before[0:RIM, :]
    skip[RIM : RIM + ATOMS, :] = own_skip[...]
    skip[RIM + ATOMS :, :] = after[0:RIM, :]
    y, z, c = pos[0], pos[1], pos[2]
    for ky in range(NY):
        for kz in range(NZ):
            place = lax.rem(y + NY - ky, NY) * (NZ * NC) + lax.rem(z + NZ - kz, NZ) * NC
            n = (kz * NY + ky) * ROWS
            own = pl.multiple_of((place + c) * ROWS, ROWS)
            other = pl.multiple_of((place + 1 - c) * ROWS, ROWS)
            table[pl.ds(own, ROWS), :] = near[n : n + ROWS, :]
            table[pl.ds(other, ROWS), :] = far[n : n + ROWS, :]
    for i in range(CHUNKS):
        rows = slice(i * CHUNK, (i + 1) * CHUNK)
        taken = table[pl.ds(pl.multiple_of(starts[i], 16), 128), :]
        now = skip[rows, :].astype(F32) + dot(select[rows, :], taken)
        state[rows, :] = now
        xs[rows, :] = (scale[rows, :] * norm(now) + shift[rows, :]).astype(BF16)
    x = xs[...]
    own = slice(RIM, RIM + ATOMS)
    mine = xs[own, :]
    qs[...] = (
        (dot_nt(mine, weights[2]) + offset[1:2, :]) * (LOG2E / math.sqrt(CA // HA))
    ).astype(BF16)
    ks[...] = dot_nt(x, weights[3]).astype(BF16)
    vs[...] = dot_nt(x, weights[4]).astype(BF16)
    gs[...] = sigmoid(dot_nt(mine, weights[5]).astype(BF16).astype(F32))
    width = CA // HA
    head_of_row = lax.broadcasted_iota(jnp.int32, (HA * WQ, CA), 0) // WQ
    head_of_lane = lax.broadcasted_iota(jnp.int32, (HA * WQ, CA), 1) // width
    same = head_of_row == head_of_lane
    lane_head = lax.broadcasted_iota(jnp.int32, (WQ, CA), 1) // width
    key_slot = lax.broadcasted_iota(jnp.int32, (HA * WQ, WK), 1)

    def window(b):
        rows = pl.ds(pl.multiple_of(b * WQ, WQ), WQ)
        span = pl.ds(pl.multiple_of(b * WQ, WQ), WK)
        one = qs[rows, :].astype(F32)
        four = jnp.where(same, jnp.concatenate([one] * HA, axis=0), 0.0).astype(BF16)
        extra = jnp.concatenate([bias[i, rows, :] for i in range(HA)], axis=0).astype(F32)
        scores = dot_nt(four, ks[span, :]) + extra * LOG2E
        base = pos[3] + b * WQ - RIM
        low = bounds[0, b] - base
        high = bounds[1, b] - base
        scores = jnp.where((key_slot >= low) & (key_slot < high), scores, FAR)
        probs = jnp.exp2(scores - jnp.max(scores, axis=1, keepdims=True))
        total = jnp.sum(probs, axis=1, keepdims=True)
        summed = dot(probs.astype(BF16), vs[span, :]) * (1.0 / total)
        picked = summed[0:WQ]
        for i in range(1, HA):
            picked = jnp.where(lane_head == i, summed[i * WQ : (i + 1) * WQ], picked)
        at_all[rows, :] = picked

    def windows(step, carry):
        for i in range(8):
            window(step * 8 + i)
        return carry

    lax.fori_loop(0, ATOMS // WQ // 8, windows, 0)
    gated = (at_all[...] * gs[...]).astype(BF16)
    new = state[own, :] + dot_nt(gated, weights[6])
    final = norm(new).astype(BF16)
    update = dot_nt(spots[...], final)
    for i in range(3):
        out[i] = update[i : i + 1, :]


def per_device(
    token_act,
    token_cond,
    pair_bias,
    token_mask,
    ada_weights,
    attention_in,
    attention_out,
    transition_in,
    transition_out,
    token_vectors,
    atom_skip,
    atom_cond,
    atom_bias,
    window_bounds,
    atom_token,
    atom_weights,
    token_to_atom,
    atom_vectors,
    position_out,
):
    f = lax.axis_index("fsdp").astype(jnp.int32)
    t = lax.axis_index("seq").astype(jnp.int32)
    y, z, c = t // (NZ * NC), (t // NC) % NZ, t % NC
    f_pos = f.reshape(1)
    act = token_act[0]

    sent = kernel_call(
        prepare_body,
        "prepare",
        [sent_shape((ROWS, DIM + COLS))] * 4,
        (act, token_cond[0]),
        (f_pos,),
        size=2 << 20,
    )
    normed = [sent[0]] + [x_shift(sent[k], k) for k in (1, 2, 3)]
    edge_skip, edge_cond, edge_token, _ = lax.optimization_barrier(
        (atom_skip[0], atom_cond, atom_token, sent[0])
    )

    turned = jnp.swapaxes(atom_weights, 1, 2).reshape(7 * 32, CA)
    own_maps = jnp.concatenate([token_to_atom, turned], axis=0)
    skip = atom_skip[0]
    coded = jnp.stack([edge_token // 64, edge_token % 64]).astype(BF16)

    def edge(lo, hi):
        codes = jnp.pad(coded[:, lo:hi], ((0, 14), (0, CA - RIM)))
        return jnp.concatenate([edge_skip[lo:hi], edge_cond[lo:hi], codes], axis=0)

    size = lax.axis_size("seq")
    up = [(i, i + 1) for i in range(size - 1)]
    before = lax.ppermute(edge(ATOMS - RIM, ATOMS), "seq", up)
    after = lax.ppermute(edge(0, RIM), "seq", [(j, i) for i, j in up])

    span = pair_bias.shape[2] // NY
    cut = jnp.stack([pair_bias[:, :, i * span : (i + 1) * span] for i in range(NY)])
    bias = y_exchange(cut)

    def decoded(side):
        pair = side[2 * RIM : 2 * RIM + 2, 0:RIM].astype(jnp.int32)
        return pair[0] * 64 + pair[1]

    cond_ext = jnp.concatenate([before[RIM : 2 * RIM], atom_cond, after[RIM : 2 * RIM]], axis=0)
    token_ext = jnp.concatenate([decoded(before), atom_token, decoded(after)])
    by_chunk = token_ext.reshape(CHUNKS, CHUNK)
    token_count = size * ROWS
    starts = jnp.minimum((by_chunk[:, 0] // 16) * 16, token_count - 128)

    offsets = lax.dynamic_slice_in_dim(token_vectors, f * COLS, COLS, 1)
    attend, message = kernel_call(
        adaptive_body,
        "adaptive",
        [sent_shape((ROWS, DIM)), shape((DIM + COLS + 7 * 32, CA))],
        (*normed, ada_weights, offsets[0:2], own_maps),
        free=4,
        flops=4 * 2 * 512 * 768 * 192,
        size=3 << 20,
    )
    attend_all = [attend] + [x_shift(attend, k) for k in (1, 2, 3)]
    q, kv, gate = kernel_call(
        project_body,
        "project",
        [sent_shape((ROWS, DIM)), sent_shape((2 * ROWS, DIM)), shape((ROWS, DIM))],
        free=4,
        args=(*attend_all, attention_in, offsets[2:3], token_mask.reshape(ROWS, 1)),
        scalars=(f_pos,),
        flops=4 * 2 * 512 * 768 * 192,
        size=4 << 20,
    )
    near = [kv] + [z_shift(kv, k) for k in (1, 2, 3)]
    pairs = near + [c_shift(a) for a in near]
    q, _ = lax.optimization_barrier((q, pairs[NZ]))
    q_all = y_collect(q)

    message, _ = lax.optimization_barrier((message, q))
    messages = lax.all_gather(message, "fsdp", axis=0)
    ffn = kernel_call(
        hidden_body,
        "hidden",
        shape((NX * ROWS, DIM), F32),
        (messages, transition_in, transition_out),
        (f_pos,),
        flops=3 * 2 * 512 * 768 * 384,
        size=6 << 20,
    )
    atom_maps, project_full, scale, shift, select = kernel_call(
        atom_first_body,
        "atom_first",
        [
            shape((7, CA, CA)),
            shape((DIM, CA)),
            shape((EXT, CA), F32),
            shape((EXT, CA), F32),
            shape((EXT, 128)),
        ],
        (messages, cond_ext, by_chunk, atom_vectors),
        (starts,),
        flops=4 * EXT * CA * CA,
        size=3 << 20,
    )

    place = jnp.stack([y, z, c])
    out = attention(place, q_all, pairs, bias)
    parts = [out[0]] + [y_shift(out[k], NY - k) for k in (1, 2, 3)]
    sums = kernel_call(
        combine_body,
        "combine",
        [shape((ROWS, DIM), F32)]
        + [sent_shape((ROWS, DIM))] * 3
        + [sent_shape((ROWS, CA), F32)]
        + [sent_shape((ROWS, CA))] * 3,
        (*parts, gate, ffn, attention_out, project_full, act),
        free=4,
        flops=4 * 2 * 128 * 768 * (192 + 128) + 8 * 2 * 128 * 128 * 768,
        size=5 << 20,
    )
    arrived = [x_shift(sums[4 + k], NX - k) for k in (1, 2, 3)]
    rows = (
        sums[4] + arrived[0].astype(F32) + arrived[1].astype(F32) + arrived[2].astype(F32)
    ).astype(BF16)

    turns = [y_shift(rows, k) for k in (1, 2, 3)]
    by_y = jnp.concatenate([rows] + turns, axis=0)
    _, *partial = lax.optimization_barrier((by_y, *sums[1:4]))
    main = [x_shift(partial[k - 1], NX - k) for k in (1, 2, 3)]
    turns = [z_shift(by_y, k) for k in (1, 2, 3)]
    turns, main = lax.optimization_barrier((turns, main))
    by_z = jnp.concatenate([by_y] + turns, axis=0)
    token_result = (
        sums[0] + main[0].astype(F32) + main[1].astype(F32) + main[2].astype(F32)
    ).astype(BF16)
    by_c = c_shift(by_z)
    by_c, token_result = lax.optimization_barrier((by_c, token_result))

    scalars = (jnp.stack([y, z, c, t * ATOMS]), starts, window_bounds.T)
    update = kernel_call(
        atom_body,
        "atoms",
        shape((3, 1, ATOMS), F32),
        (
            by_z,
            by_c,
            before,
            skip,
            after,
            scale,
            shift,
            select,
            atom_maps,
            atom_vectors,
            atom_bias,
            position_out,
        ),
        scalars,
        free=2,
        scratch=[
            pltpu.VMEM((token_count, CA), BF16),
            pltpu.VMEM((EXT, CA), BF16),
            pltpu.VMEM((EXT, CA), F32),
            pltpu.VMEM((EXT, CA), BF16),
            pltpu.VMEM((ATOMS, CA), BF16),
            pltpu.VMEM((EXT, CA), BF16),
            pltpu.VMEM((EXT, CA), BF16),
            pltpu.VMEM((ATOMS, CA), F32),
            pltpu.VMEM((ATOMS, CA), F32),
        ],
        flops=2 * 1120 * 128 * 128 * 10,
        size=6 << 20,
    )
    return (token_result[None], jnp.swapaxes(update, 0, 1))


def solution(mesh):
    in_specs = (
        P(("sample", "fsdp"), "seq", None),
        P(("sample", "fsdp"), "seq", None),
        P("fsdp", "seq", None),
        P("seq"),
        P(None, None, "fsdp"),
        P(None, None, "fsdp"),
        P("fsdp", None),
        P(None, None, "fsdp"),
        P("fsdp", None),
        P(),
        P(("sample", "fsdp"), "seq", None),
        P("seq", None),
        P(None, "seq", None),
        P("seq", None),
        P("seq"),
        P(None, None, "fsdp"),
        P("fsdp", None),
        P(),
        P(),
    )
    out_specs = (P(("sample", "fsdp"), "seq", None), P(("sample", "fsdp"), None, "seq"))
    return jax.shard_map(
        per_device, mesh=mesh, in_specs=in_specs, out_specs=out_specs, check_vma=False
    )
```

```python
import functools
import math

import jax
import jax.numpy as jnp
from jax import lax
from jax.experimental import pallas as pl
from jax.experimental.pallas import tpu as pltpu
from jax.sharding import PartitionSpec as P

EPS = 1e-05
FAR = -1e30
SENT = 1e30
LOG2E = 1.4426950408889634
HD = 48
HA = 4
WQ = 32
WK = 128
RIM = 48
NX = 4
NY = 4
NZ = 4
NC = 2
ROWS = 128
DIM = 768
COLS = 192
HEADS = 4
ATOMS = 1024
EXT = ATOMS + 2 * RIM
CHUNK = 112
CHUNKS = EXT // CHUNK
CA = 128
F32 = jnp.float32
BF16 = jnp.bfloat16


def x_shift(a, k):
    return lax.ppermute(a, "fsdp", [(i, (i + k) % NX) for i in range(NX)])


def y_shift(a, k):
    group = NZ * NC
    pairs = [(t, ((t // group + k) % NY) * group + t % group) for t in range(NY * group)]
    return lax.ppermute(a, "seq", pairs)


def z_shift(a, k):
    group = NZ * NC
    pairs = [
        (t, (t // group) * group + ((t // NC + k) % NZ) * NC + t % NC) for t in range(NY * group)
    ]
    return lax.ppermute(a, "seq", pairs)


def z_swap(a, k):
    return lax.ppermute(a, "seq", [(t, t ^ (NC * k)) for t in range(NY * NZ * NC)])


def y_exchange(a):
    group = NZ * NC
    groups = [[y * group + n for y in range(NY)] for n in range(group)]
    return lax.all_to_all(
        a, "seq", split_axis=0, concat_axis=0, axis_index_groups=groups, tiled=True
    )


def y_collect(a):
    group = NZ * NC
    groups = [[y * group + n for y in range(NY)] for n in range(group)]
    return lax.all_gather(a, "seq", axis=0, axis_index_groups=groups)


def c_shift(a):
    return lax.ppermute(a, "seq", [(t, t ^ 1) for t in range(NY * NZ * NC)])


def norm(values):
    center = values - jnp.mean(values, axis=-1, keepdims=True)
    spread = jnp.mean(center * center, axis=-1, keepdims=True)
    return center * lax.rsqrt(spread + EPS)


def sigmoid(v):
    return 1.0 / (1.0 + jnp.exp(-v))


def dot(a, b):
    return jnp.dot(a, b, preferred_element_type=F32)


def dot_nt(a, b):
    return lax.dot_general(a, b, (((1,), (1,)), ((), ())), preferred_element_type=F32)


def kernel_call(body, name, out_shape, args, scalars=(), scratch=(), flops=0, size=0, free=0):
    def whole(a):
        return pl.BlockSpec(
            a.shape, lambda i, n=len(a.shape): (0,) * n, pipeline_mode=pl.Buffered(1)
        )

    args = [
        a if i < free else pltpu.with_memory_space_constraint(a, pltpu.HBM)
        for i, a in enumerate(args)
    ]
    return pl.pallas_call(
        body,
        grid=(1,),
        out_shape=out_shape,
        in_specs=[pl.BlockSpec(memory_space=pltpu.SMEM)] * len(scalars) + [whole(a) for a in args],
        out_specs=jax.tree.map(whole, out_shape),
        scratch_shapes=list(scratch),
        compiler_params=pltpu.CompilerParams(
            dimension_semantics=("arbitrary",), vmem_limit_bytes=24 << 20
        ),
        cost_estimate=pl.CostEstimate(flops=flops, bytes_accessed=size, transcendentals=0),
        name=name,
    )(*scalars, *args)


def shape(dims, kind=BF16):
    return pltpu.HBM(dims, kind)


def sent_shape(dims, kind=BF16):
    return jax.ShapeDtypeStruct(dims, kind)


def prepare_body(pos, act, cond, bias, *refs):
    outs, cut, sems = refs[0:4], refs[4], refs[5]
    copies = []
    for i in range(NY):
        copies.append(
            pltpu.make_async_copy(bias.at[:, :, pl.ds(i * KEYS, KEYS)], cut.at[i], sems.at[i])
        )
        copies[i].start()
    f = pos[0]
    normed = norm(cond[...].astype(F32)).astype(BF16)
    hat = norm(act[...].astype(F32))
    for k in range(NX):
        dest = lax.rem(f + k, NX)
        part = hat[:, 0:COLS]
        for j in range(1, NX):
            part = jnp.where(dest == j, hat[:, j * COLS : (j + 1) * COLS], part)
        outs[k][:, 0:DIM] = normed
        outs[k][:, DIM : DIM + COLS] = part.astype(BF16)
    for copy in copies:
        copy.wait()


def adaptive_body(m0, m1, m2, m3, ada, offset, maps, attend, message):
    parts = (m0, m1, m2, m3)
    normed = jnp.concatenate([m[:, 0:DIM] for m in parts], axis=0)
    hat = jnp.concatenate([m[:, DIM : DIM + COLS] for m in parts], axis=0).astype(F32)
    message[DIM:, :] = maps[...]
    for n in range(2):
        scale = sigmoid(dot(normed, ada[2 * n]) + offset[n : n + 1, :])
        result = (scale * hat + dot(normed, ada[2 * n + 1])).astype(BF16)
        wide = jnp.concatenate([result[k * ROWS : (k + 1) * ROWS] for k in range(NX)], axis=1)
        if n == 0:
            attend[...] = wide
        else:
            for i in range(DIM // 128):
                message[i * ROWS : (i + 1) * ROWS, :] = wide[:, i * 128 : (i + 1) * 128]


def gathered_rows(part, j):
    return jnp.concatenate(
        [part[:, ((r - j) % NX) * COLS : ((r - j) % NX + 1) * COLS] for r in range(NX)],
        axis=0,
    )


def project_body(pos, a0, a1, a2, a3, weights, offset, mask, q, kv, g):
    f = pos[0]
    parts = (a0, a1, a2, a3)
    sums = [None] * 4
    for j in range(NX):
        rows = gathered_rows(parts[j][...], j)
        at = pl.multiple_of(lax.rem(f + NX - j, NX) * COLS, COLS)
        for n in range(4):
            term = dot(rows, weights[n, pl.ds(at, COLS), :])
            sums[n] = term if j == 0 else sums[n] + term
    live = mask[...] > 0
    for r in range(NX):
        own = slice(r * ROWS, (r + 1) * ROWS)
        to = slice(r * COLS, (r + 1) * COLS)
        q[:, to] = ((sums[0][own] + offset[0:1, :]) * (LOG2E / math.sqrt(HD))).astype(BF16)
        kv[0:ROWS, to] = jnp.where(live, sums[1][own], SENT).astype(BF16)
        kv[ROWS:, to] = sums[2][own].astype(BF16)
        g[:, to] = sums[3][own].astype(BF16)


def hidden_body(pos, w_in, w_out, parts, out):
    f = pos[0]
    gate, up = None, None
    for j in range(NX):
        src = lax.rem(f + NX - j, NX)
        wide = jnp.concatenate(
            [parts[src, i * ROWS : (i + 1) * ROWS, :] for i in range(DIM // 128)], axis=1
        )
        rows = gathered_rows(wide, j)
        at = pl.multiple_of(src * COLS, COLS)
        gate_term = dot(rows, w_in[0, pl.ds(at, COLS), :])
        up_term = dot(rows, w_in[1, pl.ds(at, COLS), :])
        gate = gate_term if j == 0 else gate + gate_term
        up = up_term if j == 0 else up + up_term
    hidden = (gate / (1.0 + jnp.exp(-gate)) * up).astype(BF16)
    out[...] = dot(hidden, w_out[...])


KEYS = NZ * NC * ROWS
PART = KEYS // 2


def spread_heads(first):
    head = (lax.broadcasted_iota(jnp.int32, (128, DIM), 0) - first) * HD
    lane = lax.broadcasted_iota(jnp.int32, (128, DIM), 1)
    return ((lane >= head) & (lane < head + HD)).astype(F32).astype(BF16)


def spread_rows(share, spread):
    high = share.astype(BF16)
    low = (share - high.astype(F32)).astype(BF16)
    return dot(high, spread) + dot(low, spread)


def attention_body(merge, pos, q, *refs):
    pairs = refs[0:4]
    bias = refs[4]
    refs = refs[5:]
    if merge:
        earlier, earlier_stats, refs = refs[0:4], refs[4:8], refs[8:]
        out, refs = refs[0:4], refs[4:]
    else:
        out, out_stats, refs = refs[0:4], refs[4:8], refs[8:]
    q_all, key_all, value_all, far_row, bias_all, stats, probs, total_all = refs[0:8]
    scores = refs[8:10]
    h = pl.program_id(0)
    y = pos[0]

    @pl.when(h == 0)
    def _():
        unit = (lax.broadcasted_iota(jnp.int32, (8, 128), 1) == 0).astype(F32).astype(BF16)
        for i in range(4):
            at = slice(i * ROWS, (i + 1) * ROWS)
            block = pairs[i][0:ROWS, :]
            first = dot_nt(unit, block[:, 0:128])
            far_row[:, at] = jnp.where(first > 1e20, FAR, 0.0)
            wide = block.astype(F32)
            key_all[at, :] = jnp.where(wide[:, 0:1] > 1e20, 0.0, wide).astype(BF16)
            value_all[at, :] = pairs[i][ROWS:, :]
        for n in range(NY):
            q_all[n * ROWS : (n + 1) * ROWS, :] = q[lax.rem(y + NY - n, NY)]
        stats[...] = jnp.zeros_like(stats)

    for n in range(NY):
        src = lax.rem(y + NY - n, NY)
        for i in range(4):
            at = slice(i * ROWS, (i + 1) * ROWS)
            part = bias[src, 0, :, pl.ds(pl.multiple_of(pos[1 + i] * ROWS, ROWS), ROWS)]
            bias_all[n, :, at] = part.astype(F32) * LOG2E + far_row[0:1, at]

    lane = lax.broadcasted_iota(jnp.int32, (NY * ROWS, 256), 1)
    slot = lax.broadcasted_iota(jnp.int32, (ROWS, 128), 1)
    windows, mines, rows = [], [], []
    for s in range(NX):
        lane0 = COLS * s + HD * h
        start = jnp.minimum(lane0 // 128, (DIM - 256) // 128)
        off = lane0 - start * 128
        window = pl.ds(pl.multiple_of(start * 128, 128), 256)
        mine = (lane >= off) & (lane < off + HD)
        windows.append(window)
        mines.append(mine)
        rows.append(jnp.where(mine, q_all[:, window].astype(F32), 0.0).astype(BF16))

    def score(s, j):
        keys = slice(j * 256, (j + 1) * 256)
        scores[s % 2][:, keys] = dot_nt(rows[s], key_all[keys, windows[s]])

    for j in range(PART // 256):
        score(0, j)
    for s in range(NX):
        index = s * HEADS + h
        of_max = (lax.rem(slot, 16) == index) & (slot < 48)
        of_total = (lax.rem(slot, 16) == index) & (slot >= 48) & (slot < 96)
        totals = []
        for n in range(NY):
            if s + 1 < NX and n < PART // 256:
                score(s + 1, n)
            own = slice(n * ROWS, (n + 1) * ROWS)
            part = scores[s % 2][own, :] + bias_all[n]
            top = jnp.max(part, axis=1, keepdims=True)
            part = jnp.exp2(part - top)
            total = jnp.sum(part, axis=1, keepdims=True)
            probs[own, :] = part.astype(BF16)
            totals.append(total)
            stats[n] = jnp.where(of_max, top, jnp.where(of_total, total, stats[n]))
        summed = dot(probs[...], value_all[:, windows[s]])
        for n in range(NY):
            own = slice(n * ROWS, (n + 1) * ROWS)
            scaled = summed[own] * (1.0 / totals[n])
            before = total_all[own, windows[s]]
            total_all[own, windows[s]] = jnp.where(mines[s][own], scaled, before)

    @pl.when(h == HEADS - 1)
    def _():
        third = lax.rem(slot // 16, 3)
        spread = spread_heads(48)
        for n in range(NY):
            own = slice(n * ROWS, (n + 1) * ROWS)
            whole = stats[n]
            if not merge:
                out[n][...] = total_all[own, :].astype(BF16)
                out_stats[n][...] = whole
                continue
            other = earlier_stats[n][...]
            top = jnp.maximum(whole, other)
            top_there = pltpu.roll(top, 48, 1)
            now = whole * jnp.exp2(jnp.minimum(pltpu.roll(whole, 48, 1) - top_there, 0.0))
            then = other * jnp.exp2(jnp.minimum(pltpu.roll(other, 48, 1) - top_there, 0.0))
            both = now + then
            used = (slot >= 48) & (slot < 64)
            share_now = jnp.where(used, now / both, 0.0)
            share_then = jnp.where(used, then / both, 0.0)
            merged = spread_rows(share_now, spread) * total_all[own, :]
            merged += spread_rows(share_then, spread) * earlier[n][...].astype(F32)
            out[n][:, 0:DIM] = merged.astype(BF16)
            whole = jnp.where(slot < 48, top, jnp.where(slot < 96, both, 0.0))
            high = whole.astype(BF16).astype(F32)
            rest = whole - high
            middle = rest.astype(BF16).astype(F32)
            low = rest - middle
            sent = jnp.where(third == 0, high, jnp.where(third == 1, middle, low))
            out[n][:, DIM : DIM + 128] = sent.astype(BF16)


def attention(pos, q, pairs, bias, earlier=None):
    once = pl.Buffered(1)

    def whole(dims):
        return pl.BlockSpec(dims, lambda h, n=len(dims): (0,) * n, pipeline_mode=once)

    merge = earlier is not None
    in_specs = [pl.BlockSpec(memory_space=pltpu.SMEM), whole((NY, ROWS, DIM))]
    in_specs += [whole((2 * ROWS, DIM))] * 4
    in_specs += [pl.BlockSpec((NY, 1, ROWS, KEYS), lambda h: (0, h, 0, 0))]
    args = [q, *pairs, bias]
    if merge:
        in_specs += [whole((ROWS, DIM))] * 4 + [whole((ROWS, 128))] * 4
        args += earlier
        outs = [sent_shape((ROWS, DIM + 128))] * 4
    else:
        outs = [shape((ROWS, DIM))] * 4 + [shape((ROWS, 128), F32)] * 4
    return pl.pallas_call(
        functools.partial(attention_body, merge),
        grid=(HEADS,),
        out_shape=outs,
        in_specs=in_specs,
        out_specs=[whole(o.shape) for o in outs],
        scratch_shapes=[
            pltpu.VMEM((NY * ROWS, DIM), BF16),
            pltpu.VMEM((PART, DIM), BF16),
            pltpu.VMEM((PART, DIM), BF16),
            pltpu.VMEM((8, PART), F32),
            pltpu.VMEM((NY, ROWS, PART), F32),
            pltpu.VMEM((NY, ROWS, 128), F32),
            pltpu.VMEM((NY * ROWS, PART), BF16),
            pltpu.VMEM((NY * ROWS, DIM), F32),
            pltpu.VMEM((NY * ROWS, PART), F32),
            pltpu.VMEM((NY * ROWS, PART), F32),
        ],
        compiler_params=pltpu.CompilerParams(
            dimension_semantics=("arbitrary",), vmem_limit_bytes=32 << 20
        ),
        name="attention_last" if merge else "attention_first",
    )(pos, *(pltpu.with_memory_space_constraint(a, pltpu.HBM) for a in args))


def combined(parts):
    tops, totals = [], []
    for o in parts:
        sent = o[:, DIM : DIM + 128].astype(F32)
        whole = sent + pltpu.roll(sent, 128 - 16, 1) + pltpu.roll(sent, 128 - 32, 1)
        tops.append(whole)
        totals.append(pltpu.roll(whole, 128 - 48, 1))
    used = lax.broadcasted_iota(jnp.int32, (ROWS, 128), 1) < NX * HEADS
    tops = [jnp.where(used, t, 0.0) for t in tops]
    totals = [jnp.where(used, t, 1.0) for t in totals]
    top = jnp.maximum(jnp.maximum(tops[0], tops[1]), jnp.maximum(tops[2], tops[3]))
    shares = [n * jnp.exp2(t - top) for t, n in zip(tops, totals)]
    inverse = 1.0 / (shares[0] + shares[1] + shares[2] + shares[3])
    spread = spread_heads(0)
    attended = None
    for o, share in zip(parts, shares):
        term = spread_rows(share * inverse, spread) * o[:, 0:DIM].astype(F32)
        attended = term if attended is None else attended + term
    return attended


def combine_body(*refs):
    gate, ffn, w_out, w_atom, act = refs[4:9]
    outs = refs[9:]
    attended = combined(refs[0:4])
    gated = (attended * sigmoid(gate[...].astype(F32))).astype(BF16)
    for r in range(NX):
        part = dot(gated[:, r * COLS : (r + 1) * COLS], w_out[...]) + ffn[r * ROWS : (r + 1) * ROWS]
        small = part.astype(BF16)
        rows = dot(small, w_atom[...])
        if r == 0:
            outs[0][...] = part + act[...].astype(F32)
            outs[4][...] = rows + dot(act[...], w_atom[...])
        else:
            outs[r][...] = small
            outs[4 + r][...] = rows.astype(BF16)


def atom_first_body(starts, maps, cond, tokens, offset, *outs):
    weights, project, scale, shift, select = outs
    for src in range(NX):
        project[src * COLS : (src + 1) * COLS, :] = maps[src, DIM : DIM + COLS, :]
        for i in range(7):
            line = DIM + COLS + i * 32
            weights[i, src * 32 : (src + 1) * 32, :] = maps[src, line : line + 32, :]
    normed = norm(cond[...].astype(F32)).astype(BF16)
    scale[...] = sigmoid(dot_nt(normed, weights[0]) + offset[0:1, :])
    shift[...] = dot_nt(normed, weights[1])
    row = lax.broadcasted_iota(jnp.int32, (128, CHUNK), 0)
    for i in range(CHUNKS):
        hit = ((row + starts[i]) == tokens[i : i + 1, :]).astype(F32)
        select[i * CHUNK : (i + 1) * CHUNK, :] = hit.T.astype(BF16)


def atom_body(pos, starts, bounds, near, far, before, own_skip, after, *refs):
    scale, shift, select, weights, offset, bias, spots, out = refs[0:8]
    table, skip, state, xs, qs, ks, vs, gs, at_all = refs[8:]
    skip[0:RIM, :] = before[0:RIM, :]
    skip[RIM : RIM + ATOMS, :] = own_skip[...]
    skip[RIM + ATOMS :, :] = after[0:RIM, :]
    y, z, c = pos[0], pos[1], pos[2]
    for ky in range(NY):
        for kz in range(NZ):
            place = lax.rem(y + NY - ky, NY) * (NZ * NC) + lax.rem(z + NZ - kz, NZ) * NC
            n = (kz * NY + ky) * ROWS
            own = pl.multiple_of((place + c) * ROWS, ROWS)
            other = pl.multiple_of((place + 1 - c) * ROWS, ROWS)
            table[pl.ds(own, ROWS), :] = near[n : n + ROWS, :]
            table[pl.ds(other, ROWS), :] = far[n : n + ROWS, :]
    for i in range(CHUNKS):
        rows = slice(i * CHUNK, (i + 1) * CHUNK)
        taken = table[pl.ds(pl.multiple_of(starts[i], 16), 128), :]
        now = skip[rows, :].astype(F32) + dot(select[rows, :], taken)
        state[rows, :] = now
        xs[rows, :] = (scale[rows, :] * norm(now) + shift[rows, :]).astype(BF16)
    x = xs[...]
    own = slice(RIM, RIM + ATOMS)
    mine = xs[own, :]
    qs[...] = (
        (dot_nt(mine, weights[2]) + offset[1:2, :]) * (LOG2E / math.sqrt(CA // HA))
    ).astype(BF16)
    ks[...] = dot_nt(x, weights[3]).astype(BF16)
    vs[...] = dot_nt(x, weights[4]).astype(BF16)
    gs[...] = sigmoid(dot_nt(mine, weights[5]).astype(BF16).astype(F32))
    width = CA // HA
    head_of_row = lax.broadcasted_iota(jnp.int32, (HA * WQ, CA), 0) // WQ
    head_of_lane = lax.broadcasted_iota(jnp.int32, (HA * WQ, CA), 1) // width
    same = head_of_row == head_of_lane
    lane_head = lax.broadcasted_iota(jnp.int32, (WQ, CA), 1) // width
    key_slot = lax.broadcasted_iota(jnp.int32, (HA * WQ, WK), 1)

    def window(b):
        rows = pl.ds(pl.multiple_of(b * WQ, WQ), WQ)
        span = pl.ds(pl.multiple_of(b * WQ, WQ), WK)
        one = qs[rows, :].astype(F32)
        four = jnp.where(same, jnp.concatenate([one] * HA, axis=0), 0.0).astype(BF16)
        extra = jnp.concatenate([bias[i, rows, :] for i in range(HA)], axis=0).astype(F32)
        scores = dot_nt(four, ks[span, :]) + extra * LOG2E
        base = pos[3] + b * WQ - RIM
        low = bounds[0, b] - base
        high = bounds[1, b] - base
        scores = jnp.where((key_slot >= low) & (key_slot < high), scores, FAR)
        probs = jnp.exp2(scores - jnp.max(scores, axis=1, keepdims=True))
        total = jnp.sum(probs, axis=1, keepdims=True)
        summed = dot(probs.astype(BF16), vs[span, :]) * (1.0 / total)
        picked = summed[0:WQ]
        for i in range(1, HA):
            picked = jnp.where(lane_head == i, summed[i * WQ : (i + 1) * WQ], picked)
        at_all[rows, :] = picked

    def windows(step, carry):
        for i in range(8):
            window(step * 8 + i)
        return carry

    lax.fori_loop(0, ATOMS // WQ // 8, windows, 0)
    gated = (at_all[...] * gs[...]).astype(BF16)
    new = state[own, :] + dot_nt(gated, weights[6])
    final = norm(new).astype(BF16)
    update = dot_nt(spots[...], final)
    for i in range(3):
        out[i] = update[i : i + 1, :]


def per_device(
    token_act,
    token_cond,
    pair_bias,
    token_mask,
    ada_weights,
    attention_in,
    attention_out,
    transition_in,
    transition_out,
    token_vectors,
    atom_skip,
    atom_cond,
    atom_bias,
    window_bounds,
    atom_token,
    atom_weights,
    token_to_atom,
    atom_vectors,
    position_out,
):
    f = lax.axis_index("fsdp").astype(jnp.int32)
    t = lax.axis_index("seq").astype(jnp.int32)
    y, z, c = t // (NZ * NC), (t // NC) % NZ, t % NC
    f_pos = f.reshape(1)
    act = token_act[0]

    block = pl.BlockSpec((ROWS, DIM), lambda i: (0, 0), pipeline_mode=pl.Buffered(1))
    wide = pl.BlockSpec((ROWS, DIM + COLS), lambda i: (0, 0), pipeline_mode=pl.Buffered(1))
    *sent, cut = pl.pallas_call(
        prepare_body,
        grid=(1,),
        out_shape=[sent_shape((ROWS, DIM + COLS))] * 4 + [shape((NY, HEADS, ROWS, KEYS))],
        in_specs=[
            pl.BlockSpec(memory_space=pltpu.SMEM),
            block,
            block,
            pl.BlockSpec(memory_space=pltpu.HBM),
        ],
        out_specs=[wide] * 4 + [pl.BlockSpec(memory_space=pltpu.HBM)],
        scratch_shapes=[pltpu.SemaphoreType.DMA((NY,))],
        compiler_params=pltpu.CompilerParams(dimension_semantics=("arbitrary",)),
        cost_estimate=pl.CostEstimate(flops=1 << 20, bytes_accessed=10 << 20, transcendentals=0),
        name="prepare",
    )(
        f_pos,
        pltpu.with_memory_space_constraint(act, pltpu.HBM),
        pltpu.with_memory_space_constraint(token_cond[0], pltpu.HBM),
        pair_bias,
    )
    normed = [sent[0]] + [x_shift(sent[k], k) for k in (1, 2, 3)]
    edge_skip, edge_cond, edge_token, _ = lax.optimization_barrier(
        (atom_skip[0], atom_cond, atom_token, sent[0])
    )

    turned = jnp.swapaxes(atom_weights, 1, 2).reshape(7 * 32, CA)
    own_maps = jnp.concatenate([token_to_atom, turned], axis=0)
    skip = atom_skip[0]
    coded = jnp.stack([edge_token // 64, edge_token % 64]).astype(BF16)

    def edge(lo, hi):
        codes = jnp.pad(coded[:, lo:hi], ((0, 14), (0, CA - RIM)))
        return jnp.concatenate([edge_skip[lo:hi], edge_cond[lo:hi], codes], axis=0)

    size = lax.axis_size("seq")
    up = [(i, i + 1) for i in range(size - 1)]
    before = lax.ppermute(edge(ATOMS - RIM, ATOMS), "seq", up)
    after = lax.ppermute(edge(0, RIM), "seq", [(j, i) for i, j in up])

    bias = y_exchange(cut)

    def decoded(side):
        pair = side[2 * RIM : 2 * RIM + 2, 0:RIM].astype(jnp.int32)
        return pair[0] * 64 + pair[1]

    cond_ext = jnp.concatenate([before[RIM : 2 * RIM], atom_cond, after[RIM : 2 * RIM]], axis=0)
    token_ext = jnp.concatenate([decoded(before), atom_token, decoded(after)])
    by_chunk = token_ext.reshape(CHUNKS, CHUNK)
    token_count = size * ROWS
    starts = jnp.minimum((by_chunk[:, 0] // 16) * 16, token_count - 128)

    offsets = lax.dynamic_slice_in_dim(token_vectors, f * COLS, COLS, 1)
    attend, message = kernel_call(
        adaptive_body,
        "adaptive",
        [sent_shape((ROWS, DIM)), shape((DIM + COLS + 7 * 32, CA))],
        (*normed, ada_weights, offsets[0:2], own_maps),
        free=7,
        flops=4 * 2 * 512 * 768 * 192,
        size=3 << 20,
    )
    attend_all = [attend] + [x_shift(attend, k) for k in (1, 2, 3)]
    q, kv, gate = kernel_call(
        project_body,
        "project",
        [sent_shape((ROWS, DIM)), sent_shape((2 * ROWS, DIM)), shape((ROWS, DIM))],
        free=7,
        args=(*attend_all, attention_in, offsets[2:3], token_mask.reshape(ROWS, 1)),
        scalars=(f_pos,),
        flops=4 * 2 * 512 * 768 * 192,
        size=4 << 20,
    )
    near = [kv] + [z_swap(kv, k) for k in (1, 2, 3)]
    across = c_shift(kv)
    q, _ = lax.optimization_barrier((q, across))
    q_all = y_collect(q)
    q_all, near_1 = lax.optimization_barrier((q_all, near[1]))
    early = [kv, near_1, across, c_shift(near_1)]

    message, _ = lax.optimization_barrier((message, q))
    messages = lax.all_gather(message, "fsdp", axis=0)
    ffn = kernel_call(
        hidden_body,
        "hidden",
        shape((NX * ROWS, DIM), F32),
        (transition_in, transition_out, messages),
        (f_pos,),
        free=2,
        flops=3 * 2 * 512 * 768 * 384,
        size=6 << 20,
    )
    atom_maps, project_full, scale, shift, select = kernel_call(
        atom_first_body,
        "atom_first",
        [
            shape((7, CA, CA)),
            shape((DIM, CA)),
            shape((EXT, CA), F32),
            shape((EXT, CA), F32),
            shape((EXT, 128)),
        ],
        (messages, cond_ext, by_chunk, atom_vectors),
        (starts,),
        flops=4 * EXT * CA * CA,
        size=3 << 20,
    )

    def places(n):
        at = [(z ^ n) * NC + c, (z ^ (n + 1)) * NC + c]
        return jnp.stack([y, *at, at[0] ^ 1, at[1] ^ 1])

    first = attention(places(0), q_all, early, bias)
    _, near_2, near_3 = lax.optimization_barrier((first[0], near[2], near[3]))
    late = [near_2, near_3, c_shift(near_2), c_shift(near_3)]
    out = attention(places(2), q_all, late, bias, first)
    parts = [out[0]] + [y_shift(out[k], NY - k) for k in (1, 2, 3)]
    sums = kernel_call(
        combine_body,
        "combine",
        [shape((ROWS, DIM), F32)]
        + [sent_shape((ROWS, DIM))] * 3
        + [sent_shape((ROWS, CA), F32)]
        + [sent_shape((ROWS, CA))] * 3,
        (*parts, gate, ffn, attention_out, project_full, act),
        free=4,
        flops=4 * 2 * 128 * 768 * (192 + 128) + 8 * 2 * 128 * 128 * 768,
        size=5 << 20,
    )
    arrived = [x_shift(sums[4 + k], NX - k) for k in (1, 2, 3)]
    rows = (
        sums[4] + arrived[0].astype(F32) + arrived[1].astype(F32) + arrived[2].astype(F32)
    ).astype(BF16)

    turns = [y_shift(rows, k) for k in (1, 2, 3)]
    by_y = jnp.concatenate([rows] + turns, axis=0)
    _, *partial = lax.optimization_barrier((by_y, *sums[1:4]))
    main = [x_shift(partial[k - 1], NX - k) for k in (1, 2, 3)]
    turns = [z_shift(by_y, k) for k in (1, 2, 3)]
    turns, main = lax.optimization_barrier((turns, main))
    by_z = jnp.concatenate([by_y] + turns, axis=0)
    token_result = (
        sums[0] + main[0].astype(F32) + main[1].astype(F32) + main[2].astype(F32)
    ).astype(BF16)
    by_c = c_shift(by_z)
    by_c, token_result = lax.optimization_barrier((by_c, token_result))

    scalars = (jnp.stack([y, z, c, t * ATOMS]), starts, window_bounds.T)
    update = kernel_call(
        atom_body,
        "atoms",
        shape((3, 1, ATOMS), F32),
        (
            by_z,
            by_c,
            before,
            skip,
            after,
            scale,
            shift,
            select,
            atom_maps,
            atom_vectors,
            atom_bias,
            position_out,
        ),
        scalars,
        free=2,
        scratch=[
            pltpu.VMEM((token_count, CA), BF16),
            pltpu.VMEM((EXT, CA), BF16),
            pltpu.VMEM((EXT, CA), F32),
            pltpu.VMEM((EXT, CA), BF16),
            pltpu.VMEM((ATOMS, CA), BF16),
            pltpu.VMEM((EXT, CA), BF16),
            pltpu.VMEM((EXT, CA), BF16),
            pltpu.VMEM((ATOMS, CA), F32),
            pltpu.VMEM((ATOMS, CA), F32),
        ],
        flops=2 * 1120 * 128 * 128 * 10,
        size=6 << 20,
    )
    return (token_result[None], jnp.swapaxes(update, 0, 1))


def solution(mesh):
    in_specs = (
        P(("sample", "fsdp"), "seq", None),
        P(("sample", "fsdp"), "seq", None),
        P("fsdp", "seq", None),
        P("seq"),
        P(None, None, "fsdp"),
        P(None, None, "fsdp"),
        P("fsdp", None),
        P(None, None, "fsdp"),
        P("fsdp", None),
        P(),
        P(("sample", "fsdp"), "seq", None),
        P("seq", None),
        P(None, "seq", None),
        P("seq", None),
        P("seq"),
        P(None, None, "fsdp"),
        P("fsdp", None),
        P(),
        P(),
    )
    out_specs = (P(("sample", "fsdp"), "seq", None), P(("sample", "fsdp"), None, "seq"))
    return jax.shard_map(
        per_device, mesh=mesh, in_specs=in_specs, out_specs=out_specs, check_vma=False
    )
```

```python
import functools
import math

import jax
import jax.numpy as jnp
from jax import lax
from jax.experimental import pallas as pl
from jax.experimental.pallas import tpu as pltpu
from jax.sharding import PartitionSpec as P

EPS = 1e-05
FAR = -1e30
SENT = 1e30
LOG2E = 1.4426950408889634
HD = 48
HA = 4
WQ = 32
WK = 128
RIM = 48
NX = 4
NY = 4
NZ = 4
NC = 2
ROWS = 128
DIM = 768
COLS = 192
HEADS = 4
ATOMS = 1024
EXT = ATOMS + 2 * RIM
CHUNK = 112
CHUNKS = EXT // CHUNK
CA = 128
F32 = jnp.float32
BF16 = jnp.bfloat16


def x_shift(a, k):
    return lax.ppermute(a, "fsdp", [(i, (i + k) % NX) for i in range(NX)])


def y_shift(a, k):
    group = NZ * NC
    pairs = [(t, ((t // group + k) % NY) * group + t % group) for t in range(NY * group)]
    return lax.ppermute(a, "seq", pairs)


def z_shift(a, k):
    group = NZ * NC
    pairs = [
        (t, (t // group) * group + ((t // NC + k) % NZ) * NC + t % NC) for t in range(NY * group)
    ]
    return lax.ppermute(a, "seq", pairs)


def z_swap(a, k):
    return lax.ppermute(a, "seq", [(t, t ^ (NC * k)) for t in range(NY * NZ * NC)])


def y_exchange(a):
    group = NZ * NC
    groups = [[y * group + n for y in range(NY)] for n in range(group)]
    return lax.all_to_all(
        a, "seq", split_axis=0, concat_axis=0, axis_index_groups=groups, tiled=True
    )


def y_collect(a):
    group = NZ * NC
    groups = [[y * group + n for y in range(NY)] for n in range(group)]
    return lax.all_gather(a, "seq", axis=0, axis_index_groups=groups)


def c_shift(a):
    return lax.ppermute(a, "seq", [(t, t ^ 1) for t in range(NY * NZ * NC)])


def norm(values):
    center = values - jnp.mean(values, axis=-1, keepdims=True)
    spread = jnp.mean(center * center, axis=-1, keepdims=True)
    return center * lax.rsqrt(spread + EPS)


def sigmoid(v):
    return 1.0 / (1.0 + jnp.exp(-v))


def dot(a, b):
    return jnp.dot(a, b, preferred_element_type=F32)


def dot_nt(a, b):
    return lax.dot_general(a, b, (((1,), (1,)), ((), ())), preferred_element_type=F32)


def kernel_call(body, name, out_shape, args, scalars=(), scratch=(), flops=0, size=0, free=0, late=0):
    def whole(a):
        return pl.BlockSpec(
            a.shape, lambda i, n=len(a.shape): (0,) * n, pipeline_mode=pl.Buffered(1)
        )

    args = [
        a if i < free else pltpu.with_memory_space_constraint(a, pltpu.HBM)
        for i, a in enumerate(args)
    ]
    return pl.pallas_call(
        body,
        grid=(1,),
        out_shape=out_shape,
        in_specs=[pl.BlockSpec(memory_space=pltpu.SMEM)] * len(scalars)
        + [whole(a) for a in args[: len(args) - late]]
        + [pl.BlockSpec(memory_space=pltpu.HBM)] * late,
        out_specs=jax.tree.map(whole, out_shape),
        scratch_shapes=list(scratch),
        compiler_params=pltpu.CompilerParams(
            dimension_semantics=("arbitrary",), vmem_limit_bytes=24 << 20
        ),
        cost_estimate=pl.CostEstimate(flops=flops, bytes_accessed=size, transcendentals=0),
        name=name,
    )(*scalars, *args)


def shape(dims, kind=BF16):
    return pltpu.HBM(dims, kind)


def sent_shape(dims, kind=BF16):
    return jax.ShapeDtypeStruct(dims, kind)


def prepare_body(pos, act, cond, bias, *refs):
    outs, cut = refs[0:4], refs[4]
    cut[0] = bias[...]

    @pl.when(pl.program_id(0) == 0)
    def _():
        f = pos[0]
        normed = norm(cond[...].astype(F32)).astype(BF16)
        hat = norm(act[...].astype(F32))
        for k in range(NX):
            dest = lax.rem(f + k, NX)
            part = hat[:, 0:COLS]
            for j in range(1, NX):
                part = jnp.where(dest == j, hat[:, j * COLS : (j + 1) * COLS], part)
            outs[k][:, 0:DIM] = normed
            outs[k][:, DIM : DIM + COLS] = part.astype(BF16)


def adaptive_body(m0, m1, m2, m3, ada, offset, maps, attend, message):
    parts = (m0, m1, m2, m3)
    normed = jnp.concatenate([m[:, 0:DIM] for m in parts], axis=0)
    hat = jnp.concatenate([m[:, DIM : DIM + COLS] for m in parts], axis=0).astype(F32)
    message[DIM:, :] = maps[...]
    for n in range(2):
        scale = sigmoid(dot(normed, ada[2 * n]) + offset[n : n + 1, :])
        result = (scale * hat + dot(normed, ada[2 * n + 1])).astype(BF16)
        wide = jnp.concatenate([result[k * ROWS : (k + 1) * ROWS] for k in range(NX)], axis=1)
        if n == 0:
            attend[...] = wide
        else:
            for i in range(DIM // 128):
                message[i * ROWS : (i + 1) * ROWS, :] = wide[:, i * 128 : (i + 1) * 128]


def gathered_rows(part, j):
    return jnp.concatenate(
        [part[:, ((r - j) % NX) * COLS : ((r - j) % NX + 1) * COLS] for r in range(NX)],
        axis=0,
    )


def project_body(pos, a0, a1, a2, a3, weights, offset, mask, q, kv, g):
    f = pos[0]
    parts = (a0, a1, a2, a3)
    sums = [None] * 4
    for j in range(NX):
        rows = gathered_rows(parts[j][...], j)
        at = pl.multiple_of(lax.rem(f + NX - j, NX) * COLS, COLS)
        for n in range(4):
            term = dot(rows, weights[n, pl.ds(at, COLS), :])
            sums[n] = term if j == 0 else sums[n] + term
    live = mask[...] > 0
    for r in range(NX):
        own = slice(r * ROWS, (r + 1) * ROWS)
        to = slice(r * COLS, (r + 1) * COLS)
        q[:, to] = ((sums[0][own] + offset[0:1, :]) * (LOG2E / math.sqrt(HD))).astype(BF16)
        kv[0:ROWS, to] = jnp.where(live, sums[1][own], SENT).astype(BF16)
        kv[ROWS:, to] = sums[2][own].astype(BF16)
        g[:, to] = sums[3][own].astype(BF16)


def hidden_body(pos, w_in, w_out, parts, out):
    f = pos[0]
    gate, up = None, None
    for j in range(NX):
        src = lax.rem(f + NX - j, NX)
        wide = jnp.concatenate(
            [parts[src, i * ROWS : (i + 1) * ROWS, :] for i in range(DIM // 128)], axis=1
        )
        rows = gathered_rows(wide, j)
        at = pl.multiple_of(src * COLS, COLS)
        gate_term = dot(rows, w_in[0, pl.ds(at, COLS), :])
        up_term = dot(rows, w_in[1, pl.ds(at, COLS), :])
        gate = gate_term if j == 0 else gate + gate_term
        up = up_term if j == 0 else up + up_term
    hidden = (gate / (1.0 + jnp.exp(-gate)) * up).astype(BF16)
    out[...] = dot(hidden, w_out[...])


KEYS = NZ * NC * ROWS
PART = KEYS // 2


def spread_heads(first):
    head = (lax.broadcasted_iota(jnp.int32, (128, DIM), 0) - first) * HD
    lane = lax.broadcasted_iota(jnp.int32, (128, DIM), 1)
    return ((lane >= head) & (lane < head + HD)).astype(F32).astype(BF16)


def spread_rows(share, spread):
    high = share.astype(BF16)
    low = (share - high.astype(F32)).astype(BF16)
    return dot(high, spread) + dot(low, spread)


def attention_body(merge, pos, q, *refs):
    pairs = refs[0:4]
    bias = refs[4]
    refs = refs[5:]
    if merge:
        earlier, earlier_stats, refs = refs[0:4], refs[4:8], refs[8:]
        out, refs = refs[0:4], refs[4:]
    else:
        out, out_stats, refs = refs[0:4], refs[4:8], refs[8:]
    q_all, key_all, value_all, far_row, bias_all, stats, probs, total_all = refs[0:8]
    scores = refs[8:10]
    h = pl.program_id(0)
    y = pos[0]

    @pl.when(h == 0)
    def _():
        unit = (lax.broadcasted_iota(jnp.int32, (8, 128), 1) == 0).astype(F32).astype(BF16)
        for i in range(4):
            at = slice(i * ROWS, (i + 1) * ROWS)
            block = pairs[i][0:ROWS, :]
            first = dot_nt(unit, block[:, 0:128])
            far_row[:, at] = jnp.where(first > 1e20, FAR, 0.0)
            wide = block.astype(F32)
            key_all[at, :] = jnp.where(wide[:, 0:1] > 1e20, 0.0, wide).astype(BF16)
            value_all[at, :] = pairs[i][ROWS:, :]
        for n in range(NY):
            q_all[n * ROWS : (n + 1) * ROWS, :] = q[lax.rem(y + NY - n, NY)]
        stats[...] = jnp.zeros_like(stats)

    for n in range(NY):
        src = lax.rem(y + NY - n, NY)
        for i in range(4):
            at = slice(i * ROWS, (i + 1) * ROWS)
            part = bias[src, 0, :, pl.ds(pl.multiple_of(pos[1 + i] * ROWS, ROWS), ROWS)]
            bias_all[n, :, at] = part.astype(F32) * LOG2E + far_row[0:1, at]

    lane = lax.broadcasted_iota(jnp.int32, (NY * ROWS, 256), 1)
    slot = lax.broadcasted_iota(jnp.int32, (ROWS, 128), 1)
    windows, mines, rows = [], [], []
    for s in range(NX):
        lane0 = COLS * s + HD * h
        start = jnp.minimum(lane0 // 128, (DIM - 256) // 128)
        off = lane0 - start * 128
        window = pl.ds(pl.multiple_of(start * 128, 128), 256)
        mine = (lane >= off) & (lane < off + HD)
        windows.append(window)
        mines.append(mine)
        rows.append(jnp.where(mine, q_all[:, window].astype(F32), 0.0).astype(BF16))

    def score(s, j):
        keys = slice(j * 256, (j + 1) * 256)
        scores[s % 2][:, keys] = dot_nt(rows[s], key_all[keys, windows[s]])

    for j in range(PART // 256):
        score(0, j)
    for s in range(NX):
        index = s * HEADS + h
        of_max = (lax.rem(slot, 16) == index) & (slot < 48)
        of_total = (lax.rem(slot, 16) == index) & (slot >= 48) & (slot < 96)
        totals = []
        for n in range(NY):
            if s + 1 < NX and n < PART // 256:
                score(s + 1, n)
            own = slice(n * ROWS, (n + 1) * ROWS)
            part = scores[s % 2][own, :] + bias_all[n]
            top = jnp.max(part, axis=1, keepdims=True)
            part = jnp.exp2(part - top)
            total = jnp.sum(part, axis=1, keepdims=True)
            probs[own, :] = part.astype(BF16)
            totals.append(total)
            stats[n] = jnp.where(of_max, top, jnp.where(of_total, total, stats[n]))
        summed = dot(probs[...], value_all[:, windows[s]])
        for n in range(NY):
            own = slice(n * ROWS, (n + 1) * ROWS)
            scaled = summed[own] * (1.0 / totals[n])
            before = total_all[own, windows[s]]
            total_all[own, windows[s]] = jnp.where(mines[s][own], scaled, before)

    @pl.when(h == HEADS - 1)
    def _():
        third = lax.rem(slot // 16, 3)
        spread = spread_heads(48)
        for n in range(NY):
            own = slice(n * ROWS, (n + 1) * ROWS)
            whole = stats[n]
            if not merge:
                out[n][...] = total_all[own, :].astype(BF16)
                out_stats[n][...] = whole
                continue
            other = earlier_stats[n][...]
            top = jnp.maximum(whole, other)
            top_there = pltpu.roll(top, 48, 1)
            now = whole * jnp.exp2(jnp.minimum(pltpu.roll(whole, 48, 1) - top_there, 0.0))
            then = other * jnp.exp2(jnp.minimum(pltpu.roll(other, 48, 1) - top_there, 0.0))
            both = now + then
            used = (slot >= 48) & (slot < 64)
            share_now = jnp.where(used, now / both, 0.0)
            share_then = jnp.where(used, then / both, 0.0)
            merged = spread_rows(share_now, spread) * total_all[own, :]
            merged += spread_rows(share_then, spread) * earlier[n][...].astype(F32)
            out[n][:, 0:DIM] = merged.astype(BF16)
            whole = jnp.where(slot < 48, top, jnp.where(slot < 96, both, 0.0))
            high = whole.astype(BF16).astype(F32)
            rest = whole - high
            middle = rest.astype(BF16).astype(F32)
            low = rest - middle
            sent = jnp.where(third == 0, high, jnp.where(third == 1, middle, low))
            out[n][:, DIM : DIM + 128] = sent.astype(BF16)


def attention(pos, q, pairs, bias, earlier=None):
    once = pl.Buffered(1)

    def whole(dims):
        return pl.BlockSpec(dims, lambda h, n=len(dims): (0,) * n, pipeline_mode=once)

    merge = earlier is not None
    in_specs = [pl.BlockSpec(memory_space=pltpu.SMEM), whole((NY, ROWS, DIM))]
    in_specs += [whole((2 * ROWS, DIM))] * 4
    in_specs += [pl.BlockSpec((NY, 1, ROWS, KEYS), lambda h: (0, h, 0, 0))]
    args = [q, *pairs, bias]
    if merge:
        in_specs += [whole((ROWS, DIM))] * 4 + [whole((ROWS, 128))] * 4
        args += earlier
        outs = [sent_shape((ROWS, DIM + 128))] * 4
    else:
        outs = [shape((ROWS, DIM))] * 4 + [shape((ROWS, 128), F32)] * 4
    return pl.pallas_call(
        functools.partial(attention_body, merge),
        grid=(HEADS,),
        out_shape=outs,
        in_specs=in_specs,
        out_specs=[whole(o.shape) for o in outs],
        scratch_shapes=[
            pltpu.VMEM((NY * ROWS, DIM), BF16),
            pltpu.VMEM((PART, DIM), BF16),
            pltpu.VMEM((PART, DIM), BF16),
            pltpu.VMEM((8, PART), F32),
            pltpu.VMEM((NY, ROWS, PART), F32),
            pltpu.VMEM((NY, ROWS, 128), F32),
            pltpu.VMEM((NY * ROWS, PART), BF16),
            pltpu.VMEM((NY * ROWS, DIM), F32),
            pltpu.VMEM((NY * ROWS, PART), F32),
            pltpu.VMEM((NY * ROWS, PART), F32),
        ],
        compiler_params=pltpu.CompilerParams(
            dimension_semantics=("arbitrary",), vmem_limit_bytes=32 << 20
        ),
        name="attention_last" if merge else "attention_first",
    )(pos, *(pltpu.with_memory_space_constraint(a, pltpu.HBM) for a in args))


def combined(parts):
    tops, totals = [], []
    for o in parts:
        sent = o[:, DIM : DIM + 128].astype(F32)
        whole = sent + pltpu.roll(sent, 128 - 16, 1) + pltpu.roll(sent, 128 - 32, 1)
        tops.append(whole)
        totals.append(pltpu.roll(whole, 128 - 48, 1))
    used = lax.broadcasted_iota(jnp.int32, (ROWS, 128), 1) < NX * HEADS
    tops = [jnp.where(used, t, 0.0) for t in tops]
    totals = [jnp.where(used, t, 1.0) for t in totals]
    top = jnp.maximum(jnp.maximum(tops[0], tops[1]), jnp.maximum(tops[2], tops[3]))
    shares = [n * jnp.exp2(t - top) for t, n in zip(tops, totals)]
    inverse = 1.0 / (shares[0] + shares[1] + shares[2] + shares[3])
    spread = spread_heads(0)
    attended = None
    for o, share in zip(parts, shares):
        term = spread_rows(share * inverse, spread) * o[:, 0:DIM].astype(F32)
        attended = term if attended is None else attended + term
    return attended


def combine_body(*refs):
    gate, ffn, w_out, w_atom, act = refs[4:9]
    outs = refs[9:]
    attended = combined(refs[0:4])
    gated = (attended * sigmoid(gate[...].astype(F32))).astype(BF16)
    for r in range(NX):
        part = dot(gated[:, r * COLS : (r + 1) * COLS], w_out[...]) + ffn[r * ROWS : (r + 1) * ROWS]
        small = part.astype(BF16)
        rows = dot(small, w_atom[...])
        if r == 0:
            outs[0][...] = part + act[...].astype(F32)
            outs[4][...] = rows + dot(act[...], w_atom[...])
        else:
            outs[r][...] = small
            outs[4 + r][...] = rows.astype(BF16)


def atom_first_body(starts, maps, cond, tokens, offset, *outs):
    weights, project, scale, shift, select = outs
    for src in range(NX):
        project[src * COLS : (src + 1) * COLS, :] = maps[src, DIM : DIM + COLS, :]
        for i in range(7):
            line = DIM + COLS + i * 32
            weights[i, src * 32 : (src + 1) * 32, :] = maps[src, line : line + 32, :]
    normed = norm(cond[...].astype(F32)).astype(BF16)
    scale[...] = sigmoid(dot_nt(normed, weights[0]) + offset[0:1, :])
    shift[...] = dot_nt(normed, weights[1])
    row = lax.broadcasted_iota(jnp.int32, (128, CHUNK), 0)
    for i in range(CHUNKS):
        hit = ((row + starts[i]) == tokens[i : i + 1, :]).astype(F32)
        select[i * CHUNK : (i + 1) * CHUNK, :] = hit.T.astype(BF16)


def atom_body(pos, starts, bounds, near, far, before, own_skip, after, offset, spots, *refs):
    out = refs[5]
    table, skip, state, xs, qs, ks, vs, gs, at_all = refs[6:15]
    select, scale, shift, weights, bias = refs[15:20]
    sems = refs[20]
    copies = []
    for i, there in enumerate(refs[0:5]):
        copies.append(pltpu.make_async_copy(there, refs[15 + i], sems.at[i]))
        copies[i].start()
    skip[0:RIM, :] = before[0:RIM, :]
    skip[RIM : RIM + ATOMS, :] = own_skip[...]
    skip[RIM + ATOMS :, :] = after[0:RIM, :]
    y, z, c = pos[0], pos[1], pos[2]
    for ky in range(NY):
        for kz in range(NZ):
            place = lax.rem(y + NY - ky, NY) * (NZ * NC) + lax.rem(z + NZ - kz, NZ) * NC
            n = (kz * NY + ky) * ROWS
            own = pl.multiple_of((place + c) * ROWS, ROWS)
            other = pl.multiple_of((place + 1 - c) * ROWS, ROWS)
            table[pl.ds(own, ROWS), :] = near[n : n + ROWS, :]
            table[pl.ds(other, ROWS), :] = far[n : n + ROWS, :]
    for i in range(3):
        copies[i].wait()
    for i in range(CHUNKS):
        rows = slice(i * CHUNK, (i + 1) * CHUNK)
        taken = table[pl.ds(pl.multiple_of(starts[i], 16), 128), :]
        now = skip[rows, :].astype(F32) + dot(select[rows, :], taken)
        state[rows, :] = now
        xs[rows, :] = (scale[rows, :] * norm(now) + shift[rows, :]).astype(BF16)
    copies[3].wait()
    x = xs[...]
    own = slice(RIM, RIM + ATOMS)
    mine = xs[own, :]
    qs[...] = (
        (dot_nt(mine, weights[2]) + offset[1:2, :]) * (LOG2E / math.sqrt(CA // HA))
    ).astype(BF16)
    ks[...] = dot_nt(x, weights[3]).astype(BF16)
    vs[...] = dot_nt(x, weights[4]).astype(BF16)
    gs[...] = sigmoid(dot_nt(mine, weights[5]).astype(BF16).astype(F32))
    width = CA // HA
    head_of_row = lax.broadcasted_iota(jnp.int32, (HA * WQ, CA), 0) // WQ
    head_of_lane = lax.broadcasted_iota(jnp.int32, (HA * WQ, CA), 1) // width
    same = head_of_row == head_of_lane
    lane_head = lax.broadcasted_iota(jnp.int32, (WQ, CA), 1) // width
    key_slot = lax.broadcasted_iota(jnp.int32, (HA * WQ, WK), 1)

    def window(b):
        rows = pl.ds(pl.multiple_of(b * WQ, WQ), WQ)
        span = pl.ds(pl.multiple_of(b * WQ, WQ), WK)
        one = qs[rows, :].astype(F32)
        four = jnp.where(same, jnp.concatenate([one] * HA, axis=0), 0.0).astype(BF16)
        extra = jnp.concatenate([bias[i, rows, :] for i in range(HA)], axis=0).astype(F32)
        scores = dot_nt(four, ks[span, :]) + extra * LOG2E
        base = pos[3] + b * WQ - RIM
        low = bounds[0, b] - base
        high = bounds[1, b] - base
        scores = jnp.where((key_slot >= low) & (key_slot < high), scores, FAR)
        probs = jnp.exp2(scores - jnp.max(scores, axis=1, keepdims=True))
        total = jnp.sum(probs, axis=1, keepdims=True)
        summed = dot(probs.astype(BF16), vs[span, :]) * (1.0 / total)
        picked = summed[0:WQ]
        for i in range(1, HA):
            picked = jnp.where(lane_head == i, summed[i * WQ : (i + 1) * WQ], picked)
        at_all[rows, :] = picked

    copies[4].wait()

    def windows(step, carry):
        for i in range(8):
            window(step * 8 + i)
        return carry

    lax.fori_loop(0, ATOMS // WQ // 8, windows, 0)
    gated = (at_all[...] * gs[...]).astype(BF16)
    new = state[own, :] + dot_nt(gated, weights[6])
    final = norm(new).astype(BF16)
    update = dot_nt(spots[...], final)
    for i in range(3):
        out[i] = update[i : i + 1, :]


def per_device(
    token_act,
    token_cond,
    pair_bias,
    token_mask,
    ada_weights,
    attention_in,
    attention_out,
    transition_in,
    transition_out,
    token_vectors,
    atom_skip,
    atom_cond,
    atom_bias,
    window_bounds,
    atom_token,
    atom_weights,
    token_to_atom,
    atom_vectors,
    position_out,
):
    f = lax.axis_index("fsdp").astype(jnp.int32)
    t = lax.axis_index("seq").astype(jnp.int32)
    y, z, c = t // (NZ * NC), (t // NC) % NZ, t % NC
    f_pos = f.reshape(1)
    act = token_act[0]

    block = pl.BlockSpec((ROWS, DIM), lambda i: (0, 0), pipeline_mode=pl.Buffered(1))
    wide = pl.BlockSpec((ROWS, DIM + COLS), lambda i: (0, 0), pipeline_mode=pl.Buffered(1))
    *sent, cut = pl.pallas_call(
        prepare_body,
        grid=(NY,),
        out_shape=[sent_shape((ROWS, DIM + COLS))] * 4 + [shape((NY, HEADS, ROWS, KEYS))],
        in_specs=[
            pl.BlockSpec(memory_space=pltpu.SMEM),
            block,
            block,
            pl.BlockSpec((HEADS, ROWS, KEYS), lambda i: (0, 0, i)),
        ],
        out_specs=[wide] * 4 + [pl.BlockSpec((1, HEADS, ROWS, KEYS), lambda i: (i, 0, 0, 0))],
        compiler_params=pltpu.CompilerParams(
            dimension_semantics=("arbitrary",), vmem_limit_bytes=24 << 20
        ),
        name="prepare",
    )(
        f_pos,
        pltpu.with_memory_space_constraint(act, pltpu.HBM),
        pltpu.with_memory_space_constraint(token_cond[0], pltpu.HBM),
        pltpu.with_memory_space_constraint(pair_bias, pltpu.HBM),
    )
    normed = [sent[0]] + [x_shift(sent[k], k) for k in (1, 2, 3)]
    edge_skip, edge_cond, edge_token, _ = lax.optimization_barrier(
        (atom_skip[0], atom_cond, atom_token, sent[0])
    )

    turned = jnp.swapaxes(atom_weights, 1, 2).reshape(7 * 32, CA)
    own_maps = jnp.concatenate([token_to_atom, turned], axis=0)
    skip = atom_skip[0]
    coded = jnp.stack([edge_token // 64, edge_token % 64]).astype(BF16)

    def edge(lo, hi):
        codes = jnp.pad(coded[:, lo:hi], ((0, 14), (0, CA - RIM)))
        return jnp.concatenate([edge_skip[lo:hi], edge_cond[lo:hi], codes], axis=0)

    size = lax.axis_size("seq")
    up = [(i, i + 1) for i in range(size - 1)]
    before = lax.ppermute(edge(ATOMS - RIM, ATOMS), "seq", up)
    after = lax.ppermute(edge(0, RIM), "seq", [(j, i) for i, j in up])

    bias = y_exchange(cut)

    def decoded(side):
        pair = side[2 * RIM : 2 * RIM + 2, 0:RIM].astype(jnp.int32)
        return pair[0] * 64 + pair[1]

    cond_ext = jnp.concatenate([before[RIM : 2 * RIM], atom_cond, after[RIM : 2 * RIM]], axis=0)
    token_ext = jnp.concatenate([decoded(before), atom_token, decoded(after)])
    by_chunk = token_ext.reshape(CHUNKS, CHUNK)
    token_count = size * ROWS
    starts = jnp.minimum((by_chunk[:, 0] // 16) * 16, token_count - 128)

    offsets = lax.dynamic_slice_in_dim(token_vectors, f * COLS, COLS, 1)
    attend, message = kernel_call(
        adaptive_body,
        "adaptive",
        [sent_shape((ROWS, DIM)), shape((DIM + COLS + 7 * 32, CA))],
        (*normed, ada_weights, offsets[0:2], own_maps),
        free=7,
        flops=4 * 2 * 512 * 768 * 192,
        size=3 << 20,
    )
    attend_all = [attend] + [x_shift(attend, k) for k in (1, 2, 3)]
    attend_all[3], before, after = lax.optimization_barrier((attend_all[3], before, after))
    q, kv, gate = kernel_call(
        project_body,
        "project",
        [sent_shape((ROWS, DIM)), sent_shape((2 * ROWS, DIM)), shape((ROWS, DIM))],
        free=7,
        args=(*attend_all, attention_in, offsets[2:3], token_mask.reshape(ROWS, 1)),
        scalars=(f_pos,),
        flops=4 * 2 * 512 * 768 * 192,
        size=4 << 20,
    )
    near = [kv] + [z_swap(kv, k) for k in (1, 2, 3)]
    across = c_shift(kv)
    q_all = y_collect(q)
    q_all, near_1 = lax.optimization_barrier((q_all, near[1]))
    early = [kv, near_1, across, c_shift(near_1)]

    message, _ = lax.optimization_barrier((message, q))
    messages = lax.all_gather(message, "fsdp", axis=0)
    ffn = kernel_call(
        hidden_body,
        "hidden",
        shape((NX * ROWS, DIM), F32),
        (transition_in, transition_out, messages),
        (f_pos,),
        free=2,
        flops=3 * 2 * 512 * 768 * 384,
        size=6 << 20,
    )
    atom_maps, project_full, scale, shift, select = kernel_call(
        atom_first_body,
        "atom_first",
        [
            shape((7, CA, CA)),
            shape((DIM, CA)),
            shape((EXT, CA), F32),
            shape((EXT, CA), F32),
            shape((EXT, 128)),
        ],
        (messages, cond_ext, by_chunk, atom_vectors),
        (starts,),
        flops=4 * EXT * CA * CA,
        size=3 << 20,
    )

    def places(n):
        at = [(z ^ n) * NC + c, (z ^ (n + 1)) * NC + c]
        return jnp.stack([y, *at, at[0] ^ 1, at[1] ^ 1])

    first = attention(places(0), q_all, early, bias)
    _, near_2, near_3 = lax.optimization_barrier((first[0], near[2], near[3]))
    late = [near_2, near_3, c_shift(near_2), c_shift(near_3)]
    out = attention(places(2), q_all, late, bias, first)
    parts = [out[0]] + [y_shift(out[k], NY - k) for k in (1, 2, 3)]
    sums = kernel_call(
        combine_body,
        "combine",
        [shape((ROWS, DIM), F32)]
        + [sent_shape((ROWS, DIM))] * 3
        + [sent_shape((ROWS, CA), F32)]
        + [sent_shape((ROWS, CA))] * 3,
        (*parts, gate, ffn, attention_out, project_full, act),
        free=4,
        flops=4 * 2 * 128 * 768 * (192 + 128) + 8 * 2 * 128 * 128 * 768,
        size=5 << 20,
    )
    arrived = [x_shift(sums[4 + k], NX - k) for k in (1, 2, 3)]
    rows = (
        sums[4] + arrived[0].astype(F32) + arrived[1].astype(F32) + arrived[2].astype(F32)
    ).astype(BF16)

    turns = [y_shift(rows, k) for k in (1, 2, 3)]
    by_y = jnp.concatenate([rows] + turns, axis=0)
    turns = [z_shift(by_y, k) for k in (1, 2, 3)]
    by_z = jnp.concatenate([by_y] + turns, axis=0)
    by_c = c_shift(by_z)
    _, *partial = lax.optimization_barrier((by_z, *sums[1:4]))
    main = [x_shift(partial[k - 1], NX - k) for k in (1, 2, 3)]

    scalars = (jnp.stack([y, z, c, t * ATOMS]), starts, window_bounds.T)
    update = kernel_call(
        atom_body,
        "atoms",
        shape((3, 1, ATOMS), F32),
        (
            by_z,
            by_c,
            before,
            skip,
            after,
            atom_vectors,
            position_out,
            select,
            scale,
            shift,
            atom_maps,
            atom_bias,
        ),
        scalars,
        free=2,
        scratch=[
            pltpu.VMEM((token_count, CA), BF16),
            pltpu.VMEM((EXT, CA), BF16),
            pltpu.VMEM((EXT, CA), F32),
            pltpu.VMEM((EXT, CA), BF16),
            pltpu.VMEM((ATOMS, CA), BF16),
            pltpu.VMEM((EXT, CA), BF16),
            pltpu.VMEM((EXT, CA), BF16),
            pltpu.VMEM((ATOMS, CA), F32),
            pltpu.VMEM((ATOMS, CA), F32),
            pltpu.VMEM((EXT, 128), BF16),
            pltpu.VMEM((EXT, CA), F32),
            pltpu.VMEM((EXT, CA), F32),
            pltpu.VMEM((7, CA, CA), BF16),
            pltpu.VMEM((HA, ATOMS, WK), BF16),
            pltpu.SemaphoreType.DMA((5,)),
        ],
        late=5,
        flops=2 * 1120 * 128 * 128 * 10,
        size=6 << 20,
    )
    update, *main = lax.optimization_barrier((update, *main))
    token_result = (
        sums[0] + main[0].astype(F32) + main[1].astype(F32) + main[2].astype(F32)
    ).astype(BF16)
    return (token_result[None], jnp.swapaxes(update, 0, 1))


def solution(mesh):
    in_specs = (
        P(("sample", "fsdp"), "seq", None),
        P(("sample", "fsdp"), "seq", None),
        P("fsdp", "seq", None),
        P("seq"),
        P(None, None, "fsdp"),
        P(None, None, "fsdp"),
        P("fsdp", None),
        P(None, None, "fsdp"),
        P("fsdp", None),
        P(),
        P(("sample", "fsdp"), "seq", None),
        P("seq", None),
        P(None, "seq", None),
        P("seq", None),
        P("seq"),
        P(None, None, "fsdp"),
        P("fsdp", None),
        P(),
        P(),
    )
    out_specs = (P(("sample", "fsdp"), "seq", None), P(("sample", "fsdp"), None, "seq"))
    return jax.shard_map(
        per_device, mesh=mesh, in_specs=in_specs, out_specs=out_specs, check_vma=False
    )
```

```python
import functools
import math

import jax
import jax.numpy as jnp
from jax import lax
from jax.experimental import pallas as pl
from jax.experimental.pallas import tpu as pltpu
from jax.sharding import PartitionSpec as P

EPS = 1e-05
FAR = -1e30
SENT = 1e30
LOG2E = 1.4426950408889634
HD = 48
HA = 4
WQ = 32
WK = 128
RIM = 48
NX = 4
NY = 4
NZ = 4
NC = 2
ROWS = 128
DIM = 768
COLS = 192
HEADS = 4
ATOMS = 1024
EXT = ATOMS + 2 * RIM
CHUNK = 112
CHUNKS = EXT // CHUNK
CA = 128
F32 = jnp.float32
BF16 = jnp.bfloat16


def x_shift(a, k):
    return lax.ppermute(a, "fsdp", [(i, (i + k) % NX) for i in range(NX)])


def y_shift(a, k):
    group = NZ * NC
    pairs = [(t, ((t // group + k) % NY) * group + t % group) for t in range(NY * group)]
    return lax.ppermute(a, "seq", pairs)


def z_shift(a, k):
    group = NZ * NC
    pairs = [
        (t, (t // group) * group + ((t // NC + k) % NZ) * NC + t % NC) for t in range(NY * group)
    ]
    return lax.ppermute(a, "seq", pairs)


def z_swap(a, k):
    return lax.ppermute(a, "seq", [(t, t ^ (NC * k)) for t in range(NY * NZ * NC)])


def y_exchange(a):
    group = NZ * NC
    groups = [[y * group + n for y in range(NY)] for n in range(group)]
    return lax.all_to_all(
        a, "seq", split_axis=0, concat_axis=0, axis_index_groups=groups, tiled=True
    )


def y_collect(a):
    group = NZ * NC
    groups = [[y * group + n for y in range(NY)] for n in range(group)]
    return lax.all_gather(a, "seq", axis=0, axis_index_groups=groups)


def c_shift(a):
    return lax.ppermute(a, "seq", [(t, t ^ 1) for t in range(NY * NZ * NC)])


def norm(values):
    center = values - jnp.mean(values, axis=-1, keepdims=True)
    spread = jnp.mean(center * center, axis=-1, keepdims=True)
    return center * lax.rsqrt(spread + EPS)


def sigmoid(v):
    return 1.0 / (1.0 + jnp.exp(-v))


def dot(a, b):
    return jnp.dot(a, b, preferred_element_type=F32)


def dot_nt(a, b):
    return lax.dot_general(a, b, (((1,), (1,)), ((), ())), preferred_element_type=F32)


def kernel_call(body, name, out_shape, args, scalars=(), scratch=(), flops=0, size=0, free=0, late=0, here=0):
    def whole(a):
        return pl.BlockSpec(
            a.shape, lambda i, n=len(a.shape): (0,) * n, pipeline_mode=pl.Buffered(1)
        )

    args = [
        a if i < free else pltpu.with_memory_space_constraint(a, pltpu.HBM)
        for i, a in enumerate(args)
    ]
    return pl.pallas_call(
        body,
        grid=(1,),
        out_shape=out_shape,
        in_specs=[pl.BlockSpec(memory_space=pltpu.SMEM)] * len(scalars)
        + [pl.BlockSpec(memory_space=pltpu.VMEM)] * here
        + [whole(a) for a in args[here : len(args) - late]]
        + [pl.BlockSpec(memory_space=pltpu.HBM)] * late,
        out_specs=jax.tree.map(whole, out_shape),
        scratch_shapes=list(scratch),
        compiler_params=pltpu.CompilerParams(
            dimension_semantics=("arbitrary",), vmem_limit_bytes=24 << 20
        ),
        cost_estimate=pl.CostEstimate(flops=flops, bytes_accessed=size, transcendentals=0)
        if size
        else None,
        name=name,
    )(*scalars, *args)


def shape(dims, kind=BF16):
    return pltpu.HBM(dims, kind)


def sent_shape(dims, kind=BF16):
    return jax.ShapeDtypeStruct(dims, kind)


def prepare_body(pos, act, cond, bias, *refs):
    outs, cut = refs[0:4], refs[4]
    cut[0] = bias[...]
    f = pos[0]
    normed = norm(cond[...].astype(F32)).astype(BF16)
    hat = norm(act[...].astype(F32))
    for k in range(NX):
        dest = lax.rem(f + k, NX)
        part = hat[:, 0:COLS]
        for j in range(1, NX):
            part = jnp.where(dest == j, hat[:, j * COLS : (j + 1) * COLS], part)
        outs[k][:, 0:DIM] = normed
        outs[k][:, DIM : DIM + COLS] = part.astype(BF16)


def adaptive_body(m0, m1, m2, m3, ada, offset, maps, attend, message):
    parts = (m0, m1, m2, m3)
    normed = jnp.concatenate([m[:, 0:DIM] for m in parts], axis=0)
    hat = jnp.concatenate([m[:, DIM : DIM + COLS] for m in parts], axis=0).astype(F32)
    message[DIM:, :] = maps[...]
    for n in range(2):
        scale = sigmoid(dot(normed, ada[2 * n]) + offset[n : n + 1, :])
        result = (scale * hat + dot(normed, ada[2 * n + 1])).astype(BF16)
        wide = jnp.concatenate([result[k * ROWS : (k + 1) * ROWS] for k in range(NX)], axis=1)
        if n == 0:
            attend[...] = wide
        else:
            for i in range(DIM // 128):
                message[i * ROWS : (i + 1) * ROWS, :] = wide[:, i * 128 : (i + 1) * 128]


def gathered_rows(part, j):
    return jnp.concatenate(
        [part[:, ((r - j) % NX) * COLS : ((r - j) % NX + 1) * COLS] for r in range(NX)],
        axis=0,
    )


def project_body(pos, a0, a1, a2, a3, weights, offset, mask, q, kv, g):
    f = pos[0]
    parts = (a0, a1, a2, a3)
    sums = [None] * 4
    for j in range(NX):
        rows = gathered_rows(parts[j][...], j)
        at = pl.multiple_of(lax.rem(f + NX - j, NX) * COLS, COLS)
        for n in range(4):
            term = dot(rows, weights[n, pl.ds(at, COLS), :])
            sums[n] = term if j == 0 else sums[n] + term
    live = mask[...] > 0
    for r in range(NX):
        own = slice(r * ROWS, (r + 1) * ROWS)
        to = slice(r * COLS, (r + 1) * COLS)
        q[:, to] = ((sums[0][own] + offset[0:1, :]) * (LOG2E / math.sqrt(HD))).astype(BF16)
        kv[0:ROWS, to] = jnp.where(live, sums[1][own], SENT).astype(BF16)
        kv[ROWS:, to] = sums[2][own].astype(BF16)
        g[:, to] = sums[3][own].astype(BF16)


def hidden_body(pos, w_in, w_out, parts, out):
    f = pos[0]
    gate, up = None, None
    for j in range(NX):
        src = lax.rem(f + NX - j, NX)
        wide = jnp.concatenate(
            [parts[src, i * ROWS : (i + 1) * ROWS, :] for i in range(DIM // 128)], axis=1
        )
        rows = gathered_rows(wide, j)
        at = pl.multiple_of(src * COLS, COLS)
        gate_term = dot(rows, w_in[0, pl.ds(at, COLS), :])
        up_term = dot(rows, w_in[1, pl.ds(at, COLS), :])
        gate = gate_term if j == 0 else gate + gate_term
        up = up_term if j == 0 else up + up_term
    hidden = (gate / (1.0 + jnp.exp(-gate)) * up).astype(BF16)
    out[...] = dot(hidden, w_out[...])


KEYS = NZ * NC * ROWS
PART = KEYS // 2


def spread_heads(first):
    head = (lax.broadcasted_iota(jnp.int32, (128, DIM), 0) - first) * HD
    lane = lax.broadcasted_iota(jnp.int32, (128, DIM), 1)
    return ((lane >= head) & (lane < head + HD)).astype(F32).astype(BF16)


def spread_rows(share, spread):
    high = share.astype(BF16)
    low = (share - high.astype(F32)).astype(BF16)
    return dot(high, spread) + dot(low, spread)


def attention_body(merge, pos, q, *refs):
    pairs = refs[0:4]
    bias = refs[4]
    refs = refs[5:]
    if merge:
        earlier, earlier_stats, refs = refs[0:4], refs[4:8], refs[8:]
        out, refs = refs[0:4], refs[4:]
    else:
        out, out_stats, refs = refs[0:4], refs[4:8], refs[8:]
    q_all, key_all, value_all, far_row, bias_all, stats, probs, total_all = refs[0:8]
    scores = refs[8:10]
    h = pl.program_id(0)
    y = pos[0]

    @pl.when(h == 0)
    def _():
        unit = (lax.broadcasted_iota(jnp.int32, (8, 128), 1) == 0).astype(F32).astype(BF16)
        for i in range(4):
            at = slice(i * ROWS, (i + 1) * ROWS)
            block = pairs[i][0:ROWS, :]
            first = dot_nt(unit, block[:, 0:128])
            far_row[:, at] = jnp.where(first > 1e20, FAR, 0.0)
            wide = block.astype(F32)
            key_all[at, :] = jnp.where(wide[:, 0:1] > 1e20, 0.0, wide).astype(BF16)
            value_all[at, :] = pairs[i][ROWS:, :]
        for n in range(NY):
            q_all[n * ROWS : (n + 1) * ROWS, :] = q[lax.rem(y + NY - n, NY)]
        stats[...] = jnp.zeros_like(stats)

    for n in range(NY):
        src = lax.rem(y + NY - n, NY)
        for i in range(4):
            at = slice(i * ROWS, (i + 1) * ROWS)
            part = bias[src, 0, :, pl.ds(pl.multiple_of(pos[1 + i] * ROWS, ROWS), ROWS)]
            bias_all[n, :, at] = part.astype(F32) * LOG2E + far_row[0:1, at]

    lane = lax.broadcasted_iota(jnp.int32, (NY * ROWS, 256), 1)
    slot = lax.broadcasted_iota(jnp.int32, (ROWS, 128), 1)
    windows, mines, rows = [], [], []
    for s in range(NX):
        lane0 = COLS * s + HD * h
        start = jnp.minimum(lane0 // 128, (DIM - 256) // 128)
        off = lane0 - start * 128
        window = pl.ds(pl.multiple_of(start * 128, 128), 256)
        mine = (lane >= off) & (lane < off + HD)
        windows.append(window)
        mines.append(mine)
        rows.append(jnp.where(mine, q_all[:, window].astype(F32), 0.0).astype(BF16))

    def score(s, j):
        keys = slice(j * 256, (j + 1) * 256)
        scores[s % 2][:, keys] = dot_nt(rows[s], key_all[keys, windows[s]])

    for j in range(PART // 256):
        score(0, j)
    for s in range(NX):
        index = s * HEADS + h
        of_max = (lax.rem(slot, 16) == index) & (slot < 48)
        of_total = (lax.rem(slot, 16) == index) & (slot >= 48) & (slot < 96)
        totals = []
        for n in range(NY):
            if s + 1 < NX and n < PART // 256:
                score(s + 1, n)
            own = slice(n * ROWS, (n + 1) * ROWS)
            part = scores[s % 2][own, :] + bias_all[n]
            top = jnp.max(part, axis=1, keepdims=True)
            part = jnp.exp2(part - top)
            total = jnp.sum(part, axis=1, keepdims=True)
            probs[own, :] = part.astype(BF16)
            totals.append(total)
            stats[n] = jnp.where(of_max, top, jnp.where(of_total, total, stats[n]))
        summed = dot(probs[...], value_all[:, windows[s]])
        for n in range(NY):
            own = slice(n * ROWS, (n + 1) * ROWS)
            scaled = summed[own] * (1.0 / totals[n])
            before = total_all[own, windows[s]]
            total_all[own, windows[s]] = jnp.where(mines[s][own], scaled, before)

    @pl.when(h == HEADS - 1)
    def _():
        third = lax.rem(slot // 16, 3)
        spread = spread_heads(48)
        for n in range(NY):
            own = slice(n * ROWS, (n + 1) * ROWS)
            whole = stats[n]
            if not merge:
                out[n][...] = total_all[own, :].astype(BF16)
                out_stats[n][...] = whole
                continue
            other = earlier_stats[n][...]
            top = jnp.maximum(whole, other)
            top_there = pltpu.roll(top, 48, 1)
            now = whole * jnp.exp2(jnp.minimum(pltpu.roll(whole, 48, 1) - top_there, 0.0))
            then = other * jnp.exp2(jnp.minimum(pltpu.roll(other, 48, 1) - top_there, 0.0))
            both = now + then
            used = (slot >= 48) & (slot < 64)
            share_now = jnp.where(used, now / both, 0.0)
            share_then = jnp.where(used, then / both, 0.0)
            merged = spread_rows(share_now, spread) * total_all[own, :]
            merged += spread_rows(share_then, spread) * earlier[n][...].astype(F32)
            out[n][:, 0:DIM] = merged.astype(BF16)
            whole = jnp.where(slot < 48, top, jnp.where(slot < 96, both, 0.0))
            high = whole.astype(BF16).astype(F32)
            rest = whole - high
            middle = rest.astype(BF16).astype(F32)
            low = rest - middle
            sent = jnp.where(third == 0, high, jnp.where(third == 1, middle, low))
            out[n][:, DIM : DIM + 128] = sent.astype(BF16)


def attention(pos, q, pairs, bias, earlier=None):
    once = pl.Buffered(1)

    def whole(dims):
        return pl.BlockSpec(dims, lambda h, n=len(dims): (0,) * n, pipeline_mode=once)

    merge = earlier is not None
    in_specs = [pl.BlockSpec(memory_space=pltpu.SMEM), whole((NY, ROWS, DIM))]
    in_specs += [whole((2 * ROWS, DIM))] * 4
    in_specs += [pl.BlockSpec((NY, 1, ROWS, KEYS), lambda h: (0, h, 0, 0))]
    args = [q, *pairs, bias]
    if merge:
        in_specs += [whole((ROWS, DIM))] * 4 + [whole((ROWS, 128))] * 4
        args += earlier
        outs = [sent_shape((ROWS, DIM + 128))] * 4
    else:
        outs = [shape((ROWS, DIM))] * 4 + [shape((ROWS, 128), F32)] * 4
    return pl.pallas_call(
        functools.partial(attention_body, merge),
        grid=(HEADS,),
        out_shape=outs,
        in_specs=in_specs,
        out_specs=[whole(o.shape) for o in outs],
        scratch_shapes=[
            pltpu.VMEM((NY * ROWS, DIM), BF16),
            pltpu.VMEM((PART, DIM), BF16),
            pltpu.VMEM((PART, DIM), BF16),
            pltpu.VMEM((8, PART), F32),
            pltpu.VMEM((NY, ROWS, PART), F32),
            pltpu.VMEM((NY, ROWS, 128), F32),
            pltpu.VMEM((NY * ROWS, PART), BF16),
            pltpu.VMEM((NY * ROWS, DIM), F32),
            pltpu.VMEM((NY * ROWS, PART), F32),
            pltpu.VMEM((NY * ROWS, PART), F32),
        ],
        compiler_params=pltpu.CompilerParams(
            dimension_semantics=("arbitrary",), vmem_limit_bytes=32 << 20
        ),
        name="attention_last" if merge else "attention_first",
    )(pos, *(pltpu.with_memory_space_constraint(a, pltpu.HBM) for a in args))


def combined(parts):
    tops, totals = [], []
    for o in parts:
        sent = o[:, DIM : DIM + 128].astype(F32)
        whole = sent + pltpu.roll(sent, 128 - 16, 1) + pltpu.roll(sent, 128 - 32, 1)
        tops.append(whole)
        totals.append(pltpu.roll(whole, 128 - 48, 1))
    used = lax.broadcasted_iota(jnp.int32, (ROWS, 128), 1) < NX * HEADS
    tops = [jnp.where(used, t, 0.0) for t in tops]
    totals = [jnp.where(used, t, 1.0) for t in totals]
    top = jnp.maximum(jnp.maximum(tops[0], tops[1]), jnp.maximum(tops[2], tops[3]))
    shares = [n * jnp.exp2(t - top) for t, n in zip(tops, totals)]
    inverse = 1.0 / (shares[0] + shares[1] + shares[2] + shares[3])
    spread = spread_heads(0)
    attended = None
    for o, share in zip(parts, shares):
        term = spread_rows(share * inverse, spread) * o[:, 0:DIM].astype(F32)
        attended = term if attended is None else attended + term
    return attended


def combine_body(*refs):
    gate, ffn, w_out, w_atom, act = refs[4:9]
    outs = refs[9:]
    attended = combined(refs[0:4])
    gated = (attended * sigmoid(gate[...].astype(F32))).astype(BF16)
    for r in range(NX):
        part = dot(gated[:, r * COLS : (r + 1) * COLS], w_out[...]) + ffn[r * ROWS : (r + 1) * ROWS]
        small = part.astype(BF16)
        rows = dot(small, w_atom[...])
        if r == 0:
            outs[0][...] = part + act[...].astype(F32)
            outs[4][...] = rows + dot(act[...], w_atom[...])
        else:
            outs[r][...] = small
            outs[4 + r][...] = rows.astype(BF16)


def atom_first_body(starts, maps, cond, tokens, offset, *outs):
    weights, project, scale, shift, select = outs
    for src in range(NX):
        project[src * COLS : (src + 1) * COLS, :] = maps[src, DIM : DIM + COLS, :]
        for i in range(7):
            line = DIM + COLS + i * 32
            weights[i, src * 32 : (src + 1) * 32, :] = maps[src, line : line + 32, :]
    normed = norm(cond[...].astype(F32)).astype(BF16)
    scale[...] = sigmoid(dot_nt(normed, weights[0]) + offset[0:1, :])
    shift[...] = dot_nt(normed, weights[1])
    row = lax.broadcasted_iota(jnp.int32, (128, CHUNK), 0)
    for i in range(CHUNKS):
        hit = ((row + starts[i]) == tokens[i : i + 1, :]).astype(F32)
        select[i * CHUNK : (i + 1) * CHUNK, :] = hit.T.astype(BF16)


def atom_body(pos, starts, bounds, near, far, offset, spots, *refs):
    out = refs[8]
    table, skip, state, xs, qs, ks, vs, gs, at_all = refs[9:18]
    select, scale, shift, weights, bias = refs[18:23]
    sems = refs[23]
    rim = pl.ds(0, RIM)
    moves = [
        (refs[0].at[rim], skip.at[rim]),
        (refs[1], skip.at[pl.ds(RIM, ATOMS)]),
        (refs[2].at[rim], skip.at[pl.ds(RIM + ATOMS, RIM)]),
    ]
    moves += [(refs[3 + i], refs[18 + i]) for i in range(5)]
    copies = []
    for i, (there, here) in enumerate(moves):
        copies.append(pltpu.make_async_copy(there, here, sems.at[i]))
        copies[i].start()
    y, z, c = pos[0], pos[1], pos[2]
    for ky in range(NY):
        for kz in range(NZ):
            place = lax.rem(y + NY - ky, NY) * (NZ * NC) + lax.rem(z + NZ - kz, NZ) * NC
            n = (kz * NY + ky) * ROWS
            own = pl.multiple_of((place + c) * ROWS, ROWS)
            other = pl.multiple_of((place + 1 - c) * ROWS, ROWS)
            table[pl.ds(own, ROWS), :] = near[n : n + ROWS, :]
            table[pl.ds(other, ROWS), :] = far[n : n + ROWS, :]
    for i in range(6):
        copies[i].wait()
    for i in range(CHUNKS):
        rows = slice(i * CHUNK, (i + 1) * CHUNK)
        taken = table[pl.ds(pl.multiple_of(starts[i], 16), 128), :]
        now = skip[rows, :].astype(F32) + dot(select[rows, :], taken)
        state[rows, :] = now
        xs[rows, :] = (scale[rows, :] * norm(now) + shift[rows, :]).astype(BF16)
    copies[6].wait()
    x = xs[...]
    own = slice(RIM, RIM + ATOMS)
    mine = xs[own, :]
    qs[...] = (
        (dot_nt(mine, weights[2]) + offset[1:2, :]) * (LOG2E / math.sqrt(CA // HA))
    ).astype(BF16)
    ks[...] = dot_nt(x, weights[3]).astype(BF16)
    vs[...] = dot_nt(x, weights[4]).astype(BF16)
    gs[...] = sigmoid(dot_nt(mine, weights[5]).astype(BF16).astype(F32))
    width = CA // HA
    head_of_row = lax.broadcasted_iota(jnp.int32, (HA * WQ, CA), 0) // WQ
    head_of_lane = lax.broadcasted_iota(jnp.int32, (HA * WQ, CA), 1) // width
    same = head_of_row == head_of_lane
    lane_head = lax.broadcasted_iota(jnp.int32, (WQ, CA), 1) // width
    key_slot = lax.broadcasted_iota(jnp.int32, (HA * WQ, WK), 1)

    def window(b):
        rows = slice(b * WQ, (b + 1) * WQ)
        span = slice(b * WQ, b * WQ + WK)
        one = qs[rows, :].astype(F32)
        four = jnp.where(same, jnp.concatenate([one] * HA, axis=0), 0.0).astype(BF16)
        extra = jnp.concatenate([bias[i, rows, :] for i in range(HA)], axis=0).astype(F32)
        scores = dot_nt(four, ks[span, :]) + extra * LOG2E
        base = pos[3] + b * WQ - RIM
        low = bounds[0, b] - base
        high = bounds[1, b] - base
        scores = jnp.where((key_slot >= low) & (key_slot < high), scores, FAR)
        probs = jnp.exp2(scores - jnp.max(scores, axis=1, keepdims=True))
        total = jnp.sum(probs, axis=1, keepdims=True)
        summed = dot(probs.astype(BF16), vs[span, :]) * (1.0 / total)
        picked = summed[0:WQ]
        for i in range(1, HA):
            picked = jnp.where(lane_head == i, summed[i * WQ : (i + 1) * WQ], picked)
        at_all[rows, :] = picked

    copies[7].wait()
    for b in range(ATOMS // WQ):
        window(b)
    gated = (at_all[...] * gs[...]).astype(BF16)
    new = state[own, :] + dot_nt(gated, weights[6])
    final = norm(new).astype(BF16)
    update = dot_nt(spots[...], final)
    for i in range(3):
        out[i] = update[i : i + 1, :]


def per_device(
    token_act,
    token_cond,
    pair_bias,
    token_mask,
    ada_weights,
    attention_in,
    attention_out,
    transition_in,
    transition_out,
    token_vectors,
    atom_skip,
    atom_cond,
    atom_bias,
    window_bounds,
    atom_token,
    atom_weights,
    token_to_atom,
    atom_vectors,
    position_out,
):
    f = lax.axis_index("fsdp").astype(jnp.int32)
    t = lax.axis_index("seq").astype(jnp.int32)
    y, z, c = t // (NZ * NC), (t // NC) % NZ, t % NC
    f_pos = f.reshape(1)
    act = token_act[0]

    block = pl.BlockSpec((ROWS // NY, DIM), lambda i: (i, 0))
    wide = pl.BlockSpec((ROWS // NY, DIM + COLS), lambda i: (i, 0))
    *sent, cut = pl.pallas_call(
        prepare_body,
        grid=(NY,),
        out_shape=[sent_shape((ROWS, DIM + COLS))] * 4 + [shape((NY, HEADS, ROWS, KEYS))],
        in_specs=[
            pl.BlockSpec(memory_space=pltpu.SMEM),
            block,
            block,
            pl.BlockSpec((HEADS, ROWS, KEYS), lambda i: (0, 0, i)),
        ],
        out_specs=[wide] * 4 + [pl.BlockSpec((1, HEADS, ROWS, KEYS), lambda i: (i, 0, 0, 0))],
        compiler_params=pltpu.CompilerParams(
            dimension_semantics=("arbitrary",), vmem_limit_bytes=24 << 20
        ),
        name="prepare",
    )(
        f_pos,
        pltpu.with_memory_space_constraint(act, pltpu.HBM),
        pltpu.with_memory_space_constraint(token_cond[0], pltpu.HBM),
        pltpu.with_memory_space_constraint(pair_bias, pltpu.HBM),
    )
    normed = [sent[0]] + [x_shift(sent[k], k) for k in (1, 2, 3)]
    edge_skip, edge_cond, edge_token, _ = lax.optimization_barrier(
        (atom_skip[0], atom_cond, atom_token, sent[0])
    )

    turned = jnp.swapaxes(atom_weights, 1, 2).reshape(7 * 32, CA)
    own_maps = jnp.concatenate([token_to_atom, turned], axis=0)
    skip = atom_skip[0]
    coded = jnp.stack([edge_token // 64, edge_token % 64]).astype(BF16)

    def edge(lo, hi):
        codes = jnp.pad(coded[:, lo:hi], ((0, 14), (0, CA - RIM)))
        return jnp.concatenate([edge_skip[lo:hi], edge_cond[lo:hi], codes], axis=0)

    size = lax.axis_size("seq")
    up = [(i, i + 1) for i in range(size - 1)]
    before = lax.ppermute(edge(ATOMS - RIM, ATOMS), "seq", up)
    after = lax.ppermute(edge(0, RIM), "seq", [(j, i) for i, j in up])

    bias = y_exchange(cut)

    def decoded(side):
        pair = side[2 * RIM : 2 * RIM + 2, 0:RIM].astype(jnp.int32)
        return pair[0] * 64 + pair[1]

    cond_ext = jnp.concatenate([before[RIM : 2 * RIM], atom_cond, after[RIM : 2 * RIM]], axis=0)
    token_ext = jnp.concatenate([decoded(before), atom_token, decoded(after)])
    by_chunk = token_ext.reshape(CHUNKS, CHUNK)
    token_count = size * ROWS
    starts = jnp.minimum((by_chunk[:, 0] // 16) * 16, token_count - 128)

    offsets = lax.dynamic_slice_in_dim(token_vectors, f * COLS, COLS, 1)
    attend, message = kernel_call(
        adaptive_body,
        "adaptive",
        [sent_shape((ROWS, DIM)), shape((DIM + COLS + 7 * 32, CA))],
        (*normed, ada_weights, offsets[0:2], own_maps),
        free=7,
        flops=4 * 2 * 512 * 768 * 192,
        size=3 << 20,
    )
    attend_all = [attend] + [x_shift(attend, k) for k in (1, 2, 3)]
    attend_all[3], before, after = lax.optimization_barrier((attend_all[3], before, after))
    q, kv, gate = kernel_call(
        project_body,
        "project",
        [sent_shape((ROWS, DIM)), sent_shape((2 * ROWS, DIM)), shape((ROWS, DIM))],
        free=7,
        args=(*attend_all, attention_in, offsets[2:3], token_mask.reshape(ROWS, 1)),
        scalars=(f_pos,),
        flops=4 * 2 * 512 * 768 * 192,
        size=4 << 20,
    )
    near = [kv] + [z_swap(kv, k) for k in (1, 2, 3)]
    across = c_shift(kv)
    q_all = y_collect(q)
    q_all, near_1 = lax.optimization_barrier((q_all, near[1]))
    early = [kv, near_1, across, c_shift(near_1)]

    message, _ = lax.optimization_barrier((message, q))
    messages = lax.all_gather(message, "fsdp", axis=0)
    ffn = kernel_call(
        hidden_body,
        "hidden",
        shape((NX * ROWS, DIM), F32),
        (transition_in, transition_out, messages),
        (f_pos,),
        free=2,
        flops=3 * 2 * 512 * 768 * 384,
        size=6 << 20,
    )
    atom_maps, project_full, scale, shift, select = kernel_call(
        atom_first_body,
        "atom_first",
        [
            shape((7, CA, CA)),
            shape((DIM, CA)),
            shape((EXT, CA), F32),
            shape((EXT, CA), F32),
            shape((EXT, 128)),
        ],
        (messages, cond_ext, by_chunk, atom_vectors),
        (starts,),
        flops=4 * EXT * CA * CA,
        size=3 << 20,
    )

    def places(n):
        at = [(z ^ n) * NC + c, (z ^ (n + 1)) * NC + c]
        return jnp.stack([y, *at, at[0] ^ 1, at[1] ^ 1])

    first = attention(places(0), q_all, early, bias)
    _, near_2, near_3 = lax.optimization_barrier((first[0], near[2], near[3]))
    late = [near_2, near_3, c_shift(near_2), c_shift(near_3)]
    out = attention(places(2), q_all, late, bias, first)
    parts = [out[0]] + [y_shift(out[k], NY - k) for k in (1, 2, 3)]
    sums = kernel_call(
        combine_body,
        "combine",
        [shape((ROWS, DIM), F32)]
        + [sent_shape((ROWS, DIM))] * 3
        + [sent_shape((ROWS, CA), F32)]
        + [sent_shape((ROWS, CA))] * 3,
        (*parts, gate, ffn, attention_out, project_full, act),
        free=4,
        flops=4 * 2 * 128 * 768 * (192 + 128) + 8 * 2 * 128 * 128 * 768,
        size=5 << 20,
    )
    arrived = [x_shift(sums[4 + k], NX - k) for k in (1, 2, 3)]
    rows = (
        sums[4] + arrived[0].astype(F32) + arrived[1].astype(F32) + arrived[2].astype(F32)
    ).astype(BF16)

    turns = [y_shift(rows, k) for k in (1, 2, 3)]
    by_y = jnp.concatenate([rows] + turns, axis=0)
    turns = [z_shift(by_y, k) for k in (1, 2, 3)]
    by_z = jnp.concatenate([by_y] + turns, axis=0)
    by_c = c_shift(by_z)
    _, *partial = lax.optimization_barrier((by_y, *sums[1:4]))
    main = [x_shift(partial[k - 1], NX - k) for k in (1, 2, 3)]

    scalars = (jnp.stack([y, z, c, t * ATOMS]), starts, window_bounds.T)
    update = kernel_call(
        atom_body,
        "atoms",
        shape((3, 1, ATOMS), F32),
        (
            by_z,
            by_c,
            atom_vectors,
            position_out,
            before,
            skip,
            after,
            select,
            scale,
            shift,
            atom_maps,
            atom_bias,
        ),
        scalars,
        free=2,
        scratch=[
            pltpu.VMEM((token_count, CA), BF16),
            pltpu.VMEM((EXT, CA), BF16),
            pltpu.VMEM((EXT, CA), F32),
            pltpu.VMEM((EXT, CA), BF16),
            pltpu.VMEM((ATOMS, CA), BF16),
            pltpu.VMEM((EXT, CA), BF16),
            pltpu.VMEM((EXT, CA), BF16),
            pltpu.VMEM((ATOMS, CA), F32),
            pltpu.VMEM((ATOMS, CA), F32),
            pltpu.VMEM((EXT, 128), BF16),
            pltpu.VMEM((EXT, CA), F32),
            pltpu.VMEM((EXT, CA), F32),
            pltpu.VMEM((7, CA, CA), BF16),
            pltpu.VMEM((HA, ATOMS, WK), BF16),
            pltpu.SemaphoreType.DMA((8,)),
        ],
        late=8,
        here=2,
    )
    update, *main = lax.optimization_barrier((update, *main))
    token_result = (
        sums[0] + main[0].astype(F32) + main[1].astype(F32) + main[2].astype(F32)
    ).astype(BF16)
    return (token_result[None], jnp.swapaxes(update, 0, 1))


def solution(mesh):
    in_specs = (
        P(("sample", "fsdp"), "seq", None),
        P(("sample", "fsdp"), "seq", None),
        P("fsdp", "seq", None),
        P("seq"),
        P(None, None, "fsdp"),
        P(None, None, "fsdp"),
        P("fsdp", None),
        P(None, None, "fsdp"),
        P("fsdp", None),
        P(),
        P(("sample", "fsdp"), "seq", None),
        P("seq", None),
        P(None, "seq", None),
        P("seq", None),
        P("seq"),
        P(None, None, "fsdp"),
        P("fsdp", None),
        P(),
        P(),
    )
    out_specs = (P(("sample", "fsdp"), "seq", None), P(("sample", "fsdp"), None, "seq"))
    return jax.shard_map(
        per_device, mesh=mesh, in_specs=in_specs, out_specs=out_specs, check_vma=False
    )
```

```python
import functools
import math

import jax
import jax.numpy as jnp
from jax import lax
from jax.experimental import pallas as pl
from jax.experimental.pallas import tpu as pltpu
from jax.sharding import PartitionSpec as P

EPS = 1e-05
FAR = -1e30
SENT = 1e30
LOG2E = 1.4426950408889634
HD = 48
HA = 4
WQ = 32
WK = 128
RIM = 48
NX = 4
NY = 4
NZ = 4
NC = 2
ROWS = 128
DIM = 768
COLS = 192
HEADS = 4
ATOMS = 1024
EXT = ATOMS + 2 * RIM
CHUNK = 112
CHUNKS = EXT // CHUNK
CA = 128
F32 = jnp.float32
BF16 = jnp.bfloat16


def x_shift(a, k):
    return lax.ppermute(a, "fsdp", [(i, (i + k) % NX) for i in range(NX)])


def y_shift(a, k):
    group = NZ * NC
    pairs = [(t, ((t // group + k) % NY) * group + t % group) for t in range(NY * group)]
    return lax.ppermute(a, "seq", pairs)


def z_shift(a, k):
    group = NZ * NC
    pairs = [
        (t, (t // group) * group + ((t // NC + k) % NZ) * NC + t % NC) for t in range(NY * group)
    ]
    return lax.ppermute(a, "seq", pairs)


def z_swap(a, k):
    return lax.ppermute(a, "seq", [(t, t ^ (NC * k)) for t in range(NY * NZ * NC)])


def y_exchange(a):
    group = NZ * NC
    groups = [[y * group + n for y in range(NY)] for n in range(group)]
    return lax.all_to_all(
        a, "seq", split_axis=0, concat_axis=0, axis_index_groups=groups, tiled=True
    )


def y_collect(a):
    group = NZ * NC
    groups = [[y * group + n for y in range(NY)] for n in range(group)]
    return lax.all_gather(a, "seq", axis=0, axis_index_groups=groups)


def c_shift(a):
    return lax.ppermute(a, "seq", [(t, t ^ 1) for t in range(NY * NZ * NC)])


def norm(values):
    center = values - jnp.mean(values, axis=-1, keepdims=True)
    spread = jnp.mean(center * center, axis=-1, keepdims=True)
    return center * lax.rsqrt(spread + EPS)


def sigmoid(v):
    return 1.0 / (1.0 + jnp.exp(-v))


def dot(a, b):
    return jnp.dot(a, b, preferred_element_type=F32)


def dot_nt(a, b):
    return lax.dot_general(a, b, (((1,), (1,)), ((), ())), preferred_element_type=F32)


def kernel_call(body, name, out_shape, args, scalars=(), scratch=(), flops=0, size=0, free=0, late=0, here=0):
    def whole(a):
        return pl.BlockSpec(
            a.shape, lambda i, n=len(a.shape): (0,) * n, pipeline_mode=pl.Buffered(1)
        )

    args = [
        a if i < free else pltpu.with_memory_space_constraint(a, pltpu.HBM)
        for i, a in enumerate(args)
    ]
    return pl.pallas_call(
        body,
        grid=(1,),
        out_shape=out_shape,
        in_specs=[pl.BlockSpec(memory_space=pltpu.SMEM)] * len(scalars)
        + [pl.BlockSpec(memory_space=pltpu.VMEM)] * here
        + [whole(a) for a in args[here : len(args) - late]]
        + [pl.BlockSpec(memory_space=pltpu.HBM)] * late,
        out_specs=jax.tree.map(whole, out_shape),
        scratch_shapes=list(scratch),
        compiler_params=pltpu.CompilerParams(
            dimension_semantics=("arbitrary",), vmem_limit_bytes=24 << 20
        ),
        cost_estimate=pl.CostEstimate(flops=flops, bytes_accessed=size, transcendentals=0)
        if size
        else None,
        name=name,
    )(*scalars, *args)


def shape(dims, kind=BF16):
    return pltpu.HBM(dims, kind)


def sent_shape(dims, kind=BF16):
    return jax.ShapeDtypeStruct(dims, kind)


def cut_body(bias, cut):
    cut[0] = bias[...]


def prepare_body(pos, act, cond, *outs):
    f = pos[0]
    normed = norm(cond[...].astype(F32)).astype(BF16)
    hat = norm(act[...].astype(F32))
    for k in range(NX):
        dest = lax.rem(f + k, NX)
        part = hat[:, 0:COLS]
        for j in range(1, NX):
            part = jnp.where(dest == j, hat[:, j * COLS : (j + 1) * COLS], part)
        outs[k][:, 0:DIM] = normed
        outs[k][:, DIM : DIM + COLS] = part.astype(BF16)


def adaptive_body(m0, m1, m2, m3, ada, offset, maps, attend, message):
    parts = (m0, m1, m2, m3)
    normed = jnp.concatenate([m[:, 0:DIM] for m in parts], axis=0)
    hat = jnp.concatenate([m[:, DIM : DIM + COLS] for m in parts], axis=0).astype(F32)
    message[DIM:, :] = maps[...]
    for n in range(2):
        scale = sigmoid(dot(normed, ada[2 * n]) + offset[n : n + 1, :])
        result = (scale * hat + dot(normed, ada[2 * n + 1])).astype(BF16)
        wide = jnp.concatenate([result[k * ROWS : (k + 1) * ROWS] for k in range(NX)], axis=1)
        if n == 0:
            attend[...] = wide
        else:
            for i in range(DIM // 128):
                message[i * ROWS : (i + 1) * ROWS, :] = wide[:, i * 128 : (i + 1) * 128]


def gathered_rows(part, j):
    return jnp.concatenate(
        [part[:, ((r - j) % NX) * COLS : ((r - j) % NX + 1) * COLS] for r in range(NX)],
        axis=0,
    )


def project_body(pos, a0, a1, a2, a3, weights, offset, mask, q, kv, g):
    f = pos[0]
    parts = (a0, a1, a2, a3)
    sums = [None] * 4
    for j in range(NX):
        rows = gathered_rows(parts[j][...], j)
        at = pl.multiple_of(lax.rem(f + NX - j, NX) * COLS, COLS)
        for n in range(4):
            term = dot(rows, weights[n, pl.ds(at, COLS), :])
            sums[n] = term if j == 0 else sums[n] + term
    live = mask[...] > 0
    for r in range(NX):
        own = slice(r * ROWS, (r + 1) * ROWS)
        to = slice(r * COLS, (r + 1) * COLS)
        q[:, to] = ((sums[0][own] + offset[0:1, :]) * (LOG2E / math.sqrt(HD))).astype(BF16)
        kv[0:ROWS, to] = jnp.where(live, sums[1][own], SENT).astype(BF16)
        kv[ROWS:, to] = sums[2][own].astype(BF16)
        g[:, to] = sums[3][own].astype(BF16)


def hidden_body(pos, w_in, w_out, parts, out):
    f = pos[0]
    gate, up = None, None
    for j in range(NX):
        src = lax.rem(f + NX - j, NX)
        wide = jnp.concatenate(
            [parts[src, i * ROWS : (i + 1) * ROWS, :] for i in range(DIM // 128)], axis=1
        )
        rows = gathered_rows(wide, j)
        at = pl.multiple_of(src * COLS, COLS)
        gate_term = dot(rows, w_in[0, pl.ds(at, COLS), :])
        up_term = dot(rows, w_in[1, pl.ds(at, COLS), :])
        gate = gate_term if j == 0 else gate + gate_term
        up = up_term if j == 0 else up + up_term
    hidden = (gate / (1.0 + jnp.exp(-gate)) * up).astype(BF16)
    out[...] = dot(hidden, w_out[...])


KEYS = NZ * NC * ROWS
PART = KEYS // 2


def spread_heads(first):
    head = (lax.broadcasted_iota(jnp.int32, (128, DIM), 0) - first) * HD
    lane = lax.broadcasted_iota(jnp.int32, (128, DIM), 1)
    return ((lane >= head) & (lane < head + HD)).astype(F32).astype(BF16)


def spread_rows(share, spread):
    high = share.astype(BF16)
    low = (share - high.astype(F32)).astype(BF16)
    return dot(high, spread) + dot(low, spread)


def attention_body(merge, pos, q, *refs):
    pairs = refs[0:4]
    bias = refs[4]
    refs = refs[5:]
    if merge:
        earlier, earlier_stats, refs = refs[0:4], refs[4:8], refs[8:]
        out, refs = refs[0:4], refs[4:]
    else:
        out, out_stats, refs = refs[0:4], refs[4:8], refs[8:]
    q_all, key_all, value_all, far_row, bias_all, stats, probs, total_all = refs[0:8]
    scores = refs[8:10]
    h = pl.program_id(0)
    y = pos[0]

    @pl.when(h == 0)
    def _():
        unit = (lax.broadcasted_iota(jnp.int32, (8, 128), 1) == 0).astype(F32).astype(BF16)
        for i in range(4):
            at = slice(i * ROWS, (i + 1) * ROWS)
            block = pairs[i][0:ROWS, :]
            first = dot_nt(unit, block[:, 0:128])
            far_row[:, at] = jnp.where(first > 1e20, FAR, 0.0)
            wide = block.astype(F32)
            key_all[at, :] = jnp.where(wide[:, 0:1] > 1e20, 0.0, wide).astype(BF16)
            value_all[at, :] = pairs[i][ROWS:, :]
        for n in range(NY):
            q_all[n * ROWS : (n + 1) * ROWS, :] = q[lax.rem(y + NY - n, NY)]
        stats[...] = jnp.zeros_like(stats)

    for n in range(NY):
        src = lax.rem(y + NY - n, NY)
        for i in range(4):
            at = slice(i * ROWS, (i + 1) * ROWS)
            part = bias[src, 0, :, pl.ds(pl.multiple_of(pos[1 + i] * ROWS, ROWS), ROWS)]
            bias_all[n, :, at] = part.astype(F32) * LOG2E + far_row[0:1, at]

    lane = lax.broadcasted_iota(jnp.int32, (NY * ROWS, 256), 1)
    slot = lax.broadcasted_iota(jnp.int32, (ROWS, 128), 1)
    windows, mines, rows = [], [], []
    for s in range(NX):
        lane0 = COLS * s + HD * h
        start = jnp.minimum(lane0 // 128, (DIM - 256) // 128)
        off = lane0 - start * 128
        window = pl.ds(pl.multiple_of(start * 128, 128), 256)
        mine = (lane >= off) & (lane < off + HD)
        windows.append(window)
        mines.append(mine)
        rows.append(jnp.where(mine, q_all[:, window].astype(F32), 0.0).astype(BF16))

    def score(s, j):
        keys = slice(j * 256, (j + 1) * 256)
        scores[s % 2][:, keys] = dot_nt(rows[s], key_all[keys, windows[s]])

    for j in range(PART // 256):
        score(0, j)
    for s in range(NX):
        index = s * HEADS + h
        of_max = (lax.rem(slot, 16) == index) & (slot < 48)
        of_total = (lax.rem(slot, 16) == index) & (slot >= 48) & (slot < 96)
        totals = []
        for n in range(NY):
            if s + 1 < NX and n < PART // 256:
                score(s + 1, n)
            own = slice(n * ROWS, (n + 1) * ROWS)
            part = scores[s % 2][own, :] + bias_all[n]
            top = jnp.max(part, axis=1, keepdims=True)
            part = jnp.exp2(part - top)
            total = jnp.sum(part, axis=1, keepdims=True)
            probs[own, :] = part.astype(BF16)
            totals.append(total)
            stats[n] = jnp.where(of_max, top, jnp.where(of_total, total, stats[n]))
        summed = dot(probs[...], value_all[:, windows[s]])
        for n in range(NY):
            own = slice(n * ROWS, (n + 1) * ROWS)
            scaled = summed[own] * (1.0 / totals[n])
            before = total_all[own, windows[s]]
            total_all[own, windows[s]] = jnp.where(mines[s][own], scaled, before)

    @pl.when(h == HEADS - 1)
    def _():
        third = lax.rem(slot // 16, 3)
        spread = spread_heads(48)
        for n in range(NY):
            own = slice(n * ROWS, (n + 1) * ROWS)
            whole = stats[n]
            if not merge:
                out[n][...] = total_all[own, :].astype(BF16)
                out_stats[n][...] = whole
                continue
            other = earlier_stats[n][...]
            top = jnp.maximum(whole, other)
            top_there = pltpu.roll(top, 48, 1)
            now = whole * jnp.exp2(jnp.minimum(pltpu.roll(whole, 48, 1) - top_there, 0.0))
            then = other * jnp.exp2(jnp.minimum(pltpu.roll(other, 48, 1) - top_there, 0.0))
            both = now + then
            used = (slot >= 48) & (slot < 64)
            share_now = jnp.where(used, now / both, 0.0)
            share_then = jnp.where(used, then / both, 0.0)
            merged = spread_rows(share_now, spread) * total_all[own, :]
            merged += spread_rows(share_then, spread) * earlier[n][...].astype(F32)
            out[n][:, 0:DIM] = merged.astype(BF16)
            whole = jnp.where(slot < 48, top, jnp.where(slot < 96, both, 0.0))
            high = whole.astype(BF16).astype(F32)
            rest = whole - high
            middle = rest.astype(BF16).astype(F32)
            low = rest - middle
            sent = jnp.where(third == 0, high, jnp.where(third == 1, middle, low))
            out[n][:, DIM : DIM + 128] = sent.astype(BF16)


def attention(pos, q, pairs, bias, earlier=None):
    once = pl.Buffered(1)

    def whole(dims):
        return pl.BlockSpec(dims, lambda h, n=len(dims): (0,) * n, pipeline_mode=once)

    merge = earlier is not None
    in_specs = [pl.BlockSpec(memory_space=pltpu.SMEM), whole((NY, ROWS, DIM))]
    in_specs += [whole((2 * ROWS, DIM))] * 4
    in_specs += [pl.BlockSpec((NY, 1, ROWS, KEYS), lambda h: (0, h, 0, 0))]
    args = [q, *pairs, bias]
    if merge:
        in_specs += [whole((ROWS, DIM))] * 4 + [whole((ROWS, 128))] * 4
        args += earlier
        outs = [sent_shape((ROWS, DIM + 128))] * 4
    else:
        outs = [shape((ROWS, DIM))] * 4 + [shape((ROWS, 128), F32)] * 4
    return pl.pallas_call(
        functools.partial(attention_body, merge),
        grid=(HEADS,),
        out_shape=outs,
        in_specs=in_specs,
        out_specs=[whole(o.shape) for o in outs],
        scratch_shapes=[
            pltpu.VMEM((NY * ROWS, DIM), BF16),
            pltpu.VMEM((PART, DIM), BF16),
            pltpu.VMEM((PART, DIM), BF16),
            pltpu.VMEM((8, PART), F32),
            pltpu.VMEM((NY, ROWS, PART), F32),
            pltpu.VMEM((NY, ROWS, 128), F32),
            pltpu.VMEM((NY * ROWS, PART), BF16),
            pltpu.VMEM((NY * ROWS, DIM), F32),
            pltpu.VMEM((NY * ROWS, PART), F32),
            pltpu.VMEM((NY * ROWS, PART), F32),
        ],
        compiler_params=pltpu.CompilerParams(
            dimension_semantics=("arbitrary",), vmem_limit_bytes=32 << 20
        ),
        name="attention_last" if merge else "attention_first",
    )(pos, *(pltpu.with_memory_space_constraint(a, pltpu.HBM) for a in args))


def combined(parts):
    tops, totals = [], []
    for o in parts:
        sent = o[:, DIM : DIM + 128].astype(F32)
        whole = sent + pltpu.roll(sent, 128 - 16, 1) + pltpu.roll(sent, 128 - 32, 1)
        tops.append(whole)
        totals.append(pltpu.roll(whole, 128 - 48, 1))
    used = lax.broadcasted_iota(jnp.int32, (ROWS, 128), 1) < NX * HEADS
    tops = [jnp.where(used, t, 0.0) for t in tops]
    totals = [jnp.where(used, t, 1.0) for t in totals]
    top = jnp.maximum(jnp.maximum(tops[0], tops[1]), jnp.maximum(tops[2], tops[3]))
    shares = [n * jnp.exp2(t - top) for t, n in zip(tops, totals)]
    inverse = 1.0 / (shares[0] + shares[1] + shares[2] + shares[3])
    spread = spread_heads(0)
    attended = None
    for o, share in zip(parts, shares):
        term = spread_rows(share * inverse, spread) * o[:, 0:DIM].astype(F32)
        attended = term if attended is None else attended + term
    return attended


def combine_body(*refs):
    gate, ffn, w_out, w_atom, act = refs[4:9]
    outs = refs[9:]
    attended = combined(refs[0:4])
    gated = (attended * sigmoid(gate[...].astype(F32))).astype(BF16)
    for r in range(NX):
        part = dot(gated[:, r * COLS : (r + 1) * COLS], w_out[...]) + ffn[r * ROWS : (r + 1) * ROWS]
        small = part.astype(BF16)
        rows = dot(small, w_atom[...])
        if r == 0:
            outs[0][...] = part + act[...].astype(F32)
            outs[4][...] = rows + dot(act[...], w_atom[...])
        else:
            outs[r][...] = small
            outs[4 + r][...] = rows.astype(BF16)


def atom_first_body(starts, maps, cond, tokens, offset, *outs):
    weights, project, scale, shift, select = outs
    for src in range(NX):
        project[src * COLS : (src + 1) * COLS, :] = maps[src, DIM : DIM + COLS, :]
        for i in range(7):
            line = DIM + COLS + i * 32
            weights[i, src * 32 : (src + 1) * 32, :] = maps[src, line : line + 32, :]
    normed = norm(cond[...].astype(F32)).astype(BF16)
    scale[...] = sigmoid(dot_nt(normed, weights[0]) + offset[0:1, :])
    shift[...] = dot_nt(normed, weights[1])
    row = lax.broadcasted_iota(jnp.int32, (128, CHUNK), 0)
    for i in range(CHUNKS):
        hit = ((row + starts[i]) == tokens[i : i + 1, :]).astype(F32)
        select[i * CHUNK : (i + 1) * CHUNK, :] = hit.T.astype(BF16)


def atom_body(pos, starts, bounds, near, far, offset, spots, *refs):
    out = refs[8]
    table, skip, state, xs, qs, ks, vs, gs, at_all = refs[9:18]
    select, scale, shift, weights, bias = refs[18:23]
    sems = refs[23]
    rim = pl.ds(0, RIM)
    moves = [
        (refs[0].at[rim], skip.at[rim]),
        (refs[1], skip.at[pl.ds(RIM, ATOMS)]),
        (refs[2].at[rim], skip.at[pl.ds(RIM + ATOMS, RIM)]),
    ]
    moves += [(refs[3 + i], refs[18 + i]) for i in range(5)]
    copies = []
    for i, (there, here) in enumerate(moves):
        copies.append(pltpu.make_async_copy(there, here, sems.at[i]))
        copies[i].start()
    y, z, c = pos[0], pos[1], pos[2]
    for ky in range(NY):
        for kz in range(NZ):
            place = lax.rem(y + NY - ky, NY) * (NZ * NC) + lax.rem(z + NZ - kz, NZ) * NC
            n = (kz * NY + ky) * ROWS
            own = pl.multiple_of((place + c) * ROWS, ROWS)
            other = pl.multiple_of((place + 1 - c) * ROWS, ROWS)
            table[pl.ds(own, ROWS), :] = near[n : n + ROWS, :]
            table[pl.ds(other, ROWS), :] = far[n : n + ROWS, :]
    for i in range(6):
        copies[i].wait()
    for i in range(CHUNKS):
        rows = slice(i * CHUNK, (i + 1) * CHUNK)
        taken = table[pl.ds(pl.multiple_of(starts[i], 16), 128), :]
        now = skip[rows, :].astype(F32) + dot(select[rows, :], taken)
        state[rows, :] = now
        xs[rows, :] = (scale[rows, :] * norm(now) + shift[rows, :]).astype(BF16)
    copies[6].wait()
    x = xs[...]
    own = slice(RIM, RIM + ATOMS)
    mine = xs[own, :]
    qs[...] = (
        (dot_nt(mine, weights[2]) + offset[1:2, :]) * (LOG2E / math.sqrt(CA // HA))
    ).astype(BF16)
    ks[...] = dot_nt(x, weights[3]).astype(BF16)
    vs[...] = dot_nt(x, weights[4]).astype(BF16)
    gs[...] = sigmoid(dot_nt(mine, weights[5]).astype(BF16).astype(F32))
    width = CA // HA
    head_of_row = lax.broadcasted_iota(jnp.int32, (HA * WQ, CA), 0) // WQ
    head_of_lane = lax.broadcasted_iota(jnp.int32, (HA * WQ, CA), 1) // width
    same = head_of_row == head_of_lane
    lane_head = lax.broadcasted_iota(jnp.int32, (WQ, CA), 1) // width
    key_slot = lax.broadcasted_iota(jnp.int32, (HA * WQ, WK), 1)

    def window(b):
        rows = slice(b * WQ, (b + 1) * WQ)
        span = slice(b * WQ, b * WQ + WK)
        one = qs[rows, :].astype(F32)
        four = jnp.where(same, jnp.concatenate([one] * HA, axis=0), 0.0).astype(BF16)
        extra = jnp.concatenate([bias[i, rows, :] for i in range(HA)], axis=0).astype(F32)
        scores = dot_nt(four, ks[span, :]) + extra * LOG2E
        base = pos[3] + b * WQ - RIM
        low = bounds[0, b] - base
        high = bounds[1, b] - base
        scores = jnp.where((key_slot >= low) & (key_slot < high), scores, FAR)
        probs = jnp.exp2(scores - jnp.max(scores, axis=1, keepdims=True))
        total = jnp.sum(probs, axis=1, keepdims=True)
        summed = dot(probs.astype(BF16), vs[span, :]) * (1.0 / total)
        picked = summed[0:WQ]
        for i in range(1, HA):
            picked = jnp.where(lane_head == i, summed[i * WQ : (i + 1) * WQ], picked)
        at_all[rows, :] = picked

    copies[7].wait()
    for b in range(ATOMS // WQ):
        window(b)
    gated = (at_all[...] * gs[...]).astype(BF16)
    new = state[own, :] + dot_nt(gated, weights[6])
    final = norm(new).astype(BF16)
    update = dot_nt(spots[...], final)
    for i in range(3):
        out[i] = update[i : i + 1, :]


def per_device(
    token_act,
    token_cond,
    pair_bias,
    token_mask,
    ada_weights,
    attention_in,
    attention_out,
    transition_in,
    transition_out,
    token_vectors,
    atom_skip,
    atom_cond,
    atom_bias,
    window_bounds,
    atom_token,
    atom_weights,
    token_to_atom,
    atom_vectors,
    position_out,
):
    f = lax.axis_index("fsdp").astype(jnp.int32)
    t = lax.axis_index("seq").astype(jnp.int32)
    y, z, c = t // (NZ * NC), (t // NC) % NZ, t % NC
    f_pos = f.reshape(1)
    act = token_act[0]

    sent = kernel_call(
        prepare_body,
        "prepare",
        [sent_shape((ROWS, DIM + COLS))] * 4,
        (act, token_cond[0]),
        (f_pos,),
    )
    normed = [sent[0]] + [x_shift(sent[k], k) for k in (1, 2, 3)]
    edge_skip, edge_cond, edge_token, _ = lax.optimization_barrier(
        (atom_skip[0], atom_cond, atom_token, sent[0])
    )

    turned = jnp.swapaxes(atom_weights, 1, 2).reshape(7 * 32, CA)
    own_maps = jnp.concatenate([token_to_atom, turned], axis=0)
    skip = atom_skip[0]
    coded = jnp.stack([edge_token // 64, edge_token % 64]).astype(BF16)

    def edge(lo, hi):
        codes = jnp.pad(coded[:, lo:hi], ((0, 14), (0, CA - RIM)))
        return jnp.concatenate([edge_skip[lo:hi], edge_cond[lo:hi], codes], axis=0)

    size = lax.axis_size("seq")
    up = [(i, i + 1) for i in range(size - 1)]
    before = lax.ppermute(edge(ATOMS - RIM, ATOMS), "seq", up)
    after = lax.ppermute(edge(0, RIM), "seq", [(j, i) for i, j in up])

    pair_bias, _ = lax.optimization_barrier((pair_bias, sent[0]))
    cut = pl.pallas_call(
        cut_body,
        grid=(NY,),
        out_shape=shape((NY, HEADS, ROWS, KEYS)),
        in_specs=[pl.BlockSpec((HEADS, ROWS, KEYS), lambda i: (0, 0, i))],
        out_specs=pl.BlockSpec((1, HEADS, ROWS, KEYS), lambda i: (i, 0, 0, 0)),
        compiler_params=pltpu.CompilerParams(
            dimension_semantics=("arbitrary",), vmem_limit_bytes=16 << 20
        ),
        name="cut",
    )(pltpu.with_memory_space_constraint(pair_bias, pltpu.HBM))
    bias = y_exchange(cut)

    def decoded(side):
        pair = side[2 * RIM : 2 * RIM + 2, 0:RIM].astype(jnp.int32)
        return pair[0] * 64 + pair[1]

    cond_ext = jnp.concatenate([before[RIM : 2 * RIM], atom_cond, after[RIM : 2 * RIM]], axis=0)
    token_ext = jnp.concatenate([decoded(before), atom_token, decoded(after)])
    by_chunk = token_ext.reshape(CHUNKS, CHUNK)
    token_count = size * ROWS
    starts = jnp.minimum((by_chunk[:, 0] // 16) * 16, token_count - 128)

    offsets = lax.dynamic_slice_in_dim(token_vectors, f * COLS, COLS, 1)
    attend, message = kernel_call(
        adaptive_body,
        "adaptive",
        [sent_shape((ROWS, DIM)), shape((DIM + COLS + 7 * 32, CA))],
        (*normed, ada_weights, offsets[0:2], own_maps),
        free=7,
        flops=1 << 37,
        size=3 << 20,
    )
    attend_all = [attend] + [x_shift(attend, k) for k in (1, 2, 3)]
    attend_all[3], before, after = lax.optimization_barrier((attend_all[3], before, after))
    q, kv, gate = kernel_call(
        project_body,
        "project",
        [sent_shape((ROWS, DIM)), sent_shape((2 * ROWS, DIM)), shape((ROWS, DIM))],
        free=7,
        args=(*attend_all, attention_in, offsets[2:3], token_mask.reshape(ROWS, 1)),
        scalars=(f_pos,),
        flops=4 * 2 * 512 * 768 * 192,
        size=4 << 20,
    )
    near = [kv] + [z_swap(kv, k) for k in (1, 2, 3)]
    across = c_shift(kv)
    q_all = y_collect(q)
    q_all, near_1 = lax.optimization_barrier((q_all, near[1]))
    early = [kv, near_1, across, c_shift(near_1)]

    message, _ = lax.optimization_barrier((message, q))
    messages = lax.all_gather(message, "fsdp", axis=0)
    ffn = kernel_call(
        hidden_body,
        "hidden",
        shape((NX * ROWS, DIM), F32),
        (transition_in, transition_out, messages),
        (f_pos,),
        free=2,
        flops=3 * 2 * 512 * 768 * 384,
        size=6 << 20,
    )
    atom_maps, project_full, scale, shift, select = kernel_call(
        atom_first_body,
        "atom_first",
        [
            shape((7, CA, CA)),
            shape((DIM, CA)),
            shape((EXT, CA), F32),
            shape((EXT, CA), F32),
            shape((EXT, 128)),
        ],
        (messages, cond_ext, by_chunk, atom_vectors),
        (starts,),
        flops=4 * EXT * CA * CA,
        size=3 << 20,
    )

    def places(n):
        at = [(z ^ n) * NC + c, (z ^ (n + 1)) * NC + c]
        return jnp.stack([y, *at, at[0] ^ 1, at[1] ^ 1])

    first = attention(places(0), q_all, early, bias)
    _, near_2, near_3 = lax.optimization_barrier((first[0], near[2], near[3]))
    late = [near_2, near_3, c_shift(near_2), c_shift(near_3)]
    out = attention(places(2), q_all, late, bias, first)
    parts = [out[0]] + [y_shift(out[k], NY - k) for k in (1, 2, 3)]
    sums = kernel_call(
        combine_body,
        "combine",
        [shape((ROWS, DIM), F32)]
        + [sent_shape((ROWS, DIM))] * 3
        + [sent_shape((ROWS, CA), F32)]
        + [sent_shape((ROWS, CA))] * 3,
        (*parts, gate, ffn, attention_out, project_full, act),
        free=4,
        flops=4 * 2 * 128 * 768 * (192 + 128) + 8 * 2 * 128 * 128 * 768,
        size=5 << 20,
    )
    arrived = [x_shift(sums[4 + k], NX - k) for k in (1, 2, 3)]
    rows = (
        sums[4] + arrived[0].astype(F32) + arrived[1].astype(F32) + arrived[2].astype(F32)
    ).astype(BF16)

    turns = [y_shift(rows, k) for k in (1, 2, 3)]
    by_y = jnp.concatenate([rows] + turns, axis=0)
    turns = [z_shift(by_y, k) for k in (1, 2, 3)]
    by_z = jnp.concatenate([by_y] + turns, axis=0)
    by_c = c_shift(by_z)
    _, *partial = lax.optimization_barrier((by_y, *sums[1:4]))
    main = [x_shift(partial[k - 1], NX - k) for k in (1, 2, 3)]

    scalars = (jnp.stack([y, z, c, t * ATOMS]), starts, window_bounds.T)
    update = kernel_call(
        atom_body,
        "atoms",
        shape((3, 1, ATOMS), F32),
        (
            by_z,
            by_c,
            atom_vectors,
            position_out,
            before,
            skip,
            after,
            select,
            scale,
            shift,
            atom_maps,
            atom_bias,
        ),
        scalars,
        free=2,
        scratch=[
            pltpu.VMEM((token_count, CA), BF16),
            pltpu.VMEM((EXT, CA), BF16),
            pltpu.VMEM((EXT, CA), F32),
            pltpu.VMEM((EXT, CA), BF16),
            pltpu.VMEM((ATOMS, CA), BF16),
            pltpu.VMEM((EXT, CA), BF16),
            pltpu.VMEM((EXT, CA), BF16),
            pltpu.VMEM((ATOMS, CA), F32),
            pltpu.VMEM((ATOMS, CA), F32),
            pltpu.VMEM((EXT, 128), BF16),
            pltpu.VMEM((EXT, CA), F32),
            pltpu.VMEM((EXT, CA), F32),
            pltpu.VMEM((7, CA, CA), BF16),
            pltpu.VMEM((HA, ATOMS, WK), BF16),
            pltpu.SemaphoreType.DMA((8,)),
        ],
        late=8,
        here=2,
    )
    update, *main = lax.optimization_barrier((update, *main))
    token_result = (
        sums[0] + main[0].astype(F32) + main[1].astype(F32) + main[2].astype(F32)
    ).astype(BF16)
    return (token_result[None], jnp.swapaxes(update, 0, 1))


def solution(mesh):
    in_specs = (
        P(("sample", "fsdp"), "seq", None),
        P(("sample", "fsdp"), "seq", None),
        P("fsdp", "seq", None),
        P("seq"),
        P(None, None, "fsdp"),
        P(None, None, "fsdp"),
        P("fsdp", None),
        P(None, None, "fsdp"),
        P("fsdp", None),
        P(),
        P(("sample", "fsdp"), "seq", None),
        P("seq", None),
        P(None, "seq", None),
        P("seq", None),
        P("seq"),
        P(None, None, "fsdp"),
        P("fsdp", None),
        P(),
        P(),
    )
    out_specs = (P(("sample", "fsdp"), "seq", None), P(("sample", "fsdp"), None, "seq"))
    return jax.shard_map(
        per_device, mesh=mesh, in_specs=in_specs, out_specs=out_specs, check_vma=False
    )
```

```python
import functools
import math

import jax
import jax.numpy as jnp
from jax import lax
from jax.experimental import pallas as pl
from jax.experimental.pallas import tpu as pltpu
from jax.sharding import PartitionSpec as P

EPS = 1e-05
FAR = -1e30
SENT = 1e30
LOG2E = 1.4426950408889634
HD = 48
HA = 4
WQ = 32
WK = 128
RIM = 48
NX = 4
NY = 4
NZ = 4
NC = 2
ROWS = 128
DIM = 768
COLS = 192
HEADS = 4
ATOMS = 1024
EXT = ATOMS + 2 * RIM
CHUNK = 112
CHUNKS = EXT // CHUNK
CA = 128
F32 = jnp.float32
BF16 = jnp.bfloat16


def x_shift(a, k):
    return lax.ppermute(a, "fsdp", [(i, (i + k) % NX) for i in range(NX)])


def y_shift(a, k):
    group = NZ * NC
    pairs = [(t, ((t // group + k) % NY) * group + t % group) for t in range(NY * group)]
    return lax.ppermute(a, "seq", pairs)


def z_shift(a, k):
    group = NZ * NC
    pairs = [
        (t, (t // group) * group + ((t // NC + k) % NZ) * NC + t % NC) for t in range(NY * group)
    ]
    return lax.ppermute(a, "seq", pairs)


def z_swap(a, k):
    return lax.ppermute(a, "seq", [(t, t ^ (NC * k)) for t in range(NY * NZ * NC)])


def y_exchange(a):
    group = NZ * NC
    groups = [[y * group + n for y in range(NY)] for n in range(group)]
    return lax.all_to_all(
        a, "seq", split_axis=0, concat_axis=0, axis_index_groups=groups, tiled=True
    )


def y_collect(a):
    group = NZ * NC
    groups = [[y * group + n for y in range(NY)] for n in range(group)]
    return lax.all_gather(a, "seq", axis=0, axis_index_groups=groups)


def c_shift(a):
    return lax.ppermute(a, "seq", [(t, t ^ 1) for t in range(NY * NZ * NC)])


def norm(values):
    center = values - jnp.mean(values, axis=-1, keepdims=True)
    spread = jnp.mean(center * center, axis=-1, keepdims=True)
    return center * lax.rsqrt(spread + EPS)


def sigmoid(v):
    return 1.0 / (1.0 + jnp.exp(-v))


def dot(a, b):
    return jnp.dot(a, b, preferred_element_type=F32)


def dot_nt(a, b):
    return lax.dot_general(a, b, (((1,), (1,)), ((), ())), preferred_element_type=F32)


def kernel_call(body, name, out_shape, args, scalars=(), scratch=(), flops=0, size=0, free=0, late=0, here=0):
    def whole(a):
        return pl.BlockSpec(
            a.shape, lambda i, n=len(a.shape): (0,) * n, pipeline_mode=pl.Buffered(1)
        )

    args = [
        a if i < free else pltpu.with_memory_space_constraint(a, pltpu.HBM)
        for i, a in enumerate(args)
    ]
    return pl.pallas_call(
        body,
        grid=(1,),
        out_shape=out_shape,
        in_specs=[pl.BlockSpec(memory_space=pltpu.SMEM)] * len(scalars)
        + [pl.BlockSpec(memory_space=pltpu.VMEM)] * here
        + [whole(a) for a in args[here : len(args) - late]]
        + [pl.BlockSpec(memory_space=pltpu.HBM)] * late,
        out_specs=jax.tree.map(whole, out_shape),
        scratch_shapes=list(scratch),
        compiler_params=pltpu.CompilerParams(
            dimension_semantics=("arbitrary",), vmem_limit_bytes=24 << 20
        ),
        cost_estimate=pl.CostEstimate(flops=flops, bytes_accessed=size, transcendentals=0),
        name=name,
    )(*scalars, *args)


def shape(dims, kind=BF16):
    return pltpu.HBM(dims, kind)


def sent_shape(dims, kind=BF16):
    return jax.ShapeDtypeStruct(dims, kind)


def prepare_body(pos, act, cond, bias, *refs):
    outs, cut = refs[0:4], refs[4]
    cut[0] = bias[...]

    @pl.when(pl.program_id(0) == 0)
    def _():
        f = pos[0]
        normed = norm(cond[...].astype(F32)).astype(BF16)
        hat = norm(act[...].astype(F32))
        for k in range(NX):
            dest = lax.rem(f + k, NX)
            part = hat[:, 0:COLS]
            for j in range(1, NX):
                part = jnp.where(dest == j, hat[:, j * COLS : (j + 1) * COLS], part)
            outs[k][:, 0:DIM] = normed
            outs[k][:, DIM : DIM + COLS] = part.astype(BF16)


def adaptive_body(m0, m1, m2, m3, ada, offset, maps, attend, message):
    parts = (m0, m1, m2, m3)
    normed = jnp.concatenate([m[:, 0:DIM] for m in parts], axis=0)
    hat = jnp.concatenate([m[:, DIM : DIM + COLS] for m in parts], axis=0).astype(F32)
    message[DIM:, :] = maps[...]
    for n in range(2):
        scale = sigmoid(dot(normed, ada[2 * n]) + offset[n : n + 1, :])
        result = (scale * hat + dot(normed, ada[2 * n + 1])).astype(BF16)
        wide = jnp.concatenate([result[k * ROWS : (k + 1) * ROWS] for k in range(NX)], axis=1)
        if n == 0:
            attend[...] = wide
        else:
            for i in range(DIM // 128):
                message[i * ROWS : (i + 1) * ROWS, :] = wide[:, i * 128 : (i + 1) * 128]


def gathered_rows(part, j):
    return jnp.concatenate(
        [part[:, ((r - j) % NX) * COLS : ((r - j) % NX + 1) * COLS] for r in range(NX)],
        axis=0,
    )


def project_body(pos, a0, a1, a2, a3, weights, offset, mask, q, kv, g):
    f = pos[0]
    parts = (a0, a1, a2, a3)
    sums = [None] * 4
    for j in range(NX):
        rows = gathered_rows(parts[j][...], j)
        at = pl.multiple_of(lax.rem(f + NX - j, NX) * COLS, COLS)
        for n in range(4):
            term = dot(rows, weights[n, pl.ds(at, COLS), :])
            sums[n] = term if j == 0 else sums[n] + term
    live = mask[...] > 0
    for r in range(NX):
        own = slice(r * ROWS, (r + 1) * ROWS)
        to = slice(r * COLS, (r + 1) * COLS)
        q[:, to] = ((sums[0][own] + offset[0:1, :]) * (LOG2E / math.sqrt(HD))).astype(BF16)
        kv[0:ROWS, to] = jnp.where(live, sums[1][own], SENT).astype(BF16)
        kv[ROWS:, to] = sums[2][own].astype(BF16)
        g[:, to] = sums[3][own].astype(BF16)


def hidden_body(pos, w_in, w_out, parts, out):
    f = pos[0]
    gate, up = None, None
    for j in range(NX):
        src = lax.rem(f + NX - j, NX)
        wide = jnp.concatenate(
            [parts[src, i * ROWS : (i + 1) * ROWS, :] for i in range(DIM // 128)], axis=1
        )
        rows = gathered_rows(wide, j)
        at = pl.multiple_of(src * COLS, COLS)
        gate_term = dot(rows, w_in[0, pl.ds(at, COLS), :])
        up_term = dot(rows, w_in[1, pl.ds(at, COLS), :])
        gate = gate_term if j == 0 else gate + gate_term
        up = up_term if j == 0 else up + up_term
    hidden = (gate / (1.0 + jnp.exp(-gate)) * up).astype(BF16)
    out[...] = dot(hidden, w_out[...])


KEYS = NZ * NC * ROWS
PART = KEYS // 2


def spread_heads(first):
    head = (lax.broadcasted_iota(jnp.int32, (128, DIM), 0) - first) * HD
    lane = lax.broadcasted_iota(jnp.int32, (128, DIM), 1)
    return ((lane >= head) & (lane < head + HD)).astype(F32).astype(BF16)


def spread_rows(share, spread):
    high = share.astype(BF16)
    low = (share - high.astype(F32)).astype(BF16)
    return dot(high, spread) + dot(low, spread)


def attention_body(merge, pos, q, *refs):
    pairs = refs[0:4]
    bias = refs[4]
    refs = refs[5:]
    if merge:
        earlier, earlier_stats, refs = refs[0:4], refs[4:8], refs[8:]
        out, refs = refs[0:4], refs[4:]
    else:
        out, out_stats, refs = refs[0:4], refs[4:8], refs[8:]
    q_all, key_all, value_all, far_row, bias_all, stats, probs, total_all = refs[0:8]
    scores = refs[8:10]
    h = pl.program_id(0)
    y = pos[0]

    @pl.when(h == 0)
    def _():
        unit = (lax.broadcasted_iota(jnp.int32, (8, 128), 1) == 0).astype(F32).astype(BF16)
        for i in range(4):
            at = slice(i * ROWS, (i + 1) * ROWS)
            block = pairs[i][0:ROWS, :]
            first = dot_nt(unit, block[:, 0:128])
            far_row[:, at] = jnp.where(first > 1e20, FAR, 0.0)
            wide = block.astype(F32)
            key_all[at, :] = jnp.where(wide[:, 0:1] > 1e20, 0.0, wide).astype(BF16)
            value_all[at, :] = pairs[i][ROWS:, :]
        for n in range(NY):
            q_all[n * ROWS : (n + 1) * ROWS, :] = q[lax.rem(y + NY - n, NY)]
        stats[...] = jnp.zeros_like(stats)

    for n in range(NY):
        src = lax.rem(y + NY - n, NY)
        for i in range(4):
            at = slice(i * ROWS, (i + 1) * ROWS)
            part = bias[src, 0, :, pl.ds(pl.multiple_of(pos[1 + i] * ROWS, ROWS), ROWS)]
            bias_all[n, :, at] = part.astype(F32) * LOG2E + far_row[0:1, at]

    lane = lax.broadcasted_iota(jnp.int32, (NY * ROWS, 256), 1)
    slot = lax.broadcasted_iota(jnp.int32, (ROWS, 128), 1)
    windows, mines, rows = [], [], []
    for s in range(NX):
        lane0 = COLS * s + HD * h
        start = jnp.minimum(lane0 // 128, (DIM - 256) // 128)
        off = lane0 - start * 128
        window = pl.ds(pl.multiple_of(start * 128, 128), 256)
        mine = (lane >= off) & (lane < off + HD)
        windows.append(window)
        mines.append(mine)
        rows.append(jnp.where(mine, q_all[:, window].astype(F32), 0.0).astype(BF16))

    def score(s, j):
        keys = slice(j * 256, (j + 1) * 256)
        scores[s % 2][:, keys] = dot_nt(rows[s], key_all[keys, windows[s]])

    for j in range(PART // 256):
        score(0, j)
    for s in range(NX):
        index = s * HEADS + h
        of_max = (lax.rem(slot, 16) == index) & (slot < 48)
        of_total = (lax.rem(slot, 16) == index) & (slot >= 48) & (slot < 96)
        totals = []
        for n in range(NY):
            if s + 1 < NX and n < PART // 256:
                score(s + 1, n)
            own = slice(n * ROWS, (n + 1) * ROWS)
            part = scores[s % 2][own, :] + bias_all[n]
            top = jnp.max(part, axis=1, keepdims=True)
            part = jnp.exp2(part - top)
            total = jnp.sum(part, axis=1, keepdims=True)
            probs[own, :] = part.astype(BF16)
            totals.append(total)
            stats[n] = jnp.where(of_max, top, jnp.where(of_total, total, stats[n]))
        summed = dot(probs[...], value_all[:, windows[s]])
        for n in range(NY):
            own = slice(n * ROWS, (n + 1) * ROWS)
            scaled = summed[own] * (1.0 / totals[n])
            before = total_all[own, windows[s]]
            total_all[own, windows[s]] = jnp.where(mines[s][own], scaled, before)

    @pl.when(h == HEADS - 1)
    def _():
        third = lax.rem(slot // 16, 3)
        spread = spread_heads(48)
        for n in range(NY):
            own = slice(n * ROWS, (n + 1) * ROWS)
            whole = stats[n]
            if not merge:
                out[n][...] = total_all[own, :].astype(BF16)
                out_stats[n][...] = whole
                continue
            other = earlier_stats[n][...]
            top = jnp.maximum(whole, other)
            top_there = pltpu.roll(top, 48, 1)
            now = whole * jnp.exp2(jnp.minimum(pltpu.roll(whole, 48, 1) - top_there, 0.0))
            then = other * jnp.exp2(jnp.minimum(pltpu.roll(other, 48, 1) - top_there, 0.0))
            both = now + then
            used = (slot >= 48) & (slot < 64)
            share_now = jnp.where(used, now / both, 0.0)
            share_then = jnp.where(used, then / both, 0.0)
            merged = spread_rows(share_now, spread) * total_all[own, :]
            merged += spread_rows(share_then, spread) * earlier[n][...].astype(F32)
            out[n][:, 0:DIM] = merged.astype(BF16)
            whole = jnp.where(slot < 48, top, jnp.where(slot < 96, both, 0.0))
            high = whole.astype(BF16).astype(F32)
            rest = whole - high
            middle = rest.astype(BF16).astype(F32)
            low = rest - middle
            sent = jnp.where(third == 0, high, jnp.where(third == 1, middle, low))
            out[n][:, DIM : DIM + 128] = sent.astype(BF16)


def attention(pos, q, pairs, bias, earlier=None):
    once = pl.Buffered(1)

    def whole(dims):
        return pl.BlockSpec(dims, lambda h, n=len(dims): (0,) * n, pipeline_mode=once)

    merge = earlier is not None
    in_specs = [pl.BlockSpec(memory_space=pltpu.SMEM), whole((NY, ROWS, DIM))]
    in_specs += [whole((2 * ROWS, DIM))] * 4
    in_specs += [pl.BlockSpec((NY, 1, ROWS, KEYS), lambda h: (0, h, 0, 0))]
    args = [q, *pairs, bias]
    if merge:
        in_specs += [whole((ROWS, DIM))] * 4 + [whole((ROWS, 128))] * 4
        args += earlier
        outs = [sent_shape((ROWS, DIM + 128))] * 4
    else:
        outs = [shape((ROWS, DIM))] * 4 + [shape((ROWS, 128), F32)] * 4
    return pl.pallas_call(
        functools.partial(attention_body, merge),
        grid=(HEADS,),
        out_shape=outs,
        in_specs=in_specs,
        out_specs=[whole(o.shape) for o in outs],
        scratch_shapes=[
            pltpu.VMEM((NY * ROWS, DIM), BF16),
            pltpu.VMEM((PART, DIM), BF16),
            pltpu.VMEM((PART, DIM), BF16),
            pltpu.VMEM((8, PART), F32),
            pltpu.VMEM((NY, ROWS, PART), F32),
            pltpu.VMEM((NY, ROWS, 128), F32),
            pltpu.VMEM((NY * ROWS, PART), BF16),
            pltpu.VMEM((NY * ROWS, DIM), F32),
            pltpu.VMEM((NY * ROWS, PART), F32),
            pltpu.VMEM((NY * ROWS, PART), F32),
        ],
        compiler_params=pltpu.CompilerParams(
            dimension_semantics=("arbitrary",), vmem_limit_bytes=32 << 20
        ),
        name="attention_last" if merge else "attention_first",
    )(pos, *(pltpu.with_memory_space_constraint(a, pltpu.HBM) for a in args))


def combined(parts):
    tops, totals = [], []
    for o in parts:
        sent = o[:, DIM : DIM + 128].astype(F32)
        whole = sent + pltpu.roll(sent, 128 - 16, 1) + pltpu.roll(sent, 128 - 32, 1)
        tops.append(whole)
        totals.append(pltpu.roll(whole, 128 - 48, 1))
    used = lax.broadcasted_iota(jnp.int32, (ROWS, 128), 1) < NX * HEADS
    tops = [jnp.where(used, t, 0.0) for t in tops]
    totals = [jnp.where(used, t, 1.0) for t in totals]
    top = jnp.maximum(jnp.maximum(tops[0], tops[1]), jnp.maximum(tops[2], tops[3]))
    shares = [n * jnp.exp2(t - top) for t, n in zip(tops, totals)]
    inverse = 1.0 / (shares[0] + shares[1] + shares[2] + shares[3])
    spread = spread_heads(0)
    attended = None
    for o, share in zip(parts, shares):
        term = spread_rows(share * inverse, spread) * o[:, 0:DIM].astype(F32)
        attended = term if attended is None else attended + term
    return attended


def combine_body(*refs):
    gate, ffn, w_out, w_atom, act = refs[4:9]
    outs = refs[9:]
    attended = combined(refs[0:4])
    gated = (attended * sigmoid(gate[...].astype(F32))).astype(BF16)
    for r in range(NX):
        part = dot(gated[:, r * COLS : (r + 1) * COLS], w_out[...]) + ffn[r * ROWS : (r + 1) * ROWS]
        small = part.astype(BF16)
        rows = dot(small, w_atom[...])
        if r == 0:
            outs[0][...] = part + act[...].astype(F32)
            outs[4][...] = rows + dot(act[...], w_atom[...])
        else:
            outs[r][...] = small
            outs[4 + r][...] = rows.astype(BF16)


def atom_first_body(starts, maps, cond, tokens, offset, *outs):
    weights, project, scale, shift, select = outs
    for src in range(NX):
        project[src * COLS : (src + 1) * COLS, :] = maps[src, DIM : DIM + COLS, :]
        for i in range(7):
            line = DIM + COLS + i * 32
            weights[i, src * 32 : (src + 1) * 32, :] = maps[src, line : line + 32, :]
    normed = norm(cond[...].astype(F32)).astype(BF16)
    scale[...] = sigmoid(dot_nt(normed, weights[0]) + offset[0:1, :])
    shift[...] = dot_nt(normed, weights[1])
    row = lax.broadcasted_iota(jnp.int32, (128, CHUNK), 0)
    for i in range(CHUNKS):
        hit = ((row + starts[i]) == tokens[i : i + 1, :]).astype(F32)
        select[i * CHUNK : (i + 1) * CHUNK, :] = hit.T.astype(BF16)


def atom_body(pos, starts, bounds, near, far, before, own_skip, after, offset, spots, *refs):
    out = refs[5]
    table, skip, state, xs, qs, ks, vs, gs, at_all = refs[6:15]
    select, scale, shift, weights, bias = refs[15:20]
    sems = refs[20]
    copies = []
    for i, there in enumerate(refs[0:5]):
        copies.append(pltpu.make_async_copy(there, refs[15 + i], sems.at[i]))
        copies[i].start()
    skip[0:RIM, :] = before[0:RIM, :]
    skip[RIM : RIM + ATOMS, :] = own_skip[...]
    skip[RIM + ATOMS :, :] = after[0:RIM, :]
    y, z, c = pos[0], pos[1], pos[2]
    for ky in range(NY):
        for kz in range(NZ):
            place = lax.rem(y + NY - ky, NY) * (NZ * NC) + lax.rem(z + NZ - kz, NZ) * NC
            n = (kz * NY + ky) * ROWS
            own = pl.multiple_of((place + c) * ROWS, ROWS)
            other = pl.multiple_of((place + 1 - c) * ROWS, ROWS)
            table[pl.ds(own, ROWS), :] = near[n : n + ROWS, :]
            table[pl.ds(other, ROWS), :] = far[n : n + ROWS, :]
    for i in range(3):
        copies[i].wait()
    for i in range(CHUNKS):
        rows = slice(i * CHUNK, (i + 1) * CHUNK)
        taken = table[pl.ds(pl.multiple_of(starts[i], 16), 128), :]
        now = skip[rows, :].astype(F32) + dot(select[rows, :], taken)
        state[rows, :] = now
        xs[rows, :] = (scale[rows, :] * norm(now) + shift[rows, :]).astype(BF16)
    copies[3].wait()
    x = xs[...]
    own = slice(RIM, RIM + ATOMS)
    mine = xs[own, :]
    qs[...] = (
        (dot_nt(mine, weights[2]) + offset[1:2, :]) * (LOG2E / math.sqrt(CA // HA))
    ).astype(BF16)
    ks[...] = dot_nt(x, weights[3]).astype(BF16)
    vs[...] = dot_nt(x, weights[4]).astype(BF16)
    gs[...] = sigmoid(dot_nt(mine, weights[5]).astype(BF16).astype(F32))
    width = CA // HA
    head_of_row = lax.broadcasted_iota(jnp.int32, (HA * WQ, CA), 0) // WQ
    head_of_lane = lax.broadcasted_iota(jnp.int32, (HA * WQ, CA), 1) // width
    same = head_of_row == head_of_lane
    lane_head = lax.broadcasted_iota(jnp.int32, (WQ, CA), 1) // width
    key_slot = lax.broadcasted_iota(jnp.int32, (HA * WQ, WK), 1)

    def window(b):
        rows = pl.ds(pl.multiple_of(b * WQ, WQ), WQ)
        span = pl.ds(pl.multiple_of(b * WQ, WQ), WK)
        one = qs[rows, :].astype(F32)
        four = jnp.where(same, jnp.concatenate([one] * HA, axis=0), 0.0).astype(BF16)
        extra = jnp.concatenate([bias[i, rows, :] for i in range(HA)], axis=0).astype(F32)
        scores = dot_nt(four, ks[span, :]) + extra * LOG2E
        base = pos[3] + b * WQ - RIM
        low = bounds[0, b] - base
        high = bounds[1, b] - base
        scores = jnp.where((key_slot >= low) & (key_slot < high), scores, FAR)
        probs = jnp.exp2(scores - jnp.max(scores, axis=1, keepdims=True))
        total = jnp.sum(probs, axis=1, keepdims=True)
        summed = dot(probs.astype(BF16), vs[span, :]) * (1.0 / total)
        picked = summed[0:WQ]
        for i in range(1, HA):
            picked = jnp.where(lane_head == i, summed[i * WQ : (i + 1) * WQ], picked)
        at_all[rows, :] = picked

    copies[4].wait()

    def windows(step, carry):
        for i in range(8):
            window(step * 8 + i)
        return carry

    lax.fori_loop(0, ATOMS // WQ // 8, windows, 0)
    gated = (at_all[...] * gs[...]).astype(BF16)
    new = state[own, :] + dot_nt(gated, weights[6])
    final = norm(new).astype(BF16)
    update = dot_nt(spots[...], final)
    for i in range(3):
        out[i] = update[i : i + 1, :]


def per_device(
    token_act,
    token_cond,
    pair_bias,
    token_mask,
    ada_weights,
    attention_in,
    attention_out,
    transition_in,
    transition_out,
    token_vectors,
    atom_skip,
    atom_cond,
    atom_bias,
    window_bounds,
    atom_token,
    atom_weights,
    token_to_atom,
    atom_vectors,
    position_out,
):
    f = lax.axis_index("fsdp").astype(jnp.int32)
    t = lax.axis_index("seq").astype(jnp.int32)
    y, z, c = t // (NZ * NC), (t // NC) % NZ, t % NC
    f_pos = f.reshape(1)
    act = token_act[0]

    block = pl.BlockSpec((ROWS, DIM), lambda i: (0, 0), pipeline_mode=pl.Buffered(1))
    wide = pl.BlockSpec((ROWS, DIM + COLS), lambda i: (0, 0), pipeline_mode=pl.Buffered(1))
    *sent, cut = pl.pallas_call(
        prepare_body,
        grid=(NY,),
        out_shape=[sent_shape((ROWS, DIM + COLS))] * 4 + [shape((NY, HEADS, ROWS, KEYS))],
        in_specs=[
            pl.BlockSpec(memory_space=pltpu.SMEM),
            block,
            block,
            pl.BlockSpec((HEADS, ROWS, KEYS), lambda i: (0, 0, i)),
        ],
        out_specs=[wide] * 4 + [pl.BlockSpec((1, HEADS, ROWS, KEYS), lambda i: (i, 0, 0, 0))],
        compiler_params=pltpu.CompilerParams(
            dimension_semantics=("arbitrary",), vmem_limit_bytes=24 << 20
        ),
        name="prepare",
    )(
        f_pos,
        pltpu.with_memory_space_constraint(act, pltpu.HBM),
        pltpu.with_memory_space_constraint(token_cond[0], pltpu.HBM),
        pltpu.with_memory_space_constraint(pair_bias, pltpu.HBM),
    )
    normed = [sent[0]] + [x_shift(sent[k], k) for k in (1, 2, 3)]
    edge_skip, edge_cond, edge_token, _ = lax.optimization_barrier(
        (atom_skip[0], atom_cond, atom_token, sent[0])
    )

    turned = jnp.swapaxes(atom_weights, 1, 2).reshape(7 * 32, CA)
    own_maps = jnp.concatenate([token_to_atom, turned], axis=0)
    skip = atom_skip[0]
    coded = jnp.stack([edge_token // 64, edge_token % 64]).astype(BF16)

    def edge(lo, hi):
        codes = jnp.pad(coded[:, lo:hi], ((0, 14), (0, CA - RIM)))
        return jnp.concatenate([edge_skip[lo:hi], edge_cond[lo:hi], codes], axis=0)

    size = lax.axis_size("seq")
    up = [(i, i + 1) for i in range(size - 1)]
    before = lax.ppermute(edge(ATOMS - RIM, ATOMS), "seq", up)
    after = lax.ppermute(edge(0, RIM), "seq", [(j, i) for i, j in up])

    bias = y_exchange(cut)

    def decoded(side):
        pair = side[2 * RIM : 2 * RIM + 2, 0:RIM].astype(jnp.int32)
        return pair[0] * 64 + pair[1]

    cond_ext = jnp.concatenate([before[RIM : 2 * RIM], atom_cond, after[RIM : 2 * RIM]], axis=0)
    token_ext = jnp.concatenate([decoded(before), atom_token, decoded(after)])
    by_chunk = token_ext.reshape(CHUNKS, CHUNK)
    token_count = size * ROWS
    starts = jnp.minimum((by_chunk[:, 0] // 16) * 16, token_count - 128)

    offsets = lax.dynamic_slice_in_dim(token_vectors, f * COLS, COLS, 1)
    attend, message = kernel_call(
        adaptive_body,
        "adaptive",
        [sent_shape((ROWS, DIM)), shape((DIM + COLS + 7 * 32, CA))],
        (*normed, ada_weights, offsets[0:2], own_maps),
        here=4,
        free=7,
        flops=4 * 2 * 512 * 768 * 192,
        size=3 << 20,
    )
    attend_all = [attend] + [x_shift(attend, k) for k in (1, 2, 3)]
    attend_all[3], before, after = lax.optimization_barrier((attend_all[3], before, after))
    q, kv, gate = kernel_call(
        project_body,
        "project",
        [sent_shape((ROWS, DIM)), sent_shape((2 * ROWS, DIM)), shape((ROWS, DIM))],
        here=4,
        free=7,
        args=(*attend_all, attention_in, offsets[2:3], token_mask.reshape(ROWS, 1)),
        scalars=(f_pos,),
        flops=4 * 2 * 512 * 768 * 192,
        size=4 << 20,
    )
    near = [kv] + [z_swap(kv, k) for k in (1, 2, 3)]
    across = c_shift(kv)
    q_all = y_collect(q)
    q_all, near_1 = lax.optimization_barrier((q_all, near[1]))
    early = [kv, near_1, across, c_shift(near_1)]

    message, _ = lax.optimization_barrier((message, q))
    messages = lax.all_gather(message, "fsdp", axis=0)
    ffn = kernel_call(
        hidden_body,
        "hidden",
        shape((NX * ROWS, DIM), F32),
        (transition_in, transition_out, messages),
        (f_pos,),
        free=2,
        flops=3 * 2 * 512 * 768 * 384,
        size=6 << 20,
    )
    atom_maps, project_full, scale, shift, select = kernel_call(
        atom_first_body,
        "atom_first",
        [
            shape((7, CA, CA)),
            shape((DIM, CA)),
            shape((EXT, CA), F32),
            shape((EXT, CA), F32),
            shape((EXT, 128)),
        ],
        (messages, cond_ext, by_chunk, atom_vectors),
        (starts,),
        flops=4 * EXT * CA * CA,
        size=3 << 20,
    )

    def places(n):
        at = [(z ^ n) * NC + c, (z ^ (n + 1)) * NC + c]
        return jnp.stack([y, *at, at[0] ^ 1, at[1] ^ 1])

    first = attention(places(0), q_all, early, bias)
    _, near_2, near_3 = lax.optimization_barrier((first[0], near[2], near[3]))
    late = [near_2, near_3, c_shift(near_2), c_shift(near_3)]
    out = attention(places(2), q_all, late, bias, first)
    parts = [out[0]] + [y_shift(out[k], NY - k) for k in (1, 2, 3)]
    sums = kernel_call(
        combine_body,
        "combine",
        [shape((ROWS, DIM), F32)]
        + [sent_shape((ROWS, DIM))] * 3
        + [sent_shape((ROWS, CA), F32)]
        + [sent_shape((ROWS, CA))] * 3,
        (*parts, gate, ffn, attention_out, project_full, act),
        here=4,
        free=4,
        flops=4 * 2 * 128 * 768 * (192 + 128) + 8 * 2 * 128 * 128 * 768,
        size=5 << 20,
    )
    arrived = [x_shift(sums[4 + k], NX - k) for k in (1, 2, 3)]
    rows = (
        sums[4] + arrived[0].astype(F32) + arrived[1].astype(F32) + arrived[2].astype(F32)
    ).astype(BF16)

    turns = [y_shift(rows, k) for k in (1, 2, 3)]
    by_y = jnp.concatenate([rows] + turns, axis=0)
    turns = [z_shift(by_y, k) for k in (1, 2, 3)]
    by_z = jnp.concatenate([by_y] + turns, axis=0)
    by_c = c_shift(by_z)
    _, *partial = lax.optimization_barrier((by_z, *sums[1:4]))
    main = [x_shift(partial[k - 1], NX - k) for k in (1, 2, 3)]

    scalars = (jnp.stack([y, z, c, t * ATOMS]), starts, window_bounds.T)
    update = kernel_call(
        atom_body,
        "atoms",
        shape((3, 1, ATOMS), F32),
        (
            by_z,
            by_c,
            before,
            skip,
            after,
            atom_vectors,
            position_out,
            select,
            scale,
            shift,
            atom_maps,
            atom_bias,
        ),
        scalars,
        here=2,
        free=2,
        scratch=[
            pltpu.VMEM((token_count, CA), BF16),
            pltpu.VMEM((EXT, CA), BF16),
            pltpu.VMEM((EXT, CA), F32),
            pltpu.VMEM((EXT, CA), BF16),
            pltpu.VMEM((ATOMS, CA), BF16),
            pltpu.VMEM((EXT, CA), BF16),
            pltpu.VMEM((EXT, CA), BF16),
            pltpu.VMEM((ATOMS, CA), F32),
            pltpu.VMEM((ATOMS, CA), F32),
            pltpu.VMEM((EXT, 128), BF16),
            pltpu.VMEM((EXT, CA), F32),
            pltpu.VMEM((EXT, CA), F32),
            pltpu.VMEM((7, CA, CA), BF16),
            pltpu.VMEM((HA, ATOMS, WK), BF16),
            pltpu.SemaphoreType.DMA((5,)),
        ],
        late=5,
        flops=2 * 1120 * 128 * 128 * 10,
        size=6 << 20,
    )
    update, *main = lax.optimization_barrier((update, *main))
    token_result = (
        sums[0] + main[0].astype(F32) + main[1].astype(F32) + main[2].astype(F32)
    ).astype(BF16)
    return (token_result[None], jnp.swapaxes(update, 0, 1))


def solution(mesh):
    in_specs = (
        P(("sample", "fsdp"), "seq", None),
        P(("sample", "fsdp"), "seq", None),
        P("fsdp", "seq", None),
        P("seq"),
        P(None, None, "fsdp"),
        P(None, None, "fsdp"),
        P("fsdp", None),
        P(None, None, "fsdp"),
        P("fsdp", None),
        P(),
        P(("sample", "fsdp"), "seq", None),
        P("seq", None),
        P(None, "seq", None),
        P("seq", None),
        P("seq"),
        P(None, None, "fsdp"),
        P("fsdp", None),
        P(),
        P(),
    )
    out_specs = (P(("sample", "fsdp"), "seq", None), P(("sample", "fsdp"), None, "seq"))
    return jax.shard_map(
        per_device, mesh=mesh, in_specs=in_specs, out_specs=out_specs, check_vma=False
    )
```
